512 devices in a mesh: branch: 4 (over z_lo), row: 16 (over x, y), col: 8 (over z_hi, core).
Axes of the slice: x: 4, y: 4, z: 16 (z_hi: 4, z_lo: 4; z = z_hi * 4 + z_lo), core: 2. Of those that a mesh axis runs over, the one named last changes fastest.
Arguments:
- alignment: bfloat16 [256, 512, 256], P(('branch', 'row'), 'col'), may hold values from -32 to 32
- pair_features: bfloat16 [512, 512, 128], P('col', 'row'), may hold values from -32 to 32
- w_row: bfloat16 [256, 1024], replicated, may hold values from -8 to 8
- row_output_weight: bfloat16 [256, 256], replicated, may hold values from -1.5 to 1.5
- w_bias: bfloat16 [128, 8], replicated, may hold values from -1 to 1
- w_column: bfloat16 [256, 1024], replicated, may hold values from -8 to 8
- column_output_weight: bfloat16 [256, 256], replicated, may hold values from -1.5 to 1.5
- outer_input_weight: bfloat16 [256, 64], replicated, may hold values from -0.375 to 0.375
- w_outer_out: bfloat16 [1024, 128], replicated, may hold values from -1.5 to 1.5
- w_triangle_in: bfloat16 [128, 512], replicated, may hold values from -0.5 to 0.5
- w_triangle_gate: bfloat16 [128, 128], replicated, may hold values from -0.5 to 0.5
- w_triangle_out: bfloat16 [128, 128], replicated, may hold values from -0.5 to 0.5
Outputs:
- alignment_out: bfloat16 [256, 512, 256], P(('branch', 'row'), 'col')
- pair_out: bfloat16 [512, 512, 128], P('col', 'row', 'branch')
The draws below stay inside these ranges and needn't reach their ends.
All inputs are finite; a program needn't handle non-finite values.
Results may differ from the reference program's by a relative error of at most 0.013.
Values may be sent and summed in bfloat16 or wider, within the bound.
No kernel may reach another device: no remote copies, remote signals or barrier semaphores. Data moves between devices by JAX's collectives and lax.ppermute only.
A program may use at most 64 MiB of HBM per device.

```python
import math
import jax
import jax.numpy as jnp
from jax import lax

ALIGN_CHANNELS = 256
PAIR_WIDTH = 128
HEAD_COUNT = 8
HEAD_CHANNELS = 32
FACTOR_CHANNELS = 32
TRIANGLE_WIDTH = 128
SEQUENCE_COUNT = 256
RESIDUE_COUNT = 512


def scaled_field(key, array_shape):
    subkeys = jax.random.split(key, 3)
    base_values = jnp.clip(jax.random.normal(subkeys[0], array_shape, jnp.float32), -3.0, 3.0)
    row_scale = jnp.exp(jax.random.uniform(subkeys[1], array_shape[:-1] + (1,), jnp.float32, math.log(0.3), math.log(3.0)))
    channel_scale = jnp.exp(jax.random.uniform(subkeys[2], (array_shape[-1],), jnp.float32, math.log(0.3), math.log(3.0)))
    return base_values * row_scale * channel_scale


def attention_weight(key, random_tweak):
    weight_entries = jax.random.normal(jax.random.fold_in(key, random_tweak), (ALIGN_CHANNELS, 4 * ALIGN_CHANNELS), jnp.float32)
    weight_entries = jnp.clip(weight_entries, -5.0, 5.0) / math.sqrt(ALIGN_CHANNELS)
    return weight_entries


def draw_alignment(key, part):
    array_shape = (SEQUENCE_COUNT, RESIDUE_COUNT, ALIGN_CHANNELS)
    field_values = scaled_field(jax.random.fold_in(key, 101), array_shape)
    return field_values.astype(jnp.bfloat16)


def draw_pair_features(key, part):
    return scaled_field(jax.random.fold_in(key, 201), (RESIDUE_COUNT, RESIDUE_COUNT, PAIR_WIDTH)).astype(jnp.bfloat16)


def draw_w_row(key, part):
    return attention_weight(key, 301).astype(jnp.bfloat16)


def draw_w_column(key, part):
    return attention_weight(key, 401).astype(jnp.bfloat16)


def noise(key, dims, width, reach, kind=jnp.bfloat16):
    return jnp.clip(width * jax.random.normal(key, dims, jnp.float32), -reach, reach).astype(kind)


def setup_inputs(seed: int = 0) -> dict:
    keys = jax.random.split(jax.random.key(seed), 13)
    return {
        "alignment": draw_alignment(jax.random.fold_in(keys[12], 71), 0),
        "pair_features": draw_pair_features(jax.random.fold_in(keys[12], 71), 0),
        "w_row": draw_w_row(jax.random.fold_in(keys[12], 71), 0),
        "row_output_weight": noise(keys[3], (ALIGN_CHANNELS, ALIGN_CHANNELS), (ALIGN_CHANNELS // 16) ** -0.5, 1.5),
        "w_bias": noise(keys[4], (PAIR_WIDTH, HEAD_COUNT), (PAIR_WIDTH // 4) ** -0.5, 1.0),
        "w_column": draw_w_column(jax.random.fold_in(keys[12], 71), 0),
        "column_output_weight": noise(keys[6], (ALIGN_CHANNELS, ALIGN_CHANNELS), (ALIGN_CHANNELS // 16) ** -0.5, 1.5),
        "outer_input_weight": noise(keys[7], (ALIGN_CHANNELS, 2 * FACTOR_CHANNELS), ALIGN_CHANNELS ** -0.5, 0.375),
        "w_outer_out": noise(keys[8], (FACTOR_CHANNELS * FACTOR_CHANNELS, PAIR_WIDTH), (FACTOR_CHANNELS * FACTOR_CHANNELS // 64) ** -0.5, 1.5),
        "w_triangle_in": noise(keys[9], (PAIR_WIDTH, 4 * TRIANGLE_WIDTH), PAIR_WIDTH ** -0.5, 0.5),
        "w_triangle_gate": noise(keys[10], (PAIR_WIDTH, PAIR_WIDTH), PAIR_WIDTH ** -0.5, 0.5),
        "w_triangle_out": noise(keys[11], (TRIANGLE_WIDTH, PAIR_WIDTH), TRIANGLE_WIDTH ** -0.5, 0.5),
    }


EPSILON = 1e-05

def layer_norm(inputs):
    inputs = inputs.astype(jnp.float32)
    average = lax.optimization_barrier(jnp.mean(inputs, axis=-1, keepdims=True))
    variance = lax.optimization_barrier(jnp.mean(jnp.square(inputs - average), axis=-1, keepdims=True))
    return (inputs - average) * lax.rsqrt(variance + EPSILON)

def split_heads(row_entries):
    return row_entries.reshape(row_entries.shape[:-1] + (HEAD_COUNT, HEAD_CHANNELS))

def attend(query_matrix, key_matrix, value_matrix, head_bias):
    query_heads = split_heads(query_matrix.astype(jnp.float32))
    key_heads = split_heads(key_matrix.astype(jnp.float32))
    value_heads = split_heads(value_matrix.astype(jnp.float32))
    scores = jnp.einsum('bqhd,bkhd->bhqk', query_heads, key_heads)
    if head_bias is not None:
        scores = scores + head_bias.astype(jnp.float32)[None]
    attention = jax.nn.softmax(scores, axis=-1).astype(jnp.bfloat16)
    mixed_channels = jnp.einsum('bhqk,bkhd->bqhd', attention.astype(jnp.float32), value_heads)
    return mixed_channels.reshape(mixed_channels.shape[:2] + (ALIGN_CHANNELS,))

def gated_attention(row_entries, weight_matrix, output_weight, head_bias):
    normed_input = layer_norm(row_entries).astype(jnp.bfloat16)
    projected_input = jnp.dot(normed_input.reshape(-1, ALIGN_CHANNELS), weight_matrix, preferred_element_type=jnp.float32)
    projected_input = projected_input.reshape(row_entries.shape[:2] + (4 * ALIGN_CHANNELS,))
    query_matrix = (projected_input[..., :ALIGN_CHANNELS] * HEAD_CHANNELS ** (-0.5)).astype(jnp.bfloat16)
    key_matrix = projected_input[..., ALIGN_CHANNELS:2 * ALIGN_CHANNELS].astype(jnp.bfloat16)
    value_matrix = projected_input[..., 2 * ALIGN_CHANNELS:3 * ALIGN_CHANNELS].astype(jnp.bfloat16)
    gate_values = jax.nn.sigmoid(projected_input[..., 3 * ALIGN_CHANNELS:])
    attended = attend(query_matrix, key_matrix, value_matrix, head_bias)
    gated_output = (gate_values * attended).astype(jnp.bfloat16)
    residual_update = jnp.dot(gated_output.reshape(-1, ALIGN_CHANNELS), output_weight, preferred_element_type=jnp.float32)
    return (row_entries.astype(jnp.float32) + residual_update.reshape(row_entries.shape)).astype(jnp.bfloat16)

def reference(alignment, pair_features, w_row, row_output_weight, w_bias, w_column, column_output_weight, outer_input_weight, w_outer_out, w_triangle_in, w_triangle_gate, w_triangle_out):
    pair_normed = layer_norm(pair_features).astype(jnp.bfloat16)
    bias_flat = jnp.dot(pair_normed.reshape(-1, PAIR_WIDTH), w_bias, preferred_element_type=jnp.float32)
    head_bias = jnp.transpose(bias_flat.reshape(RESIDUE_COUNT, RESIDUE_COUNT, HEAD_COUNT), (2, 0, 1)).astype(jnp.bfloat16)

    def row_step(row_entries):
        return gated_attention(row_entries[None], w_row, row_output_weight, head_bias)[0]
    alignment_row = lax.map(row_step, alignment)

    def column_step(row_entries):
        return gated_attention(row_entries[None], w_column, column_output_weight, None)[0]
    by_residue = lax.map(column_step, jnp.transpose(alignment_row, (1, 0, 2)))
    alignment_out = jnp.transpose(by_residue, (1, 0, 2))
    outer_normed_input = layer_norm(alignment_out).astype(jnp.bfloat16)
    factor_pairs = jnp.dot(outer_normed_input.reshape(-1, ALIGN_CHANNELS), outer_input_weight, preferred_element_type=jnp.float32)
    factor_pairs = factor_pairs.reshape(SEQUENCE_COUNT, RESIDUE_COUNT, 2 * FACTOR_CHANNELS).astype(jnp.bfloat16)
    left_factor = factor_pairs[..., :FACTOR_CHANNELS]
    right_factor = factor_pairs[..., FACTOR_CHANNELS:].astype(jnp.float32)
    left_blocks = jnp.transpose(left_factor.reshape(SEQUENCE_COUNT, RESIDUE_COUNT // 32, 32, FACTOR_CHANNELS), (1, 0, 2, 3))

    def outer_block(block_rows):
        outer_sum = jnp.einsum('sic,sje->ijce', block_rows.astype(jnp.float32), right_factor) * (1.0 / SEQUENCE_COUNT)
        flat_rows = outer_sum.reshape(-1, FACTOR_CHANNELS * FACTOR_CHANNELS).astype(jnp.bfloat16)
        residual_update = jnp.dot(flat_rows, w_outer_out, preferred_element_type=jnp.float32)
        return residual_update.astype(jnp.bfloat16).reshape(32, RESIDUE_COUNT, PAIR_WIDTH)
    outer_update = lax.map(outer_block, left_blocks).reshape(RESIDUE_COUNT, RESIDUE_COUNT, PAIR_WIDTH)
    pair_mid = (pair_features.astype(jnp.float32) + outer_update.astype(jnp.float32)).astype(jnp.bfloat16)
    triangle_normed = layer_norm(pair_mid).astype(jnp.bfloat16)
    flat_normed = triangle_normed.reshape(-1, PAIR_WIDTH)
    projected_input = jnp.dot(flat_normed, w_triangle_in, preferred_element_type=jnp.float32)
    projected_input = projected_input.reshape(RESIDUE_COUNT, RESIDUE_COUNT, 4, TRIANGLE_WIDTH)
    tri_left = (jax.nn.sigmoid(projected_input[:, :, 1]) * projected_input[:, :, 0]).astype(jnp.bfloat16)
    tri_right = (jax.nn.sigmoid(projected_input[:, :, 3]) * projected_input[:, :, 2]).astype(jnp.bfloat16)
    triangle_sum = jnp.einsum('ikc,jkc->ijc', tri_left.astype(jnp.float32), tri_right.astype(jnp.float32)).astype(jnp.bfloat16)
    triangle_scaled = layer_norm(triangle_sum).astype(jnp.bfloat16)
    mixed_channels = jnp.dot(triangle_scaled.reshape(-1, TRIANGLE_WIDTH), w_triangle_out, preferred_element_type=jnp.float32)
    output_gate = jax.nn.sigmoid(jnp.dot(flat_normed, w_triangle_gate, preferred_element_type=jnp.float32))
    pair_out = (pair_mid.reshape(-1, PAIR_WIDTH).astype(jnp.float32) + output_gate * mixed_channels).astype(jnp.bfloat16)
    return (alignment_out, pair_out.reshape(RESIDUE_COUNT, RESIDUE_COUNT, PAIR_WIDTH))
```

```python
import functools

import jax
import jax.numpy as jnp
from jax import lax
from jax.experimental import pallas as pl
from jax.experimental.pallas import tpu as pltpu
from jax.sharding import PartitionSpec as P

BF = jnp.bfloat16
F32 = jnp.float32
EPSILON = 1e-05
SCALE = 32**-0.5

NT = (((1,), (1,)), ((), ()))
TN = (((0,), (0,)), ((), ()))
TT = (((0,), (1,)), ((), ()))


def mm(a, b, dims):
    return lax.dot_general(a, b, dims, preferred_element_type=F32)


def layer_norm(inputs):
    inputs = inputs.astype(F32)
    average = jnp.mean(inputs, axis=-1, keepdims=True)
    centered = inputs - average
    variance = jnp.mean(jnp.square(centered), axis=-1, keepdims=True)
    return centered * lax.rsqrt(variance + EPSILON)


def sigmoid(x):
    return 1.0 / (1.0 + jnp.exp(-x))


def softmax_rows(scores):
    top = jnp.max(scores, axis=0, keepdims=True)
    weights = jnp.exp(scores - top)
    total = jnp.sum(weights, axis=0, keepdims=True)
    return (weights * (1.0 / total)).astype(BF)


def row_kernel(place, *refs):
    blocks = refs[:8]
    w_ref, bias_ref, wo_ref, out_ref, rows = refs[8:]
    me = place[0]
    own = None
    for m in range(8):
        normed = layer_norm(blocks[m][0]).astype(BF)
        if m == 0:
            own = normed
        start = pl.multiple_of((me ^ m) * 64, 64)
        rows[pl.ds(start, 64), :] = normed
    x = rows[...]
    key = jnp.dot(x, w_ref[:, 256:512], preferred_element_type=F32).astype(BF)
    value_t = mm(w_ref[:, 512:768], x, TT).astype(BF)
    query_t = (mm(w_ref[:, 0:256], own, TT) * SCALE).astype(BF)
    gate_t = sigmoid(mm(w_ref[:, 768:1024], own, TT))
    twice = jnp.concatenate([query_t, query_t], axis=1)
    head_row = lax.broadcasted_iota(jnp.int32, (256, 128), 0) // 32
    head_lane = lax.broadcasted_iota(jnp.int32, (256, 128), 1) // 64
    upper = lax.broadcasted_iota(jnp.int32, (64, 64), 0) < 32
    parts = []
    for p in range(4):
        diag = jnp.where(head_row == 2 * p + head_lane, twice, jnp.zeros_like(twice))
        scores = jnp.dot(key, diag, preferred_element_type=F32)
        scores = scores + bias_ref[:, p * 128 : (p + 1) * 128].astype(F32)
        weights = softmax_rows(scores)
        mixed = jnp.dot(value_t[p * 64 : (p + 1) * 64], weights, preferred_element_type=F32)
        parts.append(jnp.where(upper, mixed[:, :64], mixed[:, 64:]))
    attended_t = jnp.concatenate(parts, axis=0)
    gated = (gate_t * attended_t).astype(BF)
    update = mm(gated, wo_ref[...], TN)
    out_ref[0] = (blocks[0][0].astype(F32) + update).astype(BF)


def row_attention(place, blocks, w_row, bias, w_out):
    block = pl.BlockSpec((1, 64, 256), lambda s, p: (s, 0, 0))
    full = lambda *shape: pl.BlockSpec(shape, lambda s, p: (0,) * len(shape))
    return pl.pallas_call(
        row_kernel,
        out_shape=jax.ShapeDtypeStruct((4, 64, 256), BF),
        grid_spec=pltpu.PrefetchScalarGridSpec(
            num_scalar_prefetch=1,
            grid=(4,),
            in_specs=[block] * 8 + [full(256, 1024), full(512, 512), full(256, 256)],
            out_specs=block,
            scratch_shapes=[pltpu.VMEM((512, 256), BF)],
        ),
        name="row_attention",
    )(place, *blocks, w_row, bias, w_out)


def column_kernel(x_ref, w_ref, wo_ref, wf_ref, out_ref, factor_ref):
    x = x_ref[...]
    normed = layer_norm(x).astype(BF)
    key = jnp.dot(normed, w_ref[:, 256:512], preferred_element_type=F32).astype(BF)
    value_t = mm(w_ref[:, 512:768], normed, TT).astype(BF)
    query_t = (mm(w_ref[:, 0:256], normed, TT) * SCALE).astype(BF)
    gate_t = sigmoid(mm(w_ref[:, 768:1024], normed, TT))
    head_row = lax.broadcasted_iota(jnp.int32, (256, 256), 0) // 32
    parts = []
    for h in range(8):
        diag = jnp.where(head_row == h, query_t, jnp.zeros_like(query_t))
        weights = softmax_rows(jnp.dot(key, diag, preferred_element_type=F32))
        parts.append(
            jnp.dot(value_t[h * 32 : (h + 1) * 32], weights, preferred_element_type=F32)
        )
    gated = (gate_t * jnp.concatenate(parts, axis=0)).astype(BF)
    result = (x.astype(F32) + mm(gated, wo_ref[...], TN)).astype(BF)
    out_ref[...] = result
    factor_ref[...] = mm(wf_ref[...], layer_norm(result).astype(BF), TT).astype(BF)


def column_attention(x, w_column, w_out, w_factor):
    return pl.pallas_call(
        column_kernel,
        out_shape=(jax.ShapeDtypeStruct((256, 256), BF), jax.ShapeDtypeStruct((64, 256), BF)),
        name="column_attention",
    )(x, w_column, w_out, w_factor)


def pick_kernel(index, source_ref, out_ref):
    for r in range(16):
        out_ref[r] = source_ref[index[r // 2]]


def pick(index, source):
    return pl.pallas_call(
        pick_kernel,
        out_shape=jax.ShapeDtypeStruct((16, 32, 256), BF),
        grid_spec=pltpu.PrefetchScalarGridSpec(
            num_scalar_prefetch=1,
            grid=(1,),
            in_specs=[pl.BlockSpec((8, 32, 256), lambda g, p: (0, 0, 0))],
            out_specs=pl.BlockSpec((16, 32, 256), lambda g, p: (0, 0, 0)),
        ),
        name="pick",
    )(index, source)


def sides_kernel(n_ref, w_ref, out_ref, scratch):
    rows = n_ref[...]
    lane = lax.broadcasted_iota(jnp.int32, (64, 128), 1) < 64
    for side in range(2):
        base = side * 256
        value = mm(w_ref[:, base : base + 128], rows, TT)
        gate = mm(w_ref[:, base + 128 : base + 256], rows, TT)
        both = sigmoid(gate) * value
        for pair in range(4):
            low = both[:64, pair * 128 : (pair + 1) * 128]
            high = both[64:, pair * 128 : (pair + 1) * 128]
            scratch[side, :, 2 * pair, :] = jnp.where(lane, low, pltpu.roll(high, 64, 1))
            scratch[side, :, 2 * pair + 1, :] = jnp.where(lane, pltpu.roll(low, 64, 1), high)
    out_ref[:, 0] = scratch[0].astype(BF)
    out_ref[:, 1] = scratch[1].astype(BF)


def triangle_sides(normed, w_in):
    return pl.pallas_call(
        sides_kernel,
        out_shape=jax.ShapeDtypeStruct((64, 2, 8, 128), BF),
        scratch_shapes=[pltpu.VMEM((2, 64, 8, 128), F32)],
        name="triangle_sides",
    )(normed, w_in)


def triangle_kernel(place, left_ref, *refs):
    rights, out_ref = refs[:8], refs[8]
    me = place[0]
    left = left_ref[...]
    lane = lax.broadcasted_iota(jnp.int32, (64, 128), 1) < 64
    for m in range(8):
        product = mm(rights[m][...], left, TN)
        block = jnp.where(lane, product[:64], product[64:]).astype(BF)
        target = (me ^ m) * 2
        for b in range(4):
            for h in range(2):
                out_ref[b * 16 + target + h] = block[(b * 2 + h) * 8 : (b * 2 + h + 1) * 8]


def triangle_sums(place, left, rights):
    full = lambda *shape: pl.BlockSpec(shape, lambda g, p: (0,) * len(shape))
    return pl.pallas_call(
        triangle_kernel,
        out_shape=jax.ShapeDtypeStruct((64, 8, 128), BF),
        grid_spec=pltpu.PrefetchScalarGridSpec(
            num_scalar_prefetch=1,
            grid=(1,),
            in_specs=[full(512, 128)] * 9,
            out_specs=full(64, 8, 128),
        ),
        name="triangle_sums",
    )(place, left, *rights)


def output_kernel(sum_ref, mid_ref, n_ref, wg_ref, w_ref, out_ref, scratch):
    sums = sum_ref[...].astype(F32)
    fold = lambda v: (v + pltpu.roll(v, 64, 1)) * (1.0 / 128)
    average = fold(jnp.sum(sums, axis=0))
    centered = sums - average[None]
    variance = fold(jnp.sum(jnp.square(centered), axis=0))
    scratch[...] = centered * lax.rsqrt(variance + EPSILON)[None]
    gate = sigmoid(jnp.dot(n_ref[...], wg_ref[...], preferred_element_type=F32))
    for j in range(8):
        product = mm(scratch[:, j, :].astype(BF), w_ref[...], TN)
        mixed = product[:64, :128] + product[64:, 128:]
        part = mid_ref[j].astype(F32) + gate[j * 64 : (j + 1) * 64] * mixed
        out_ref[j] = part.astype(BF)


def pair_output(sums, mid, normed, w_gate, w_out):
    return pl.pallas_call(
        output_kernel,
        out_shape=jax.ShapeDtypeStruct((8, 64, 128), BF),
        scratch_shapes=[pltpu.VMEM((64, 8, 128), F32)],
        name="pair_output",
    )(sums, mid, normed, w_gate, w_out)


def swap(x, mask):
    return lax.ppermute(x, "col", [(c, c ^ mask) for c in range(8)])


def to_targets(x):
    s = x.reshape(4, 2, 4, 8, 2, 128)
    return jnp.transpose(s, (2, 1, 3, 4, 0, 5)).reshape(64, 8, 128)


def local(
    alignment,
    pair_features,
    w_row,
    row_output_weight,
    w_bias,
    w_column,
    column_output_weight,
    outer_input_weight,
    w_outer_out,
    w_triangle_in,
    w_triangle_gate,
    w_triangle_out,
):
    branch = lax.axis_index("branch")
    row = lax.axis_index("row")
    col = lax.axis_index("col")
    place = col.reshape(1).astype(jnp.int32)
    both = ("branch", "row")

    near, far = {0: alignment}, {}
    for mask in (2, 6, 4):
        near[mask] = swap(alignment, mask)
    for mask in (0, 2, 6, 4):
        far[mask ^ 1] = swap(near[mask], 1)
    blocks = [(near | far)[m] for m in range(8)]

    pair_normed = layer_norm(pair_features).astype(BF)
    bias_tile = jnp.einsum(
        "ijc,ch->jhi", pair_normed, w_bias, preferred_element_type=F32
    ).astype(BF)
    bias_tile = bias_tile.reshape(32, 512)
    bias = lax.all_to_all(
        jnp.broadcast_to(bias_tile[None], (16, 32, 512)), "row", 0, 0, tiled=True
    ).reshape(512, 512)

    pair_part = lax.dynamic_slice_in_dim(pair_features, branch * 8, 8, 1)
    pair_part = jnp.transpose(pair_part.reshape(2, 4, 8, 8, 128), (3, 1, 0, 2, 4))
    pair_part = pair_part.reshape(8, 64, 128)

    alignment_row = row_attention(place, blocks, w_row, bias, row_output_weight)
    columns = lax.all_to_all(to_targets(alignment_row), both, 0, 0, tiled=True)
    columns = jnp.transpose(columns.reshape(64, 2, 4, 128), (0, 2, 1, 3)).reshape(256, 256)
    column_new, factors = column_attention(
        columns, w_column, column_output_weight, outer_input_weight
    )

    left = lax.all_to_all(
        jnp.broadcast_to(factors[None, :32], (64, 32, 256)), both, 0, 0, tiled=True
    )
    right = factors[None, 32:]
    right = jnp.concatenate([right, swap(right, 1)])
    right = jnp.concatenate([right, swap(right, 2)])
    right = jnp.concatenate([right, swap(right, 6)])
    relative = jnp.arange(8, dtype=jnp.int32) ^ col.astype(jnp.int32)
    position = jnp.where(relative >= 4, relative ^ 2, relative)
    right = lax.all_to_all(pick(position, right), "row", 0, 0, tiled=True)
    right = lax.dynamic_slice_in_dim(right, (row % 2) * 8, 8, 0)

    outer = jnp.einsum("ncs,jes->jnce", left, right, preferred_element_type=F32) * (1.0 / 256)
    update = jnp.dot(
        outer.reshape(512, 1024).astype(BF), w_outer_out, preferred_element_type=F32
    ).astype(BF)
    pair_mid = (pair_part.reshape(512, 128).astype(F32) + update.astype(F32)).astype(BF)
    tri_normed = layer_norm(pair_mid).astype(BF)
    sides = triangle_sides(tri_normed, w_triangle_in)

    returning = jnp.transpose(column_new.reshape(64, 4, 2, 128), (0, 2, 1, 3))
    message = jnp.concatenate([sides, returning.reshape(64, 1, 8, 128)], axis=1)
    message = lax.all_to_all(message, both, 0, 0, tiled=True)
    back = message[:, 2].reshape(4, 2, 8, 2, 4, 128)
    alignment_out = jnp.transpose(back, (4, 1, 0, 2, 3, 5)).reshape(4, 64, 256)
    tri_left = message[:, 0].reshape(512, 128)
    tri_right = message[:, 1].reshape(512, 128)
    near, far = {0: tri_right}, {}
    for mask in (2, 6, 4):
        near[mask] = swap(tri_right, mask)
    for mask in (0, 2, 6, 4):
        far[mask ^ 1] = swap(near[mask], 1)
    rights = [(near | far)[m] for m in range(8)]
    sums = triangle_sums(place, tri_left, rights)
    sums = lax.all_to_all(sums, both, 0, 0, tiled=True)
    w_out = jnp.concatenate([w_triangle_out[:64], w_triangle_out[64:]], axis=1)
    pair_new = pair_output(sums, pair_mid.reshape(8, 64, 128), tri_normed, w_triangle_gate, w_out)

    parts = jnp.transpose(pair_new.reshape(8, 64, 4, 32), (2, 0, 1, 3))
    parts = lax.all_to_all(parts, "branch", 0, 0, tiled=True)
    parts = parts.reshape(4, 8, 4, 2, 8, 32)
    pair_out = jnp.transpose(parts, (3, 2, 4, 0, 1, 5)).reshape(64, 32, 32)
    return (alignment_out, pair_out)


def solution(mesh):
    in_specs = (P(("branch", "row"), "col", None), P("col", "row", None)) + (P(),) * 10
    out_specs = (P(("branch", "row"), "col", None), P("col", "row", "branch"))
    return jax.shard_map(local, mesh=mesh, in_specs=in_specs, out_specs=out_specs, check_vma=False)
```

```python
import jax
import jax.numpy as jnp
from jax import lax
from jax.experimental import pallas as pl
from jax.experimental.pallas import tpu as pltpu
from jax.sharding import PartitionSpec as P


BF = jnp.bfloat16
F32 = jnp.float32
EPSILON = 1e-05
SCALE = 32**-0.5

NT = (((1,), (1,)), ((), ()))
TN = (((0,), (0,)), ((), ()))


def mm(a, b, dims):
    return lax.dot_general(a, b, dims, preferred_element_type=F32)


def layer_norm(inputs):
    inputs = inputs.astype(F32)
    average = jnp.mean(inputs, axis=-1, keepdims=True)
    centered = inputs - average
    variance = jnp.mean(jnp.square(centered), axis=-1, keepdims=True)
    return centered * lax.rsqrt(variance + EPSILON)


def sigmoid(x):
    return 1.0 / (1.0 + jnp.exp(-x))


def exp_rows(scores):
    top = jnp.max(scores, axis=0, keepdims=True)
    weights = jnp.exp(scores - top)
    total = jnp.sum(weights, axis=0, keepdims=True)
    return weights.astype(BF), 1.0 / total


def row_kernel(places, *refs):
    blocks = refs[:8]
    w_ref, bias_ref, wo_ref, out_ref, rows, packed = refs[8:]
    s = pl.program_id(0)
    own = None
    for m in range(8):
        normed = layer_norm(blocks[m][0]).astype(BF)
        if m == 0:
            own = normed
        start = pl.multiple_of(places[m] * 64, 64)
        rows[pl.ds(start, 64), :] = normed
    x = rows[...]
    key = mm(x, w_ref[256:512], NT).astype(BF)
    value_t = mm(w_ref[512:768], x, NT).astype(BF)
    query_t = (mm(w_ref[0:256], own, NT) * SCALE).astype(BF)
    gate_t = sigmoid(mm(w_ref[768:1024], own, NT))
    twice = jnp.concatenate([query_t, query_t], axis=1)
    head_row = lax.broadcasted_iota(jnp.int32, (256, 128), 0) // 32
    head_lane = lax.broadcasted_iota(jnp.int32, (256, 128), 1) // 64
    upper = lax.broadcasted_iota(jnp.int32, (64, 64), 0) < 32
    parts = []
    for p in range(4):
        diag = jnp.where(head_row == 2 * p + head_lane, twice, jnp.zeros_like(twice))
        scores = jnp.dot(key, diag, preferred_element_type=F32)
        scores = scores + bias_ref[:, p * 128 : (p + 1) * 128].astype(F32)
        weights, scale = exp_rows(scores)
        mixed = jnp.dot(value_t[p * 64 : (p + 1) * 64], weights, preferred_element_type=F32)
        mixed = mixed * scale
        parts.append(jnp.where(upper, mixed[:, :64], mixed[:, 64:]))
    attended_t = jnp.concatenate(parts, axis=0)
    gated = (gate_t * attended_t).astype(BF)
    result = blocks[0][0].astype(F32) + mm(gated, wo_ref[...], TN)
    for h in range(2):
        for b in range(4):
            source = (h * 4 + b) * 8
            target = (b * 2 + h) * 8
            for half in range(2):
                packed[half, s, target : target + 8, :] = result[
                    source : source + 8, half * 128 : (half + 1) * 128
                ]

    @pl.when(s == 3)
    def _():
        parts = [packed[half, t][:, None, :] for half in range(2) for t in range(4)]
        out_ref[...] = jnp.concatenate(parts, axis=1).astype(BF)


def row_attention(places, blocks, w_row_t, bias, w_out):
    block = pl.BlockSpec((1, 64, 256), lambda s, p: (s, 0, 0))
    full = lambda *shape: pl.BlockSpec(shape, lambda s, p: (0,) * len(shape))
    return pl.pallas_call(
        row_kernel,
        out_shape=jax.ShapeDtypeStruct((64, 8, 128), BF),
        grid_spec=pltpu.PrefetchScalarGridSpec(
            num_scalar_prefetch=1,
            grid=(4,),
            in_specs=[block] * 8 + [full(1024, 256), full(512, 512), full(256, 256)],
            out_specs=full(64, 8, 128),
            scratch_shapes=[pltpu.VMEM((512, 256), BF), pltpu.VMEM((2, 4, 64, 128), F32)],
        ),
        name="row_attention",
    )(places, *blocks, w_row_t, bias, w_out)


def column_kernel(x_ref, w_ref, wo_ref, wf_ref, out_ref, left_ref, right_ref, scratch):
    scratch[...] = x_ref[...].astype(F32)
    x = jnp.concatenate(
        [
            jnp.concatenate([scratch[:, s, :], scratch[:, 4 + s, :]], axis=1)
            for s in range(4)
        ],
        axis=0,
    )
    normed = layer_norm(x).astype(BF)
    key = mm(normed, w_ref[256:512], NT).astype(BF)
    value_t = mm(w_ref[512:768], normed, NT).astype(BF)
    query_t = (mm(w_ref[0:256], normed, NT) * SCALE).astype(BF)
    gate_t = sigmoid(mm(w_ref[768:1024], normed, NT))
    head_row = lax.broadcasted_iota(jnp.int32, (256, 256), 0) // 32
    parts = []
    for h in range(8):
        diag = jnp.where(head_row == h, query_t, jnp.zeros_like(query_t))
        weights, scale = exp_rows(jnp.dot(key, diag, preferred_element_type=F32))
        mixed = jnp.dot(value_t[h * 32 : (h + 1) * 32], weights, preferred_element_type=F32)
        parts.append(mixed * scale)
    gated = (gate_t * jnp.concatenate(parts, axis=0)).astype(BF)
    result = (x + mm(gated, wo_ref[...], TN)).astype(BF)
    factors = mm(wf_ref[...], layer_norm(result).astype(BF), NT).astype(BF)
    left_ref[...] = factors[:32]
    right_ref[...] = factors[32:]
    wide = result.astype(F32)
    for s in range(4):
        for half in range(2):
            scratch[:, half * 4 + s, :] = wide[
                s * 64 : (s + 1) * 64, half * 128 : (half + 1) * 128
            ]
    out_ref[...] = scratch[...].astype(BF)


def column_attention(x, w_column_t, w_out, w_factor_t):
    factor = jax.ShapeDtypeStruct((32, 256), BF)
    return pl.pallas_call(
        column_kernel,
        out_shape=(jax.ShapeDtypeStruct((64, 8, 128), BF), factor, factor),
        scratch_shapes=[pltpu.VMEM((64, 8, 128), F32)],
        name="column_attention",
    )(x, w_column_t, w_out, w_factor_t)


def spread_kernel(index, left_ref, right_ref, out_ref):
    left = left_ref[...].reshape(128, 256)
    for r in range(16):
        out_ref[r, :128] = left
        out_ref[r, 128:] = right_ref[index[r // 2]]


def spread(index, left, right):
    full = lambda *shape: pl.BlockSpec(shape, lambda g, p: (0,) * len(shape))
    return pl.pallas_call(
        spread_kernel,
        out_shape=jax.ShapeDtypeStruct((16, 160, 256), BF),
        grid_spec=pltpu.PrefetchScalarGridSpec(
            num_scalar_prefetch=1,
            grid=(1,),
            in_specs=[full(4, 32, 256), full(8, 32, 256)],
            out_specs=full(16, 160, 256),
        ),
        name="spread",
    )(index, left, right)


def block_transpose(arrays):
    rows = arrays[0].shape[0]
    lane = lax.broadcasted_iota(jnp.int32, (rows, 128), 1)
    low = lane < 64
    even = (lane // 32) % 2 == 0
    a0, a1, a2, a3 = arrays
    u0 = jnp.where(low, a0, pltpu.roll(a2, 64, 1))
    u2 = jnp.where(low, pltpu.roll(a0, 64, 1), a2)
    u1 = jnp.where(low, a1, pltpu.roll(a3, 64, 1))
    u3 = jnp.where(low, pltpu.roll(a1, 64, 1), a3)
    b0 = jnp.where(even, u0, pltpu.roll(u1, 32, 1))
    b1 = jnp.where(even, pltpu.roll(u0, 96, 1), u1)
    b2 = jnp.where(even, u2, pltpu.roll(u3, 32, 1))
    b3 = jnp.where(even, pltpu.roll(u2, 96, 1), u3)
    return b0, b1, b2, b3


def pair_kernel(half_ref, factor_ref, pair_ref, wo_ref, w_ref, back_ref, mid_ref, out_ref,
                outer, flat, scratch):
    start = half_ref[0] * 8
    right = factor_ref[pl.ds(start, 8), 128:, :].reshape(256, 256)
    for b in range(4):
        left = factor_ref[:, b * 32 : (b + 1) * 32, :].reshape(512, 256)
        product = mm(left, right, NT) * (1.0 / 256)
        outer[b * 16 : (b + 1) * 16] = product.reshape(16, 32, 256)
    for group in range(8):
        chans = [outer[:, group * 4 + k, :] for k in range(4)]
        for tile in range(2):
            moved = block_transpose([c[:, tile * 128 : (tile + 1) * 128] for c in chans])
            for k in range(4):
                j = tile * 4 + k
                flat[j * 64 : (j + 1) * 64, group * 128 : (group + 1) * 128] = moved[k].astype(BF)
    update = jnp.dot(flat[...], wo_ref[...], preferred_element_type=F32).astype(BF)
    mid = (pair_ref[...].astype(F32) + update.astype(F32)).astype(BF)
    mid_ref[...] = mid
    rows = layer_norm(mid).astype(BF)
    lane = lax.broadcasted_iota(jnp.int32, (64, 128), 1) < 64
    for side in range(2):
        base = side * 256
        value = mm(w_ref[base : base + 128], rows, NT)
        gate = mm(w_ref[base + 128 : base + 256], rows, NT)
        both = sigmoid(gate) * value
        for pair in range(4):
            low = both[:64, pair * 128 : (pair + 1) * 128]
            high = both[64:, pair * 128 : (pair + 1) * 128]
            scratch[side, :, 2 * pair, :] = jnp.where(lane, low, pltpu.roll(high, 64, 1))
            scratch[side, :, 2 * pair + 1, :] = jnp.where(lane, pltpu.roll(low, 64, 1), high)
    out_ref[:, 0] = scratch[0].astype(BF)
    out_ref[:, 1] = scratch[1].astype(BF)
    out_ref[:, 2] = back_ref[...]


def pair_update(half, factors, pair_part, w_outer, w_in_t, returning):
    full = lambda *shape: pl.BlockSpec(shape, lambda g, p: (0,) * len(shape))
    return pl.pallas_call(
        pair_kernel,
        out_shape=(
            jax.ShapeDtypeStruct((512, 128), BF),
            jax.ShapeDtypeStruct((64, 3, 8, 128), BF),
        ),
        grid_spec=pltpu.PrefetchScalarGridSpec(
            num_scalar_prefetch=1,
            grid=(1,),
            in_specs=[
                full(16, 160, 256),
                full(512, 128),
                full(1024, 128),
                full(512, 128),
                full(64, 8, 128),
            ],
            out_specs=(full(512, 128), full(64, 3, 8, 128)),
            scratch_shapes=[
                pltpu.VMEM((64, 32, 256), F32),
                pltpu.VMEM((512, 1024), BF),
                pltpu.VMEM((2, 64, 8, 128), F32),
            ],
        ),
        name="pair_update",
    )(half, factors, pair_part, w_outer, w_in_t, returning)


def triangle_kernel(places, left_ref, *refs):
    rights, out_ref = refs[:8], refs[8]
    left = left_ref[...]
    lane = lax.broadcasted_iota(jnp.int32, (64, 128), 1) < 64
    for m in range(8):
        product = mm(rights[m][...], left, TN)
        block = jnp.where(lane, product[:64], product[64:]).astype(BF)
        target = places[m] * 2
        for b in range(4):
            for h in range(2):
                out_ref[b * 16 + target + h] = block[(b * 2 + h) * 8 : (b * 2 + h + 1) * 8]


def triangle_sums(places, left, rights):
    full = lambda *shape: pl.BlockSpec(shape, lambda g, p: (0,) * len(shape))
    return pl.pallas_call(
        triangle_kernel,
        out_shape=jax.ShapeDtypeStruct((64, 8, 128), BF),
        grid_spec=pltpu.PrefetchScalarGridSpec(
            num_scalar_prefetch=1,
            grid=(1,),
            in_specs=[full(512, 128)] * 9,
            out_specs=full(64, 8, 128),
        ),
        name="triangle_sums",
    )(places, left, *rights)


def output_kernel(sum_ref, mid_ref, wg_ref, w_ref, out_ref, scratch):
    sums = sum_ref[...].astype(F32)
    fold = lambda v: (v + pltpu.roll(v, 64, 1)) * (1.0 / 128)
    average = fold(jnp.sum(sums, axis=0))
    centered = sums - average[None]
    variance = fold(jnp.sum(jnp.square(centered), axis=0))
    scratch[...] = centered * lax.rsqrt(variance + EPSILON)[None]
    mid = mid_ref[...]
    rows = layer_norm(mid).astype(BF)
    gate = sigmoid(jnp.dot(rows, wg_ref[...], preferred_element_type=F32))
    for j in range(8):
        product = mm(scratch[:, j, :].astype(BF), w_ref[...], TN)
        mixed = product[:64, :128] + product[64:, 128:]
        part = mid[j * 64 : (j + 1) * 64].astype(F32) + gate[j * 64 : (j + 1) * 64] * mixed
        moved = block_transpose([part[u * 16 : (u + 1) * 16] for u in range(4)])
        for b in range(4):
            out_ref[b, j] = moved[b].astype(BF)


def pair_output(sums, mid, w_gate, w_out):
    return pl.pallas_call(
        output_kernel,
        out_shape=jax.ShapeDtypeStruct((4, 8, 16, 128), BF),
        scratch_shapes=[pltpu.VMEM((64, 8, 128), F32)],
        name="pair_output",
    )(sums, mid, w_gate, w_out)


def shifted(x, step, flip):
    perm = [(c, (c // 2 - step) % 4 * 2 + (c % 2 ^ flip)) for c in range(8)]
    return lax.ppermute(x, "col", perm)


def gather_col(x):
    parts = {(0, 0): x}
    for step in (1, 2, 3):
        parts[step, 0] = shifted(x, step, 0)
    for step in (0, 1, 3, 2):
        parts[step, 1] = shifted(parts[step, 0], 0, 1)
    return [parts[m // 2, m % 2] for m in range(8)]


def local(
    alignment,
    pair_features,
    w_row,
    row_output_weight,
    w_bias,
    w_column,
    column_output_weight,
    outer_input_weight,
    w_outer_out,
    w_triangle_in,
    w_triangle_gate,
    w_triangle_out,
):
    branch = lax.axis_index("branch").astype(jnp.int32)
    row = lax.axis_index("row").astype(jnp.int32)
    col = lax.axis_index("col").astype(jnp.int32)
    both = ("branch", "row")
    order = jnp.arange(8, dtype=jnp.int32)
    places = (col // 2 + order // 2) % 4 * 2 + (col % 2 ^ order % 2)

    blocks = gather_col(alignment)
    w_row_t = w_row.T
    w_column_t = w_column.T
    w_factor_t = outer_input_weight.T
    w_in_t = w_triangle_in.T
    w_out = jnp.concatenate([w_triangle_out[:64], w_triangle_out[64:]], axis=1)
    pair_part = lax.dynamic_slice_in_dim(pair_features, branch * 8, 8, 1)
    pair_part = jnp.transpose(pair_part.reshape(2, 4, 8, 8, 128), (3, 1, 0, 2, 4))
    pair_part = pair_part.reshape(512, 128)
    pair_normed = layer_norm(pair_features).astype(BF)
    bias_tile = jnp.einsum(
        "ijc,ch->jhi", pair_normed, w_bias, preferred_element_type=F32
    ).astype(BF)
    bias_tile = jnp.broadcast_to(bias_tile.reshape(1, 32, 512), (16, 32, 512))
    bias = lax.all_to_all(bias_tile, "row", 0, 0, tiled=True).reshape(512, 512)

    columns = row_attention(places, blocks, w_row_t, bias, row_output_weight)
    columns = lax.all_to_all(columns, both, 0, 0, tiled=True)
    returning, left, right = column_attention(
        columns, w_column_t, column_output_weight, w_factor_t
    )

    right = jnp.stack([right, shifted(right, 0, 1)])
    rights = [right] + [shifted(right, step, 0) for step in (1, 2, 3)]
    left = lax.all_to_all(jnp.broadcast_to(left[None], (4, 32, 256)), "branch", 0, 0, tiled=True)
    rights = jnp.concatenate(rights)
    position = (order // 2 - col // 2) % 4 * 2 + (order % 2 ^ col % 2)
    factors = lax.all_to_all(spread(position, left, rights), "row", 0, 0, tiled=True)

    half = (row % 2).reshape(1)
    mid, message = pair_update(half, factors, pair_part, w_outer_out, w_in_t, returning)
    message = lax.all_to_all(message, both, 0, 0, tiled=True)
    tri_left = message[:, 0].reshape(512, 128)
    rights = gather_col(message[:, 1].reshape(512, 128))
    back = message[:, 2].reshape(4, 2, 8, 2, 4, 128)
    alignment_out = jnp.transpose(back, (4, 1, 0, 2, 3, 5)).reshape(4, 64, 256)
    sums = triangle_sums(places, tri_left, rights)
    sums = lax.all_to_all(sums, both, 0, 0, tiled=True)
    parts = pair_output(sums, mid, w_triangle_gate, w_out)
    parts = lax.all_to_all(parts, "branch", 0, 0, tiled=True)
    parts = parts.reshape(4, 8, 2, 8, 4, 32)
    pair_out = jnp.transpose(parts, (2, 4, 3, 0, 1, 5)).reshape(64, 32, 32)
    return (alignment_out, pair_out)


def solution(mesh):
    in_specs = (P(("branch", "row"), "col", None), P("col", "row", None)) + (P(),) * 10
    out_specs = (P(("branch", "row"), "col", None), P("col", "row", "branch"))
    return jax.shard_map(local, mesh=mesh, in_specs=in_specs, out_specs=out_specs, check_vma=False)
```

```python
import jax
import jax.numpy as jnp
from jax import lax
from jax.experimental import pallas as pl
from jax.experimental.pallas import tpu as pltpu
from jax.sharding import PartitionSpec as P


BF = jnp.bfloat16
F32 = jnp.float32
EPSILON = 1e-05
SCALE = 32**-0.5

NT = (((1,), (1,)), ((), ()))
TN = (((0,), (0,)), ((), ()))
TT = (((0,), (1,)), ((), ()))


def mm(a, b, dims):
    return lax.dot_general(a, b, dims, preferred_element_type=F32)


def layer_norm(inputs):
    inputs = inputs.astype(F32)
    average = jnp.mean(inputs, axis=-1, keepdims=True)
    centered = inputs - average
    variance = jnp.mean(jnp.square(centered), axis=-1, keepdims=True)
    return centered * lax.rsqrt(variance + EPSILON)


def sigmoid(x):
    return 1.0 / (1.0 + jnp.exp(-x))


def exp_rows(scores):
    top = jnp.max(scores, axis=0, keepdims=True)
    weights = jnp.exp(scores - top)
    total = jnp.sum(weights, axis=0, keepdims=True)
    return weights.astype(BF), 1.0 / total


VM = pl.BlockSpec(memory_space=pltpu.VMEM)
SM = pl.BlockSpec(memory_space=pltpu.SMEM)


def in_vmem(kernel, outs, scratch, place, *args):
    args = [pltpu.with_memory_space_constraint(a, pltpu.VMEM) for a in args]
    outs = tuple(pltpu.VMEM(shape, BF) for shape in outs)
    results = pl.pallas_call(
        kernel,
        out_shape=outs,
        in_specs=[SM] + [VM] * len(args),
        out_specs=(VM,) * len(outs),
        scratch_shapes=scratch,
    )(place, *args)
    return results if len(outs) > 1 else results[0]


def source_of(col, m):
    return (((col >> 1) + (m >> 1)) & 3) * 2 + ((col & 1) ^ (m & 1))


def bias_kernel(place, pair_ref, w_ref, out_ref, rows, heads):
    del place
    normed = layer_norm(pair_ref[...].reshape(2048, 128)).astype(BF).astype(F32)
    rows[...] = normed.reshape(64, 32, 128)
    weight = w_ref[...]
    for j in range(16):
        pairs = jnp.concatenate([rows[:, j, :], rows[:, j + 16, :]], axis=0).astype(BF)
        heads[j] = mm(weight, pairs, TT)
    lane = lax.broadcasted_iota(jnp.int32, (16, 128), 1) < 64
    tiles = []
    for p in range(4):
        a = heads[:, 2 * p, :]
        b = heads[:, 2 * p + 1, :]
        first = jnp.where(lane, a, pltpu.roll(b, 64, 1))
        second = jnp.where(lane, pltpu.roll(a, 64, 1), b)
        tiles.append(jnp.concatenate([first, second], axis=0))
    tile = jnp.concatenate(tiles, axis=1).astype(BF)
    for r in range(16):
        out_ref[r] = tile


def row_kernel(place, *refs):
    blocks = refs[:8]
    w_ref, bias_ref, wo_ref, out_ref, rows, keys, values, packed = refs[8:]
    for m in range(8):
        start = pl.multiple_of(source_of(place[0], m) * 64, 64)
        normed = layer_norm(blocks[m][...].reshape(256, 256)).astype(BF)
        if m == 0:
            own = normed
        for s in range(4):
            rows[s, pl.ds(start, 64), :] = normed[s * 64 : (s + 1) * 64]
    x = rows[...].reshape(2048, 256)
    keys[...] = jnp.dot(x, w_ref[:, 256:512], preferred_element_type=F32).astype(BF)
    values[...] = mm(w_ref[:, 512:768], x, TT).astype(BF)
    query_t = (mm(w_ref[:, 0:256], own, TT) * SCALE).astype(BF)
    gate_t = sigmoid(mm(w_ref[:, 768:1024], own, TT))
    head_row = lax.broadcasted_iota(jnp.int32, (256, 128), 0) // 32
    head_lane = lax.broadcasted_iota(jnp.int32, (256, 128), 1) // 64
    upper = lax.broadcasted_iota(jnp.int32, (64, 64), 0) < 32
    for s in range(4):
        mine = query_t[:, s * 64 : (s + 1) * 64]
        twice = jnp.concatenate([mine, mine], axis=1)
        key = keys[s * 512 : (s + 1) * 512]
        parts = []
        for p in range(4):
            diag = jnp.where(head_row == 2 * p + head_lane, twice, jnp.zeros_like(twice))
            scores = jnp.dot(key, diag, preferred_element_type=F32)
            scores = scores + bias_ref[:, p * 128 : (p + 1) * 128].astype(F32)
            weights, scale = exp_rows(scores)
            mixed = jnp.dot(
                values[p * 64 : (p + 1) * 64, s * 512 : (s + 1) * 512],
                weights,
                preferred_element_type=F32,
            )
            mixed = mixed * scale
            parts.append(jnp.where(upper, mixed[:, :64], mixed[:, 64:]))
        attended_t = jnp.concatenate(parts, axis=0)
        gated = (gate_t[:, s * 64 : (s + 1) * 64] * attended_t).astype(BF)
        result = blocks[0][s].astype(F32) + mm(gated, wo_ref[...], TN)
        for h in range(2):
            for b in range(4):
                source = (h * 4 + b) * 8
                target = (b * 2 + h) * 8
                for half in range(2):
                    packed[target : target + 8, half * 4 + s, :] = result[
                        source : source + 8, half * 128 : (half + 1) * 128
                    ]
    out_ref[...] = packed[...].astype(BF)


def column_kernel(place, x_ref, w_ref, wo_ref, wf_ref, out_ref, left_ref, right_ref, scratch):
    del place
    scratch[...] = x_ref[...].astype(F32)
    x = jnp.concatenate(
        [
            jnp.concatenate([scratch[:, s, :], scratch[:, 4 + s, :]], axis=1)
            for s in range(4)
        ],
        axis=0,
    )
    normed = layer_norm(x).astype(BF)
    key = jnp.dot(normed, w_ref[:, 256:512], preferred_element_type=F32).astype(BF)
    value_t = mm(w_ref[:, 512:768], normed, TT).astype(BF)
    query_t = (mm(w_ref[:, 0:256], normed, TT) * SCALE).astype(BF)
    gate_t = sigmoid(mm(w_ref[:, 768:1024], normed, TT))
    head_row = lax.broadcasted_iota(jnp.int32, (256, 256), 0) // 32
    parts = []
    for h in range(8):
        diag = jnp.where(head_row == h, query_t, jnp.zeros_like(query_t))
        weights, scale = exp_rows(jnp.dot(key, diag, preferred_element_type=F32))
        mixed = jnp.dot(value_t[h * 32 : (h + 1) * 32], weights, preferred_element_type=F32)
        parts.append(mixed * scale)
    gated = (gate_t * jnp.concatenate(parts, axis=0)).astype(BF)
    result = (x + mm(gated, wo_ref[...], TN)).astype(BF)
    factors = mm(wf_ref[...], layer_norm(result).astype(BF), TT).astype(BF)
    for b in range(4):
        left_ref[b] = factors[:32]
    right_ref[...] = factors[32:]
    wide = result.astype(F32)
    for s in range(4):
        for half in range(2):
            scratch[:, half * 4 + s, :] = wide[
                s * 64 : (s + 1) * 64, half * 128 : (half + 1) * 128
            ]
    out_ref[...] = scratch[...].astype(BF)


def spread_kernel(place, left_ref, *refs):
    rights, out_ref = refs[:4], refs[4]
    left = left_ref[...].reshape(128, 256)
    for r in range(16):
        out_ref[r, :128] = left
    for m in range(8):
        target = source_of(place[0], m) * 2
        block = rights[m // 2][m % 2]
        out_ref[target, 128:] = block
        out_ref[target + 1, 128:] = block


def block_transpose(arrays):
    rows = arrays[0].shape[0]
    lane = lax.broadcasted_iota(jnp.int32, (rows, 128), 1)
    low = lane < 64
    even = (lane // 32) % 2 == 0
    a0, a1, a2, a3 = arrays
    u0 = jnp.where(low, a0, pltpu.roll(a2, 64, 1))
    u2 = jnp.where(low, pltpu.roll(a0, 64, 1), a2)
    u1 = jnp.where(low, a1, pltpu.roll(a3, 64, 1))
    u3 = jnp.where(low, pltpu.roll(a1, 64, 1), a3)
    b0 = jnp.where(even, u0, pltpu.roll(u1, 32, 1))
    b1 = jnp.where(even, pltpu.roll(u0, 96, 1), u1)
    b2 = jnp.where(even, u2, pltpu.roll(u3, 32, 1))
    b3 = jnp.where(even, pltpu.roll(u2, 96, 1), u3)
    return b0, b1, b2, b3


def by_target(rows):
    order = [(h * 4 + b) * 8 for b in range(4) for h in range(2)]
    count = rows.shape[0] // 64
    return jnp.concatenate(
        [rows[j * 64 + s : j * 64 + s + 8] for j in range(count) for s in order], axis=0
    )


def pair_kernel(place, factor_ref, pair_ref, wo_ref, w_ref, mid_ref, out_ref,
                outer, flat, scratch, tile_rows):
    right = factor_ref[pl.ds(place[1] * 8, 8), 128:, :].reshape(256, 256)
    for b in range(4):
        left = factor_ref[:, b * 32 : (b + 1) * 32, :].reshape(512, 256)
        product = (mm(left, right, NT) * (1.0 / 256)).reshape(16, 32, 256)
        for h in range(2):
            start = (h * 4 + b) * 8
            outer[start : start + 8] = product[h * 8 : (h + 1) * 8]
    for group in range(8):
        chans = [outer[:, group * 4 + k, :] for k in range(4)]
        for tile in range(2):
            moved = block_transpose([c[:, tile * 128 : (tile + 1) * 128] for c in chans])
            for k in range(4):
                j = tile * 4 + k
                flat[j * 64 : (j + 1) * 64, group * 128 : (group + 1) * 128] = moved[k].astype(BF)
    update = jnp.dot(flat[...], wo_ref[...], preferred_element_type=F32).astype(BF)
    first = pl.multiple_of(place[2] * 8, 8)
    tile_rows[...] = pair_ref[:, pl.ds(first, 8), :].astype(F32)
    pair = jnp.concatenate([tile_rows[:, j, :] for j in range(8)], axis=0)
    mid = (pair + update.astype(F32)).astype(BF)
    mid_ref[...] = mid
    normed = layer_norm(mid)
    lane = lax.broadcasted_iota(jnp.int32, (64, 128), 1) < 64
    for side in range(2):
        rows = (by_target(normed) if side else normed).astype(BF)
        base = side * 256
        value = mm(w_ref[:, base : base + 128], rows, TT)
        gate = mm(w_ref[:, base + 128 : base + 256], rows, TT)
        both = sigmoid(gate) * value
        for pair in range(4):
            low = both[:64, pair * 128 : (pair + 1) * 128]
            high = both[64:, pair * 128 : (pair + 1) * 128]
            scratch[side, :, 2 * pair, :] = jnp.where(lane, low, pltpu.roll(high, 64, 1))
            scratch[side, :, 2 * pair + 1, :] = jnp.where(lane, pltpu.roll(low, 64, 1), high)
    out_ref[:, 0] = scratch[0].astype(BF)
    out_ref[:, 1] = scratch[1].astype(BF)


def triangle_kernel(place, left_ref, back_ref, *refs):
    rights, out_ref = refs[:8], refs[8]
    left = left_ref[...]
    lane = lax.broadcasted_iota(jnp.int32, (64, 128), 1) < 64
    for m in range(8):
        product = mm(rights[m][...], left, TN)
        block = jnp.where(lane, product[:64], product[64:]).astype(BF)
        target = source_of(place[0], m) * 2
        for b in range(4):
            for h in range(2):
                out_ref[b * 16 + target + h, 0] = block[(b * 2 + h) * 8 : (b * 2 + h + 1) * 8]
    out_ref[:, 1] = back_ref[...]


def output_kernel(place, sum_ref, mid_ref, wg_ref, w_ref, out_ref, scratch):
    del place
    sums = sum_ref[:, 0].astype(F32)
    fold = lambda v: (v + pltpu.roll(v, 64, 1)) * (1.0 / 128)
    average = fold(jnp.sum(sums, axis=0))
    centered = sums - average[None]
    variance = fold(jnp.sum(jnp.square(centered), axis=0))
    scratch[...] = centered * lax.rsqrt(variance + EPSILON)[None]
    mid = mid_ref[...].astype(F32)
    gate_t = sigmoid(mm(wg_ref[...], layer_norm(mid).astype(BF), TT))
    weight = jnp.concatenate([w_ref[:64], w_ref[64:]], axis=1)
    lane = lax.broadcasted_iota(jnp.int32, (128, 128), 1) < 64

    def mixed_of(j):
        product = mm(weight, scratch[:, j, :].astype(BF), TN)
        return product[:128, :64] + product[128:, 64:]

    for j in range(4):
        mixed = jnp.concatenate([mixed_of(j), mixed_of(j + 4)], axis=1)
        ends = (slice(j * 64, (j + 1) * 64), slice((j + 4) * 64, (j + 5) * 64))
        residual = jnp.concatenate([mid[e] for e in ends], axis=0).T
        gate = jnp.concatenate([gate_t[:, e] for e in ends], axis=1)
        part = (residual + gate * mixed).astype(BF)
        for b in range(4):
            out_ref[b, j] = part[b * 32 : (b + 1) * 32]


def unpack_kernel(x_ref, out_ref):
    for b in range(4):
        for j in range(4):
            block = x_ref[b, j]
            out_ref[b * 8 + j] = block[:, :64]
            out_ref[b * 8 + 4 + j] = block[:, 64:]


def shifted(x, step, flip):
    perm = [(c, (c // 2 - step) % 4 * 2 + (c % 2 ^ flip)) for c in range(8)]
    return lax.ppermute(x, "col", perm)


def gather_col(x):
    parts = {(0, 0): x}
    for step in (1, 3, 2):
        parts[step, 0] = shifted(x, step, 0)
    for step in (0, 1, 3, 2):
        parts[step, 1] = shifted(parts[step, 0], 0, 1)
    return [parts[m // 2, m % 2] for m in range(8)]


def local(
    alignment,
    pair_features,
    w_row,
    row_output_weight,
    w_bias,
    w_column,
    column_output_weight,
    outer_input_weight,
    w_outer_out,
    w_triangle_in,
    w_triangle_gate,
    w_triangle_out,
):
    both = ("branch", "row")
    place = jnp.stack(
        [lax.axis_index("col"), lax.axis_index("row") & 1, lax.axis_index("branch")]
    ).astype(jnp.int32)
    exchange = lambda x, axis: lax.all_to_all(x, axis, 0, 0, tiled=True)

    blocks = gather_col(alignment)
    bias = in_vmem(
        bias_kernel,
        [(16, 32, 512)],
        [pltpu.VMEM((64, 32, 128), F32), pltpu.VMEM((16, 8, 128), F32)],
        place,
        pair_features,
        w_bias,
    )
    bias = exchange(bias, "row").reshape(512, 512)

    columns = in_vmem(
        row_kernel,
        [(64, 8, 128)],
        [
            pltpu.VMEM((4, 512, 256), BF),
            pltpu.VMEM((2048, 256), BF),
            pltpu.VMEM((256, 2048), BF),
            pltpu.VMEM((64, 8, 128), F32),
        ],
        place,
        *blocks,
        w_row,
        bias,
        row_output_weight,
    )
    columns = exchange(columns, both)
    returning, left, right = in_vmem(
        column_kernel,
        [(64, 8, 128), (4, 32, 256), (32, 256)],
        [pltpu.VMEM((64, 8, 128), F32)],
        place,
        columns,
        w_column,
        column_output_weight,
        outer_input_weight,
    )

    right = jnp.stack([right, shifted(right, 0, 1)])
    rights = [right]
    for step in (1, 2, 3):
        rights.append(shifted(right, step, 0))
    left = exchange(left, "branch")
    factors = in_vmem(spread_kernel, [(16, 160, 256)], [], place, left, *rights)
    factors = exchange(factors, "row")

    mid, message = in_vmem(
        pair_kernel,
        [(512, 128), (64, 2, 8, 128)],
        [
            pltpu.VMEM((64, 32, 256), F32),
            pltpu.VMEM((512, 1024), BF),
            pltpu.VMEM((2, 64, 8, 128), F32),
            pltpu.VMEM((64, 8, 128), F32),
        ],
        place,
        factors,
        pair_features,
        w_outer_out,
        w_triangle_in,
    )
    message = exchange(message, both)
    tri_left = message[:, 0].reshape(512, 128)
    rights = gather_col(message[:, 1].reshape(512, 128))
    sums = in_vmem(triangle_kernel, [(64, 2, 8, 128)], [], place, tri_left, returning, *rights)
    sums = exchange(sums, both)
    parts = in_vmem(
        output_kernel,
        [(4, 4, 32, 128)],
        [pltpu.VMEM((64, 8, 128), F32)],
        place,
        sums,
        mid,
        w_triangle_gate,
        w_triangle_out,
    )
    parts = exchange(parts, "branch")
    pair_out = pl.pallas_call(
        unpack_kernel, out_shape=jax.ShapeDtypeStruct((32, 32, 64), BF), name="unpack"
    )(parts)
    back = sums[:, 1].reshape(4, 2, 8, 2, 4, 128)
    alignment_out = jnp.transpose(back, (4, 1, 0, 2, 3, 5)).reshape(4, 64, 256)
    return (alignment_out, jnp.transpose(pair_out, (2, 0, 1)))


def solution(mesh):
    in_specs = (P(("branch", "row"), "col", None), P("col", "row", None)) + (P(),) * 10
    out_specs = (P(("branch", "row"), "col", None), P("col", "row", "branch"))
    return jax.shard_map(local, mesh=mesh, in_specs=in_specs, out_specs=out_specs, check_vma=False)
```

```python
import jax
import jax.numpy as jnp
from jax import lax
from jax.experimental import pallas as pl
from jax.experimental.pallas import tpu as pltpu
from jax.sharding import PartitionSpec as P


BF = jnp.bfloat16
F32 = jnp.float32
EPSILON = 1e-05
SCALE = 32**-0.5

NT = (((1,), (1,)), ((), ()))
TN = (((0,), (0,)), ((), ()))
TT = (((0,), (1,)), ((), ()))


def mm(a, b, dims):
    return lax.dot_general(a, b, dims, preferred_element_type=F32)


def layer_norm(inputs):
    inputs = inputs.astype(F32)
    average = jnp.mean(inputs, axis=-1, keepdims=True)
    centered = inputs - average
    variance = jnp.mean(jnp.square(centered), axis=-1, keepdims=True)
    return centered * lax.rsqrt(variance + EPSILON)


def sigmoid(x):
    return 1.0 / (1.0 + jnp.exp(-x))


def exp_rows(scores):
    top = jnp.max(scores, axis=0, keepdims=True)
    weights = jnp.exp(scores - top)
    total = jnp.sum(weights, axis=0, keepdims=True)
    return weights.astype(BF), 1.0 / total


VM = pl.BlockSpec(memory_space=pltpu.VMEM)
SM = pl.BlockSpec(memory_space=pltpu.SMEM)


def in_vmem(kernel, outs, scratch, place, *args):
    args = [pltpu.with_memory_space_constraint(a, pltpu.VMEM) for a in args]
    outs = tuple(pltpu.VMEM(shape, BF) for shape in outs)
    results = pl.pallas_call(
        kernel,
        out_shape=outs,
        in_specs=[SM] + [VM] * len(args),
        out_specs=(VM,) * len(outs),
        scratch_shapes=scratch,
    )(place, *args)
    return results if len(outs) > 1 else results[0]


def col_of(place):
    return place[0] & 7


def half_of(place):
    return (place[0] >> 3) & 1


def branch_of(place):
    return place[0] >> 7


def source_of(col, m):
    return (((col >> 1) + (m >> 1)) & 3) * 2 + ((col & 1) ^ (m & 1))


def bias_kernel(place, pair_ref, w_ref, out_ref, rows, heads):
    del place
    normed = layer_norm(pair_ref[...].reshape(2048, 128)).astype(BF).astype(F32)
    rows[...] = normed.reshape(64, 32, 128)
    weight = w_ref[...]
    for j in range(16):
        pairs = jnp.concatenate([rows[:, j, :], rows[:, j + 16, :]], axis=0).astype(BF)
        heads[j] = mm(weight, pairs, NT)
    lane = lax.broadcasted_iota(jnp.int32, (16, 128), 1) < 64
    tiles = []
    for p in range(4):
        a = heads[:, 2 * p, :]
        b = heads[:, 2 * p + 1, :]
        first = jnp.where(lane, a, pltpu.roll(b, 64, 1))
        second = jnp.where(lane, pltpu.roll(a, 64, 1), b)
        tiles.append(jnp.concatenate([first, second], axis=0))
    tile = jnp.concatenate(tiles, axis=1).astype(BF)
    for r in range(16):
        out_ref[r] = tile


def row_kernel(place, *refs):
    own_ref, z1_ref, z3_ref, z2_ref, swap_ref, last_ref = refs[:6]
    w_ref, bias_ref, wo_ref, out_ref, rows, keys, values, packed = refs[6:]
    for m, block in (
        (0, own_ref[...]),
        (2, z1_ref[...]),
        (6, z3_ref[...]),
        (1, swap_ref[0]),
        (3, swap_ref[1]),
        (7, swap_ref[2]),
        (4, z2_ref[...]),
        (5, last_ref[...]),
    ):
        start = pl.multiple_of(source_of(col_of(place), m) * 64, 64)
        normed = layer_norm(block.reshape(256, 256)).astype(BF)
        if m == 0:
            own = normed
        for s in range(4):
            rows[s, pl.ds(start, 64), :] = normed[s * 64 : (s + 1) * 64]
    x = rows[...].reshape(2048, 256)
    keys[...] = jnp.dot(x, w_ref[:, 256:512], preferred_element_type=F32).astype(BF)
    values[...] = mm(w_ref[:, 512:768], x, TT).astype(BF)
    query_t = (mm(w_ref[:, 0:256], own, TT) * SCALE).astype(BF)
    gate_t = sigmoid(mm(w_ref[:, 768:1024], own, TT))
    head_row = lax.broadcasted_iota(jnp.int32, (256, 128), 0) // 32
    head_lane = lax.broadcasted_iota(jnp.int32, (256, 128), 1) // 64
    upper = lax.broadcasted_iota(jnp.int32, (64, 64), 0) < 32
    for s in range(4):
        mine = query_t[:, s * 64 : (s + 1) * 64]
        twice = jnp.concatenate([mine, mine], axis=1)
        key = keys[s * 512 : (s + 1) * 512]
        parts = []
        for p in range(4):
            diag = jnp.where(head_row == 2 * p + head_lane, twice, jnp.zeros_like(twice))
            scores = jnp.dot(key, diag, preferred_element_type=F32)
            scores = scores + bias_ref[:, p * 128 : (p + 1) * 128].astype(F32)
            weights, scale = exp_rows(scores)
            mixed = jnp.dot(
                values[p * 64 : (p + 1) * 64, s * 512 : (s + 1) * 512],
                weights,
                preferred_element_type=F32,
            )
            mixed = mixed * scale
            parts.append(jnp.where(upper, mixed[:, :64], mixed[:, 64:]))
        attended_t = jnp.concatenate(parts, axis=0)
        gated = (gate_t[:, s * 64 : (s + 1) * 64] * attended_t).astype(BF)
        result = own_ref[s].astype(F32) + mm(gated, wo_ref[...], TN)
        for h in range(2):
            for b in range(4):
                source = (h * 4 + b) * 8
                target = (b * 2 + h) * 8
                for half in range(2):
                    packed[target : target + 8, half * 4 + s, :] = result[
                        source : source + 8, half * 128 : (half + 1) * 128
                    ]
    out_ref[...] = packed[...].astype(BF)


def column_kernel(place, x_ref, w_ref, wo_ref, wf_ref, out_ref, left_ref, right_ref, scratch):
    del place
    scratch[...] = x_ref[...].astype(F32)
    x = jnp.concatenate(
        [
            jnp.concatenate([scratch[:, s, :], scratch[:, 4 + s, :]], axis=1)
            for s in range(4)
        ],
        axis=0,
    )
    normed = layer_norm(x).astype(BF)
    key = jnp.dot(normed, w_ref[:, 256:512], preferred_element_type=F32).astype(BF)
    value_t = mm(w_ref[:, 512:768], normed, TT).astype(BF)
    query_t = (mm(w_ref[:, 0:256], normed, TT) * SCALE).astype(BF)
    gate_t = sigmoid(mm(w_ref[:, 768:1024], normed, TT))
    head_row = lax.broadcasted_iota(jnp.int32, (256, 256), 0) // 32
    parts = []
    for h in range(8):
        diag = jnp.where(head_row == h, query_t, jnp.zeros_like(query_t))
        weights, scale = exp_rows(jnp.dot(key, diag, preferred_element_type=F32))
        mixed = jnp.dot(value_t[h * 32 : (h + 1) * 32], weights, preferred_element_type=F32)
        parts.append(mixed * scale)
    gated = (gate_t * jnp.concatenate(parts, axis=0)).astype(BF)
    result = (x + mm(gated, wo_ref[...], TN)).astype(BF)
    factors = mm(wf_ref[...], layer_norm(result).astype(BF), NT).astype(BF)
    left_ref[...] = factors[:32]
    for c in range(8):
        right_ref[c] = factors[32:]
    wide = result.astype(F32)
    for s in range(4):
        for half in range(2):
            scratch[:, half * 4 + s, :] = wide[
                s * 64 : (s + 1) * 64, half * 128 : (half + 1) * 128
            ]
    out_ref[...] = scratch[...].astype(BF)


def spread_kernel(place, right_ref, *refs):
    lefts, out_ref = refs[:4], refs[4]
    blocks = [left[...] for left in lefts]
    for mask in range(4):
        start = pl.multiple_of((branch_of(place) ^ mask) * 32, 32)
        for r in range(16):
            out_ref[r, pl.ds(start, 32), :] = blocks[mask]
    for r in range(16):
        out_ref[r, 128:] = right_ref[r // 2]


def block_transpose(arrays):
    rows = arrays[0].shape[0]
    lane = lax.broadcasted_iota(jnp.int32, (rows, 128), 1)
    low = lane < 64
    even = (lane // 32) % 2 == 0
    a0, a1, a2, a3 = arrays
    u0 = jnp.where(low, a0, pltpu.roll(a2, 64, 1))
    u2 = jnp.where(low, pltpu.roll(a0, 64, 1), a2)
    u1 = jnp.where(low, a1, pltpu.roll(a3, 64, 1))
    u3 = jnp.where(low, pltpu.roll(a1, 64, 1), a3)
    b0 = jnp.where(even, u0, pltpu.roll(u1, 32, 1))
    b1 = jnp.where(even, pltpu.roll(u0, 96, 1), u1)
    b2 = jnp.where(even, u2, pltpu.roll(u3, 32, 1))
    b3 = jnp.where(even, pltpu.roll(u2, 96, 1), u3)
    return b0, b1, b2, b3


def by_target(rows):
    order = [(h * 4 + b) * 8 for b in range(4) for h in range(2)]
    count = rows.shape[0] // 64
    return jnp.concatenate(
        [rows[j * 64 + s : j * 64 + s + 8] for j in range(count) for s in order], axis=0
    )


def pair_kernel(place, factor_ref, pair_ref, wo_ref, w_ref, mid_ref, out_ref,
                outer, flat, scratch, tile_rows):
    right = factor_ref[pl.ds(half_of(place) * 8, 8), 128:, :].reshape(256, 256)
    for b in range(4):
        left = factor_ref[:, b * 32 : (b + 1) * 32, :].reshape(512, 256)
        product = (mm(left, right, NT) * (1.0 / 256)).reshape(16, 32, 256)
        for h in range(2):
            start = (h * 4 + b) * 8
            outer[start : start + 8] = product[h * 8 : (h + 1) * 8]
    for group in range(8):
        chans = [outer[:, group * 4 + k, :] for k in range(4)]
        for tile in range(2):
            moved = block_transpose([c[:, tile * 128 : (tile + 1) * 128] for c in chans])
            for k in range(4):
                j = tile * 4 + k
                flat[j * 64 : (j + 1) * 64, group * 128 : (group + 1) * 128] = moved[k].astype(BF)
    update = jnp.dot(flat[...], wo_ref[...], preferred_element_type=F32).astype(BF)
    first = pl.multiple_of(branch_of(place) * 8, 8)
    tile_rows[...] = pair_ref[:, pl.ds(first, 8), :].astype(F32)
    pair = jnp.concatenate([tile_rows[:, j, :] for j in range(8)], axis=0)
    mid = (pair + update.astype(F32)).astype(BF)
    mid_ref[...] = mid
    normed = layer_norm(mid)
    lane = lax.broadcasted_iota(jnp.int32, (64, 128), 1) < 64
    for side in range(2):
        rows = (by_target(normed) if side else normed).astype(BF)
        base = side * 256
        value = mm(w_ref[:, base : base + 128], rows, TT)
        gate = mm(w_ref[:, base + 128 : base + 256], rows, TT)
        both = sigmoid(gate) * value
        for pair in range(4):
            low = both[:64, pair * 128 : (pair + 1) * 128]
            high = both[64:, pair * 128 : (pair + 1) * 128]
            scratch[side, :, 2 * pair, :] = jnp.where(lane, low, pltpu.roll(high, 64, 1))
            scratch[side, :, 2 * pair + 1, :] = jnp.where(lane, pltpu.roll(low, 64, 1), high)
    out_ref[:, 0] = scratch[0].astype(BF)
    out_ref[:, 1] = scratch[1].astype(BF)


def triangle_kernel(place, left_ref, back_ref, *refs):
    rights, out_ref = refs[:8], refs[8]
    left = left_ref[...]
    lane = lax.broadcasted_iota(jnp.int32, (64, 128), 1) < 64
    for m in range(8):
        product = mm(rights[m][...], left, TN)
        block = jnp.where(lane, product[:64], product[64:]).astype(BF)
        target = source_of(col_of(place), m) * 2
        for b in range(4):
            for h in range(2):
                out_ref[b * 16 + target + h, 0] = block[(b * 2 + h) * 8 : (b * 2 + h + 1) * 8]
    out_ref[:, 1] = back_ref[...]


def output_kernel(place, sum_ref, mid_ref, wg_ref, w_ref, out_ref, scratch):
    del place
    sums = sum_ref[:, 0].astype(F32)
    fold = lambda v: (v + pltpu.roll(v, 64, 1)) * (1.0 / 128)
    average = fold(jnp.sum(sums, axis=0))
    centered = sums - average[None]
    variance = fold(jnp.sum(jnp.square(centered), axis=0))
    scratch[...] = centered * lax.rsqrt(variance + EPSILON)[None]
    mid = mid_ref[...].astype(F32)
    gate_t = sigmoid(mm(wg_ref[...], layer_norm(mid).astype(BF), TT))
    weight = jnp.concatenate([w_ref[:64], w_ref[64:]], axis=1)
    lane = lax.broadcasted_iota(jnp.int32, (128, 128), 1) < 64

    def mixed_of(j):
        product = mm(weight, scratch[:, j, :].astype(BF), TN)
        return product[:128, :64] + product[128:, 64:]

    for j in range(4):
        mixed = jnp.concatenate([mixed_of(j), mixed_of(j + 4)], axis=1)
        ends = (slice(j * 64, (j + 1) * 64), slice((j + 4) * 64, (j + 5) * 64))
        residual = jnp.concatenate([mid[e] for e in ends], axis=0).T
        gate = jnp.concatenate([gate_t[:, e] for e in ends], axis=1)
        part = (residual + gate * mixed).astype(BF)
        for b in range(4):
            out_ref[b, j] = part[b * 32 : (b + 1) * 32]


def unpack_kernel(x_ref, out_ref):
    for b in range(4):
        for j in range(4):
            block = x_ref[b, j]
            out_ref[b * 8 + j] = block[:, :64]
            out_ref[b * 8 + 4 + j] = block[:, 64:]


def shifted(x, step, flip):
    perm = [(c, (c // 2 - step) % 4 * 2 + (c % 2 ^ flip)) for c in range(8)]
    return lax.ppermute(x, "col", perm)


def gather_col(x):
    parts = {(0, 0): x}
    for step in (1, 3, 2):
        parts[step, 0] = shifted(x, step, 0)
    for step in (0, 1, 3, 2):
        parts[step, 1] = shifted(parts[step, 0], 0, 1)
    return [parts[m // 2, m % 2] for m in range(8)]


def local(
    alignment,
    pair_features,
    w_row,
    row_output_weight,
    w_bias,
    w_column,
    column_output_weight,
    outer_input_weight,
    w_outer_out,
    w_triangle_in,
    w_triangle_gate,
    w_triangle_out,
):
    both = ("branch", "row")
    place = lax.axis_index(("branch", "row", "col")).astype(jnp.int32).reshape(1)
    exchange = lambda x, axis: lax.all_to_all(x, axis, 0, 0, tiled=True)

    blocks = [alignment]
    for step in (1, 3, 2):
        blocks.append(shifted(alignment, step, 0))
    blocks.append(shifted(jnp.stack(blocks[:3]), 0, 1))
    blocks.append(shifted(blocks[3], 0, 1))
    bias = in_vmem(
        bias_kernel,
        [(16, 32, 512)],
        [pltpu.VMEM((64, 32, 128), F32), pltpu.VMEM((16, 8, 128), F32)],
        place,
        pair_features,
        w_bias.T,
    )
    bias = exchange(bias, "row").reshape(512, 512)

    columns = in_vmem(
        row_kernel,
        [(64, 8, 128)],
        [
            pltpu.VMEM((4, 512, 256), BF),
            pltpu.VMEM((2048, 256), BF),
            pltpu.VMEM((256, 2048), BF),
            pltpu.VMEM((64, 8, 128), F32),
        ],
        place,
        *blocks,
        w_row,
        bias,
        row_output_weight,
    )
    columns = exchange(columns, both)
    returning, left, right = in_vmem(
        column_kernel,
        [(64, 8, 128), (32, 256), (8, 32, 256)],
        [pltpu.VMEM((64, 8, 128), F32)],
        place,
        columns,
        w_column,
        column_output_weight,
        outer_input_weight.T,
    )

    right = exchange(right, "col")
    lefts = [left]
    for mask in (1, 2, 3):
        lefts.append(lax.ppermute(left, "branch", [(b, b ^ mask) for b in range(4)]))
    factors = in_vmem(spread_kernel, [(16, 160, 256)], [], place, right, *lefts)
    factors = exchange(factors, "row")

    mid, message = in_vmem(
        pair_kernel,
        [(512, 128), (64, 2, 8, 128)],
        [
            pltpu.VMEM((64, 32, 256), F32),
            pltpu.VMEM((512, 1024), BF),
            pltpu.VMEM((2, 64, 8, 128), F32),
            pltpu.VMEM((64, 8, 128), F32),
        ],
        place,
        factors,
        pair_features,
        w_outer_out,
        w_triangle_in,
    )
    message = exchange(message, both)
    tri_left = message[:, 0].reshape(512, 128)
    rights = gather_col(message[:, 1].reshape(512, 128))
    sums = in_vmem(triangle_kernel, [(64, 2, 8, 128)], [], place, tri_left, returning, *rights)
    sums = exchange(sums, both)
    parts = in_vmem(
        output_kernel,
        [(4, 4, 32, 128)],
        [pltpu.VMEM((64, 8, 128), F32)],
        place,
        sums,
        mid,
        w_triangle_gate,
        w_triangle_out,
    )
    parts = exchange(parts, "branch")
    pair_out = pl.pallas_call(
        unpack_kernel,
        out_shape=jax.ShapeDtypeStruct((32, 32, 64), BF),
        in_specs=[VM],
        name="unpack",
    )(pltpu.with_memory_space_constraint(parts, pltpu.VMEM))
    back = sums[:, 1].reshape(4, 2, 8, 2, 4, 128)
    alignment_out = jnp.transpose(back, (4, 1, 0, 2, 3, 5)).reshape(4, 64, 256)
    return (alignment_out, jnp.transpose(pair_out, (2, 0, 1)))


def solution(mesh):
    in_specs = (P(("branch", "row"), "col", None), P("col", "row", None)) + (P(),) * 10
    out_specs = (P(("branch", "row"), "col", None), P("col", "row", "branch"))
    return jax.shard_map(local, mesh=mesh, in_specs=in_specs, out_specs=out_specs, check_vma=False)
```

```python
import jax
import jax.numpy as jnp
from jax import lax
from jax.experimental import pallas as pl
from jax.experimental.pallas import tpu as pltpu
from jax.sharding import PartitionSpec as P


BF = jnp.bfloat16
F32 = jnp.float32
EPSILON = 1e-05
SCALE = 32**-0.5

NT = (((1,), (1,)), ((), ()))
TN = (((0,), (0,)), ((), ()))
TT = (((0,), (1,)), ((), ()))


def mm(a, b, dims):
    return lax.dot_general(a, b, dims, preferred_element_type=F32)


def layer_norm(inputs):
    inputs = inputs.astype(F32)
    average = jnp.mean(inputs, axis=-1, keepdims=True)
    centered = inputs - average
    variance = jnp.mean(jnp.square(centered), axis=-1, keepdims=True)
    return centered * lax.rsqrt(variance + EPSILON)


def sigmoid(x):
    return 1.0 / (1.0 + jnp.exp(-x))


def exp_rows(scores):
    top = jnp.max(scores, axis=0, keepdims=True)
    weights = jnp.exp(scores - top)
    total = jnp.sum(weights, axis=0, keepdims=True)
    return weights.astype(BF), 1.0 / total


VM = pl.BlockSpec(memory_space=pltpu.VMEM)
SM = pl.BlockSpec(memory_space=pltpu.SMEM)
HB = pl.BlockSpec(memory_space=pltpu.HBM)


def in_vmem(kernel, outs, scratch, place, *args, loose=0):
    loosely = [pltpu.with_memory_space_constraint(a, pltpu.HBM) for a in args[:loose]]
    fixed = [pltpu.with_memory_space_constraint(a, pltpu.VMEM) for a in args[loose:]]
    outs = tuple(pltpu.VMEM(shape, BF) for shape in outs)
    results = pl.pallas_call(
        kernel,
        out_shape=outs,
        in_specs=[SM] + [HB] * loose + [VM] * len(fixed),
        out_specs=(VM,) * len(outs),
        scratch_shapes=scratch,
        compiler_params=pltpu.CompilerParams(vmem_limit_bytes=24 << 20),
    )(place, *loosely, *fixed)
    return results if len(outs) > 1 else results[0]


def col_of(place):
    return place[0] & 7


def half_of(place):
    return (place[0] >> 3) & 1


def branch_of(place):
    return place[0] >> 7


def source_of(col, m):
    return (((col >> 1) + (m >> 1)) & 3) * 2 + ((col & 1) ^ (m & 1))


def bias_kernel(place, pair_ref, w_ref, out_ref, pair, weight, rows, heads, sems):
    del place
    copies = [pltpu.make_async_copy(w_ref, weight, sems.at[4])]
    for q in range(4):
        part = pl.ds(q * 16, 16)
        copies.append(pltpu.make_async_copy(pair_ref.at[part], pair.at[part], sems.at[q]))
    for copy in copies:
        copy.start()
    for q in range(4):
        copies[q + 1].wait()
        block = pair[q * 16 : (q + 1) * 16].reshape(512, 128)
        rows[q * 16 : (q + 1) * 16] = layer_norm(block).astype(BF).astype(F32).reshape(16, 32, 128)
    copies[0].wait()
    for j in range(16):
        pairs = jnp.concatenate([rows[:, j, :], rows[:, j + 16, :]], axis=0).astype(BF)
        heads[j] = mm(weight[...], pairs, NT)
    lane = lax.broadcasted_iota(jnp.int32, (16, 128), 1) < 64
    tiles = []
    for p in range(4):
        a = heads[:, 2 * p, :]
        b = heads[:, 2 * p + 1, :]
        first = jnp.where(lane, a, pltpu.roll(b, 64, 1))
        second = jnp.where(lane, pltpu.roll(a, 64, 1), b)
        tiles.append(jnp.concatenate([first, second], axis=0))
    tile = jnp.concatenate(tiles, axis=1).astype(BF)
    for r in range(16):
        out_ref[r] = tile


EARLY = (0, 1, 2, 3, 6, 7)
LATE = (4, 5)


def project_kernel(place, own_ref, z1_ref, z3_ref, swap_ref, w_ref, key_ref, value_ref):
    del place
    blocks = (own_ref[...], swap_ref[0], z1_ref[...], swap_ref[1], z3_ref[...], swap_ref[2])
    normed = [layer_norm(block.reshape(256, 256)).astype(BF) for block in blocks]
    w_key = w_ref[:, 256:512]
    w_value = w_ref[:, 512:768]
    for s in range(4):
        x = jnp.concatenate([n[s * 64 : (s + 1) * 64] for n in normed], axis=0)
        key_ref[s] = jnp.dot(x, w_key, preferred_element_type=F32).astype(BF)
        value_ref[s] = mm(w_value, x, TT).astype(BF)


def row_kernel(place, z2_ref, last_ref, own_ref, key_ref, value_ref, w_ref, bias_ref, wo_ref,
               out_ref, bias_rows, packed):
    own = layer_norm(own_ref[...].reshape(256, 256)).astype(BF)
    query_t = (mm(w_ref[:, 0:256], own, TT) * SCALE).astype(BF)
    gate_t = sigmoid(mm(w_ref[:, 768:1024], own, TT))
    for k, m in enumerate(EARLY + LATE):
        start = pl.multiple_of(source_of(col_of(place), m) * 64, 64)
        bias_rows[k * 64 : (k + 1) * 64] = bias_ref[pl.ds(start, 64), :].astype(F32)
    late = [layer_norm(r[...].reshape(256, 256)).astype(BF) for r in (z2_ref, last_ref)]
    w_key = w_ref[:, 256:512]
    w_value = w_ref[:, 512:768]
    head_row = lax.broadcasted_iota(jnp.int32, (256, 128), 0) // 32
    head_lane = lax.broadcasted_iota(jnp.int32, (256, 128), 1) // 64
    upper = lax.broadcasted_iota(jnp.int32, (64, 64), 0) < 32
    for s in range(4):
        x = jnp.concatenate([n[s * 64 : (s + 1) * 64] for n in late], axis=0)
        key = jnp.concatenate(
            [key_ref[s], jnp.dot(x, w_key, preferred_element_type=F32).astype(BF)], axis=0
        )
        value_t = jnp.concatenate([value_ref[s], mm(w_value, x, TT).astype(BF)], axis=1)
        mine = query_t[:, s * 64 : (s + 1) * 64]
        twice = jnp.concatenate([mine, mine], axis=1)
        parts = []
        for p in range(4):
            diag = jnp.where(head_row == 2 * p + head_lane, twice, jnp.zeros_like(twice))
            scores = jnp.dot(key, diag, preferred_element_type=F32)
            scores = scores + bias_rows[:, p * 128 : (p + 1) * 128]
            weights, scale = exp_rows(scores)
            mixed = jnp.dot(
                value_t[p * 64 : (p + 1) * 64], weights, preferred_element_type=F32
            )
            mixed = mixed * scale
            parts.append(jnp.where(upper, mixed[:, :64], mixed[:, 64:]))
        attended_t = jnp.concatenate(parts, axis=0)
        gated = (gate_t[:, s * 64 : (s + 1) * 64] * attended_t).astype(BF)
        result = own_ref[s].astype(F32) + mm(gated, wo_ref[...], TN)
        for h in range(2):
            for b in range(4):
                source = (h * 4 + b) * 8
                target = (b * 2 + h) * 8
                for half in range(2):
                    packed[target : target + 8, half * 4 + s, :] = result[
                        source : source + 8, half * 128 : (half + 1) * 128
                    ]
    out_ref[...] = packed[...].astype(BF)


def column_kernel(place, x_ref, w_ref, wo_ref, wf_ref, out_ref, left_ref, right_ref, scratch):
    del place
    scratch[...] = x_ref[...].astype(F32)
    x = jnp.concatenate(
        [
            jnp.concatenate([scratch[:, s, :], scratch[:, 4 + s, :]], axis=1)
            for s in range(4)
        ],
        axis=0,
    )
    normed = layer_norm(x).astype(BF)
    key = jnp.dot(normed, w_ref[:, 256:512], preferred_element_type=F32).astype(BF)
    value_t = mm(w_ref[:, 512:768], normed, TT).astype(BF)
    query_t = (mm(w_ref[:, 0:256], normed, TT) * SCALE).astype(BF)
    gate_t = sigmoid(mm(w_ref[:, 768:1024], normed, TT))
    head_row = lax.broadcasted_iota(jnp.int32, (256, 256), 0) // 32
    parts = []
    for h in range(8):
        diag = jnp.where(head_row == h, query_t, jnp.zeros_like(query_t))
        weights, scale = exp_rows(jnp.dot(key, diag, preferred_element_type=F32))
        mixed = jnp.dot(value_t[h * 32 : (h + 1) * 32], weights, preferred_element_type=F32)
        parts.append(mixed * scale)
    gated = (gate_t * jnp.concatenate(parts, axis=0)).astype(BF)
    result = (x + mm(gated, wo_ref[...], TN)).astype(BF)
    factors = mm(wf_ref[...], layer_norm(result).astype(BF), NT).astype(BF)
    left_ref[...] = factors[:32]
    for c in range(8):
        right_ref[c] = factors[32:]
    wide = result.astype(F32)
    for s in range(4):
        for half in range(2):
            scratch[:, half * 4 + s, :] = wide[
                s * 64 : (s + 1) * 64, half * 128 : (half + 1) * 128
            ]
    out_ref[...] = scratch[...].astype(BF)


def spread_kernel(place, right_ref, *refs):
    lefts, out_ref = refs[:4], refs[4]
    blocks = [left[...] for left in lefts]
    for mask in range(4):
        start = pl.multiple_of((branch_of(place) ^ mask) * 32, 32)
        for r in range(16):
            out_ref[r, pl.ds(start, 32), :] = blocks[mask]
    for r in range(16):
        out_ref[r, 128:] = right_ref[r // 2]


def block_transpose(arrays):
    rows = arrays[0].shape[0]
    lane = lax.broadcasted_iota(jnp.int32, (rows, 128), 1)
    low = lane < 64
    even = (lane // 32) % 2 == 0
    a0, a1, a2, a3 = arrays
    u0 = jnp.where(low, a0, pltpu.roll(a2, 64, 1))
    u2 = jnp.where(low, pltpu.roll(a0, 64, 1), a2)
    u1 = jnp.where(low, a1, pltpu.roll(a3, 64, 1))
    u3 = jnp.where(low, pltpu.roll(a1, 64, 1), a3)
    b0 = jnp.where(even, u0, pltpu.roll(u1, 32, 1))
    b1 = jnp.where(even, pltpu.roll(u0, 96, 1), u1)
    b2 = jnp.where(even, u2, pltpu.roll(u3, 32, 1))
    b3 = jnp.where(even, pltpu.roll(u2, 96, 1), u3)
    return b0, b1, b2, b3


def by_target(rows):
    order = [(h * 4 + b) * 8 for b in range(4) for h in range(2)]
    count = rows.shape[0] // 64
    return jnp.concatenate(
        [rows[j * 64 + s : j * 64 + s + 8] for j in range(count) for s in order], axis=0
    )


def pair_kernel(place, factor_ref, pair_ref, wo_ref, w_ref, mid_ref, out_ref,
                outer, flat, scratch, tile_rows):
    right = factor_ref[pl.ds(half_of(place) * 8, 8), 128:, :].reshape(256, 256)
    for b in range(4):
        left = factor_ref[:, b * 32 : (b + 1) * 32, :].reshape(512, 256)
        product = (mm(left, right, NT) * (1.0 / 256)).reshape(16, 32, 256)
        for h in range(2):
            start = (h * 4 + b) * 8
            outer[start : start + 8] = product[h * 8 : (h + 1) * 8]
    for group in range(8):
        chans = [outer[:, group * 4 + k, :] for k in range(4)]
        for tile in range(2):
            moved = block_transpose([c[:, tile * 128 : (tile + 1) * 128] for c in chans])
            for k in range(4):
                j = tile * 4 + k
                flat[j * 64 : (j + 1) * 64, group * 128 : (group + 1) * 128] = moved[k].astype(BF)
    update = jnp.dot(flat[...], wo_ref[...], preferred_element_type=F32).astype(BF)
    first = pl.multiple_of(branch_of(place) * 8, 8)
    tile_rows[...] = pair_ref[:, pl.ds(first, 8), :].astype(F32)
    pair = jnp.concatenate([tile_rows[:, j, :] for j in range(8)], axis=0)
    mid = (pair + update.astype(F32)).astype(BF)
    mid_ref[...] = mid
    normed = layer_norm(mid)
    lane = lax.broadcasted_iota(jnp.int32, (64, 128), 1) < 64
    for side in range(2):
        rows = (by_target(normed) if side else normed).astype(BF)
        base = side * 256
        value = mm(w_ref[:, base : base + 128], rows, TT)
        gate = mm(w_ref[:, base + 128 : base + 256], rows, TT)
        both = sigmoid(gate) * value
        for pair in range(4):
            low = both[:64, pair * 128 : (pair + 1) * 128]
            high = both[64:, pair * 128 : (pair + 1) * 128]
            scratch[side, :, 2 * pair, :] = jnp.where(lane, low, pltpu.roll(high, 64, 1))
            scratch[side, :, 2 * pair + 1, :] = jnp.where(lane, pltpu.roll(low, 64, 1), high)
    out_ref[:, 0] = scratch[0].astype(BF)
    out_ref[:, 1] = scratch[1].astype(BF)


def triangle_kernel(place, left_ref, back_ref, same_ref, other_ref, out_ref):
    left = left_ref[...]
    lane = lax.broadcasted_iota(jnp.int32, (64, 128), 1) < 64
    core = col_of(place) & 1
    for chip in range(4):
        for right_ref, source in ((same_ref, core), (other_ref, core ^ 1)):
            product = mm(right_ref[chip], left, TN)
            block = jnp.where(lane, product[:64], product[64:]).astype(BF)
            target = (chip * 2 + source) * 2
            for b in range(4):
                for h in range(2):
                    out_ref[b * 16 + target + h, 0] = block[(b * 2 + h) * 8 : (b * 2 + h + 1) * 8]
    out_ref[:, 1] = back_ref[...]


def output_kernel(place, sum_ref, mid_ref, wg_ref, w_ref, out_ref, scratch):
    del place
    sums = sum_ref[:, 0].astype(F32)
    fold = lambda v: (v + pltpu.roll(v, 64, 1)) * (1.0 / 128)
    average = fold(jnp.sum(sums, axis=0))
    centered = sums - average[None]
    variance = fold(jnp.sum(jnp.square(centered), axis=0))
    scratch[...] = centered * lax.rsqrt(variance + EPSILON)[None]
    mid = mid_ref[...].astype(F32)
    gate_t = sigmoid(mm(wg_ref[...], layer_norm(mid).astype(BF), TT))
    weight = jnp.concatenate([w_ref[:64], w_ref[64:]], axis=1)
    lane = lax.broadcasted_iota(jnp.int32, (128, 128), 1) < 64

    def mixed_of(j):
        product = mm(weight, scratch[:, j, :].astype(BF), TN)
        return product[:128, :64] + product[128:, 64:]

    for j in range(4):
        mixed = jnp.concatenate([mixed_of(j), mixed_of(j + 4)], axis=1)
        ends = (slice(j * 64, (j + 1) * 64), slice((j + 4) * 64, (j + 5) * 64))
        residual = jnp.concatenate([mid[e] for e in ends], axis=0).T
        gate = jnp.concatenate([gate_t[:, e] for e in ends], axis=1)
        part = (residual + gate * mixed).astype(BF)
        for b in range(4):
            out_ref[b, j] = part[b * 32 : (b + 1) * 32]


def unpack_kernel(x_ref, out_ref):
    for b in range(4):
        for j in range(4):
            block = x_ref[b, j]
            out_ref[b * 8 + j] = block[:, :64]
            out_ref[b * 8 + 4 + j] = block[:, 64:]


def shifted(x, step, flip):
    perm = [(c, (c // 2 - step) % 4 * 2 + (c % 2 ^ flip)) for c in range(8)]
    return lax.ppermute(x, "col", perm)


def local(
    alignment,
    pair_features,
    w_row,
    row_output_weight,
    w_bias,
    w_column,
    column_output_weight,
    outer_input_weight,
    w_outer_out,
    w_triangle_in,
    w_triangle_gate,
    w_triangle_out,
):
    both = ("branch", "row")
    place = lax.axis_index(("branch", "row", "col")).astype(jnp.int32).reshape(1)
    exchange = lambda x, axis: lax.all_to_all(x, axis, 0, 0, tiled=True)

    blocks = [alignment]
    for step in (1, 3, 2):
        blocks.append(shifted(alignment, step, 0))
    swapped = shifted(jnp.stack(blocks[:3]), 0, 1)
    last = shifted(blocks[3], 0, 1)
    bias = in_vmem(
        bias_kernel,
        [(16, 32, 512)],
        [
            pltpu.VMEM((64, 32, 128), BF),
            pltpu.VMEM((8, 128), BF),
            pltpu.VMEM((64, 32, 128), F32),
            pltpu.VMEM((16, 8, 128), F32),
            pltpu.SemaphoreType.DMA((5,)),
        ],
        place,
        pair_features,
        w_bias.T,
        loose=2,
    )
    bias = exchange(bias, "row").reshape(512, 512)

    projected = in_vmem(
        project_kernel, [(4, 384, 256), (4, 256, 384)], [], place, *blocks[:3], swapped, w_row
    )
    columns = in_vmem(
        row_kernel,
        [(64, 8, 128)],
        [pltpu.VMEM((512, 512), F32), pltpu.VMEM((64, 8, 128), F32)],
        place,
        blocks[3],
        last,
        alignment,
        *projected,
        w_row,
        bias,
        row_output_weight,
    )
    columns = exchange(columns, both)
    returning, left, right = in_vmem(
        column_kernel,
        [(64, 8, 128), (32, 256), (8, 32, 256)],
        [pltpu.VMEM((64, 8, 128), F32)],
        place,
        columns,
        w_column,
        column_output_weight,
        outer_input_weight.T,
    )

    right = exchange(right, "col")
    lefts = [left]
    for mask in (1, 2, 3):
        lefts.append(lax.ppermute(left, "branch", [(b, b ^ mask) for b in range(4)]))
    factors = in_vmem(spread_kernel, [(16, 160, 256)], [], place, right, *lefts)
    factors = exchange(factors, "row")

    mid, message = in_vmem(
        pair_kernel,
        [(512, 128), (64, 2, 8, 128)],
        [
            pltpu.VMEM((64, 32, 256), F32),
            pltpu.VMEM((512, 1024), BF),
            pltpu.VMEM((2, 64, 8, 128), F32),
            pltpu.VMEM((64, 8, 128), F32),
        ],
        place,
        factors,
        pair_features,
        w_outer_out,
        w_triangle_in,
    )
    message = exchange(message, both)
    tri_left = message[:, 0].reshape(512, 128)
    same = lax.all_to_all(
        jnp.broadcast_to(message[None, :, 1], (4, 64, 8, 128)).reshape(4, 512, 128),
        "col", 0, 0, tiled=True, axis_index_groups=[[0, 2, 4, 6], [1, 3, 5, 7]],
    )
    sums = in_vmem(
        triangle_kernel,
        [(64, 2, 8, 128)],
        [],
        place,
        tri_left,
        returning,
        same,
        shifted(same, 0, 1),
    )
    sums = exchange(sums, both)
    parts = in_vmem(
        output_kernel,
        [(4, 4, 32, 128)],
        [pltpu.VMEM((64, 8, 128), F32)],
        place,
        sums,
        mid,
        w_triangle_gate,
        w_triangle_out,
    )
    parts = exchange(parts, "branch")
    pair_out = pl.pallas_call(
        unpack_kernel,
        out_shape=jax.ShapeDtypeStruct((32, 32, 64), BF),
        in_specs=[VM],
        name="unpack",
    )(pltpu.with_memory_space_constraint(parts, pltpu.VMEM))
    back = sums[:, 1].reshape(4, 2, 8, 2, 4, 128)
    alignment_out = jnp.transpose(back, (4, 1, 0, 2, 3, 5)).reshape(4, 64, 256)
    return (alignment_out, jnp.transpose(pair_out, (2, 0, 1)))


def solution(mesh):
    in_specs = (P(("branch", "row"), "col", None), P("col", "row", None)) + (P(),) * 10
    out_specs = (P(("branch", "row"), "col", None), P("col", "row", "branch"))
    return jax.shard_map(local, mesh=mesh, in_specs=in_specs, out_specs=out_specs, check_vma=False)
```

```python
import jax
import jax.numpy as jnp
from jax import lax
from jax.experimental import pallas as pl
from jax.experimental.pallas import tpu as pltpu
from jax.sharding import PartitionSpec as P


BF = jnp.bfloat16
F32 = jnp.float32
EPSILON = 1e-05
SCALE = 32**-0.5

NT = (((1,), (1,)), ((), ()))
TN = (((0,), (0,)), ((), ()))
TT = (((0,), (1,)), ((), ()))


def mm(a, b, dims):
    return lax.dot_general(a, b, dims, preferred_element_type=F32)


def layer_norm(inputs):
    inputs = inputs.astype(F32)
    average = jnp.mean(inputs, axis=-1, keepdims=True)
    centered = inputs - average
    variance = jnp.mean(jnp.square(centered), axis=-1, keepdims=True)
    return centered * lax.rsqrt(variance + EPSILON)


def sigmoid(x):
    return 1.0 / (1.0 + jnp.exp(-x))


def exp_rows(scores):
    top = jnp.max(scores, axis=0, keepdims=True)
    weights = jnp.exp(scores - top)
    total = jnp.sum(weights, axis=0, keepdims=True)
    return weights.astype(BF), 1.0 / total


VM = pl.BlockSpec(memory_space=pltpu.VMEM)
SM = pl.BlockSpec(memory_space=pltpu.SMEM)
HB = pl.BlockSpec(memory_space=pltpu.HBM)


def in_vmem(kernel, outs, scratch, place, *args, loose=0):
    loosely = [pltpu.with_memory_space_constraint(a, pltpu.HBM) for a in args[:loose]]
    fixed = [pltpu.with_memory_space_constraint(a, pltpu.VMEM) for a in args[loose:]]
    outs = tuple(pltpu.VMEM(shape, BF) for shape in outs)
    results = pl.pallas_call(
        kernel,
        out_shape=outs,
        in_specs=[SM] + [HB] * loose + [VM] * len(fixed),
        out_specs=(VM,) * len(outs),
        scratch_shapes=scratch,
        compiler_params=pltpu.CompilerParams(vmem_limit_bytes=24 << 20),
    )(place, *loosely, *fixed)
    return results if len(outs) > 1 else results[0]


def col_of(place):
    return place[0] & 7


def half_of(place):
    return (place[0] >> 3) & 1


def branch_of(place):
    return place[0] >> 7


def source_of(col, m):
    return (((col >> 1) + (m >> 1)) & 3) * 2 + ((col & 1) ^ (m & 1))


def bias_kernel(place, pair_ref, w_ref, out_ref, pair, weight, rows, heads, sems):
    del place
    copies = [pltpu.make_async_copy(w_ref, weight, sems.at[4])]
    for q in range(4):
        part = pl.ds(q * 16, 16)
        copies.append(pltpu.make_async_copy(pair_ref.at[part], pair.at[part], sems.at[q]))
    for copy in copies:
        copy.start()
    for q in range(4):
        copies[q + 1].wait()
        block = pair[q * 16 : (q + 1) * 16].reshape(512, 128)
        rows[q * 16 : (q + 1) * 16] = layer_norm(block).astype(BF).astype(F32).reshape(16, 32, 128)
    copies[0].wait()
    for j in range(16):
        pairs = jnp.concatenate([rows[:, j, :], rows[:, j + 16, :]], axis=0).astype(BF)
        heads[j] = mm(weight[...], pairs, NT)
    lane = lax.broadcasted_iota(jnp.int32, (16, 128), 1) < 64
    tiles = []
    for p in range(4):
        a = heads[:, 2 * p, :]
        b = heads[:, 2 * p + 1, :]
        first = jnp.where(lane, a, pltpu.roll(b, 64, 1))
        second = jnp.where(lane, pltpu.roll(a, 64, 1), b)
        tiles.append(jnp.concatenate([first, second], axis=0))
    tile = jnp.concatenate(tiles, axis=1).astype(BF)
    for r in range(16):
        out_ref[r] = tile


def row_kernel(place, *refs):
    own_ref, z1_ref, z3_ref, z2_ref, swap_ref, last_ref = refs[:6]
    w_ref, bias_ref, wo_ref, out_ref, rows, keys, values, packed = refs[6:]
    for m, block in (
        (0, own_ref[...]),
        (2, z1_ref[...]),
        (6, z3_ref[...]),
        (1, swap_ref[0]),
        (3, swap_ref[1]),
        (7, swap_ref[2]),
        (4, z2_ref[...]),
        (5, last_ref[...]),
    ):
        start = pl.multiple_of(source_of(col_of(place), m) * 64, 64)
        normed = layer_norm(block.reshape(256, 256)).astype(BF)
        if m == 0:
            own = normed
        for s in range(4):
            rows[s, pl.ds(start, 64), :] = normed[s * 64 : (s + 1) * 64]
    x = rows[...].reshape(2048, 256)
    keys[...] = jnp.dot(x, w_ref[:, 256:512], preferred_element_type=F32).astype(BF)
    values[...] = mm(w_ref[:, 512:768], x, TT).astype(BF)
    query_t = (mm(w_ref[:, 0:256], own, TT) * SCALE).astype(BF)
    gate_t = sigmoid(mm(w_ref[:, 768:1024], own, TT))
    head_row = lax.broadcasted_iota(jnp.int32, (256, 512), 0) // 32
    head_lane = lax.broadcasted_iota(jnp.int32, (256, 512), 1) // 64
    upper = lax.broadcasted_iota(jnp.int32, (64, 64), 0) < 32

    def scores_of(s):
        wide = jnp.concatenate([query_t[:, s * 64 : (s + 1) * 64]] * 8, axis=1)
        diag = jnp.where(head_row == head_lane, wide, jnp.zeros_like(wide))
        scores = jnp.dot(keys[s * 512 : (s + 1) * 512], diag, preferred_element_type=F32)
        return scores + bias_ref[...].astype(F32)

    ahead = scores_of(0)
    for s in range(4):
        scores = ahead
        if s < 3:
            ahead = scores_of(s + 1)
        weights, scale = exp_rows(scores)
        parts = []
        for p in range(4):
            lanes = slice(p * 128, (p + 1) * 128)
            mixed = jnp.dot(
                values[p * 64 : (p + 1) * 64, s * 512 : (s + 1) * 512],
                weights[:, lanes],
                preferred_element_type=F32,
            )
            mixed = mixed * scale[:, lanes]
            parts.append(jnp.where(upper, mixed[:, :64], mixed[:, 64:]))
        attended_t = jnp.concatenate(parts, axis=0)
        gated = (gate_t[:, s * 64 : (s + 1) * 64] * attended_t).astype(BF)
        result = own_ref[s].astype(F32) + mm(gated, wo_ref[...], TN)
        for h in range(2):
            for b in range(4):
                source = (h * 4 + b) * 8
                target = (b * 2 + h) * 8
                for half in range(2):
                    packed[target : target + 8, half * 4 + s, :] = result[
                        source : source + 8, half * 128 : (half + 1) * 128
                    ]
    out_ref[...] = packed[...].astype(BF)


def column_kernel(place, x_ref, w_ref, wo_ref, wf_ref, out_ref, left_ref, right_ref, scratch):
    del place
    scratch[...] = x_ref[...].astype(F32)
    x = jnp.concatenate(
        [
            jnp.concatenate([scratch[:, s, :], scratch[:, 4 + s, :]], axis=1)
            for s in range(4)
        ],
        axis=0,
    )
    normed = layer_norm(x).astype(BF)
    key = jnp.dot(normed, w_ref[:, 256:512], preferred_element_type=F32).astype(BF)
    value_t = mm(w_ref[:, 512:768], normed, TT).astype(BF)
    query_t = (mm(w_ref[:, 0:256], normed, TT) * SCALE).astype(BF)
    gate_t = sigmoid(mm(w_ref[:, 768:1024], normed, TT))
    head_row = lax.broadcasted_iota(jnp.int32, (256, 1024), 0) // 32
    head_lane = lax.broadcasted_iota(jnp.int32, (256, 1024), 1) // 256
    wide = jnp.concatenate([query_t] * 4, axis=1)

    def scores_of(group):
        diag = jnp.where(head_row == head_lane + group * 4, wide, jnp.zeros_like(wide))
        return jnp.dot(key, diag, preferred_element_type=F32)

    parts = []
    ahead = scores_of(0)
    for group in range(2):
        scores = ahead
        if group == 0:
            ahead = scores_of(1)
        weights, scale = exp_rows(scores)
        for k in range(4):
            h = group * 4 + k
            lanes = slice(k * 256, (k + 1) * 256)
            mixed = jnp.dot(
                value_t[h * 32 : (h + 1) * 32], weights[:, lanes], preferred_element_type=F32
            )
            parts.append(mixed * scale[:, lanes])
    gated = (gate_t * jnp.concatenate(parts, axis=0)).astype(BF)
    result = (x + mm(gated, wo_ref[...], TN)).astype(BF)
    factors = mm(wf_ref[...], layer_norm(result).astype(BF), NT).astype(BF)
    left_ref[...] = factors[:32]
    for c in range(8):
        right_ref[c] = factors[32:]
    wide = result.astype(F32)
    for s in range(4):
        for half in range(2):
            scratch[:, half * 4 + s, :] = wide[
                s * 64 : (s + 1) * 64, half * 128 : (half + 1) * 128
            ]
    out_ref[...] = scratch[...].astype(BF)


def spread_kernel(place, right_ref, *refs):
    lefts, out_ref = refs[:4], refs[4]
    blocks = [left[...] for left in lefts]
    for mask in range(4):
        start = pl.multiple_of((branch_of(place) ^ mask) * 32, 32)
        for r in range(16):
            out_ref[r, pl.ds(start, 32), :] = blocks[mask]
    for r in range(16):
        out_ref[r, 128:] = right_ref[r // 2]


def block_transpose(arrays):
    rows = arrays[0].shape[0]
    lane = lax.broadcasted_iota(jnp.int32, (rows, 128), 1)
    low = lane < 64
    even = (lane // 32) % 2 == 0
    a0, a1, a2, a3 = arrays
    u0 = jnp.where(low, a0, pltpu.roll(a2, 64, 1))
    u2 = jnp.where(low, pltpu.roll(a0, 64, 1), a2)
    u1 = jnp.where(low, a1, pltpu.roll(a3, 64, 1))
    u3 = jnp.where(low, pltpu.roll(a1, 64, 1), a3)
    b0 = jnp.where(even, u0, pltpu.roll(u1, 32, 1))
    b1 = jnp.where(even, pltpu.roll(u0, 96, 1), u1)
    b2 = jnp.where(even, u2, pltpu.roll(u3, 32, 1))
    b3 = jnp.where(even, pltpu.roll(u2, 96, 1), u3)
    return b0, b1, b2, b3


def by_target(rows):
    order = [(h * 4 + b) * 8 for b in range(4) for h in range(2)]
    count = rows.shape[0] // 64
    return jnp.concatenate(
        [rows[j * 64 + s : j * 64 + s + 8] for j in range(count) for s in order], axis=0
    )


def pair_kernel(place, factor_ref, pair_ref, wo_ref, w_ref, mid_ref, out_ref,
                outer, flat, scratch, tile_rows):
    right = factor_ref[pl.ds(half_of(place) * 8, 8), 128:, :].reshape(256, 256)
    for b in range(4):
        left = factor_ref[:, b * 32 : (b + 1) * 32, :].reshape(512, 256)
        product = (mm(left, right, NT) * (1.0 / 256)).reshape(16, 32, 256)
        for h in range(2):
            start = (h * 4 + b) * 8
            outer[start : start + 8] = product[h * 8 : (h + 1) * 8]
    for group in range(8):
        chans = [outer[:, group * 4 + k, :] for k in range(4)]
        for tile in range(2):
            moved = block_transpose([c[:, tile * 128 : (tile + 1) * 128] for c in chans])
            for k in range(4):
                j = tile * 4 + k
                flat[j * 64 : (j + 1) * 64, group * 128 : (group + 1) * 128] = moved[k].astype(BF)
    update = jnp.dot(flat[...], wo_ref[...], preferred_element_type=F32).astype(BF)
    first = pl.multiple_of(branch_of(place) * 8, 8)
    tile_rows[...] = pair_ref[:, pl.ds(first, 8), :].astype(F32)
    pair = jnp.concatenate([tile_rows[:, j, :] for j in range(8)], axis=0)
    mid = (pair + update.astype(F32)).astype(BF)
    mid_ref[...] = mid
    normed = layer_norm(mid)
    lane = lax.broadcasted_iota(jnp.int32, (64, 128), 1) < 64
    for side in range(2):
        rows = (by_target(normed) if side else normed).astype(BF)
        base = side * 256
        value = mm(w_ref[:, base : base + 128], rows, TT)
        gate = mm(w_ref[:, base + 128 : base + 256], rows, TT)
        both = sigmoid(gate) * value
        for pair in range(4):
            low = both[:64, pair * 128 : (pair + 1) * 128]
            high = both[64:, pair * 128 : (pair + 1) * 128]
            scratch[side, :, 2 * pair, :] = jnp.where(lane, low, pltpu.roll(high, 64, 1))
            scratch[side, :, 2 * pair + 1, :] = jnp.where(lane, pltpu.roll(low, 64, 1), high)
    out_ref[:, 0] = scratch[0].astype(BF)
    out_ref[:, 1] = scratch[1].astype(BF)


def triangle_kernel(place, left_ref, back_ref, *refs):
    same, other, out_ref = refs[:4], refs[4:6], refs[6]
    left = left_ref[...]
    lane = lax.broadcasted_iota(jnp.int32, (64, 128), 1) < 64
    for m in range(8):
        step = m // 2
        right = other[step % 2][step // 2] if m % 2 else same[step][...]
        product = mm(right, left, TN)
        block = jnp.where(lane, product[:64], product[64:]).astype(BF)
        target = source_of(col_of(place), m) * 2
        for b in range(4):
            for h in range(2):
                out_ref[b * 16 + target + h, 0] = block[(b * 2 + h) * 8 : (b * 2 + h + 1) * 8]
    out_ref[:, 1] = back_ref[...]


def output_kernel(place, sum_ref, mid_ref, wg_ref, w_ref, out_ref, scratch):
    del place
    sums = sum_ref[:, 0].astype(F32)
    fold = lambda v: (v + pltpu.roll(v, 64, 1)) * (1.0 / 128)
    average = fold(jnp.sum(sums, axis=0))
    centered = sums - average[None]
    variance = fold(jnp.sum(jnp.square(centered), axis=0))
    scratch[...] = centered * lax.rsqrt(variance + EPSILON)[None]
    mid = mid_ref[...].astype(F32)
    gate_t = sigmoid(mm(wg_ref[...], layer_norm(mid).astype(BF), TT))
    weight = jnp.concatenate([w_ref[:64], w_ref[64:]], axis=1)
    lane = lax.broadcasted_iota(jnp.int32, (128, 128), 1) < 64

    def mixed_of(j):
        product = mm(weight, scratch[:, j, :].astype(BF), TN)
        return product[:128, :64] + product[128:, 64:]

    for j in range(4):
        mixed = jnp.concatenate([mixed_of(j), mixed_of(j + 4)], axis=1)
        ends = (slice(j * 64, (j + 1) * 64), slice((j + 4) * 64, (j + 5) * 64))
        residual = jnp.concatenate([mid[e] for e in ends], axis=0).T
        gate = jnp.concatenate([gate_t[:, e] for e in ends], axis=1)
        part = (residual + gate * mixed).astype(BF)
        for b in range(4):
            out_ref[b, j] = part[b * 32 : (b + 1) * 32]


def unpack_kernel(x_ref, out_ref):
    for b in range(4):
        for j in range(4):
            block = x_ref[b, j]
            out_ref[b * 8 + j] = block[:, :64]
            out_ref[b * 8 + 4 + j] = block[:, 64:]


def shifted(x, step, flip):
    perm = [(c, (c // 2 - step) % 4 * 2 + (c % 2 ^ flip)) for c in range(8)]
    return lax.ppermute(x, "col", perm)


def gather_col(x):
    same, other = {0: x}, {}
    for step in (2, 1, 3):
        same[step] = shifted(x, step, 0)
    for pair in ((0, 2), (1, 3)):
        other[pair[0]] = shifted(jnp.stack([same[k] for k in pair]), 0, 1)
    return [same[k] for k in range(4)], [other[0], other[1]]


def local(
    alignment,
    pair_features,
    w_row,
    row_output_weight,
    w_bias,
    w_column,
    column_output_weight,
    outer_input_weight,
    w_outer_out,
    w_triangle_in,
    w_triangle_gate,
    w_triangle_out,
):
    both = ("branch", "row")
    place = lax.axis_index(("branch", "row", "col")).astype(jnp.int32).reshape(1)
    exchange = lambda x, axis: lax.all_to_all(x, axis, 0, 0, tiled=True)

    blocks = [alignment]
    for step in (1, 3, 2):
        blocks.append(shifted(alignment, step, 0))
    blocks.append(shifted(jnp.stack(blocks[:3]), 0, 1))
    blocks.append(shifted(blocks[3], 0, 1))
    bias = in_vmem(
        bias_kernel,
        [(16, 32, 512)],
        [
            pltpu.VMEM((64, 32, 128), BF),
            pltpu.VMEM((8, 128), BF),
            pltpu.VMEM((64, 32, 128), F32),
            pltpu.VMEM((16, 8, 128), F32),
            pltpu.SemaphoreType.DMA((5,)),
        ],
        place,
        pair_features,
        w_bias.T,
        loose=2,
    )
    bias = exchange(bias, "row").reshape(512, 512)

    columns = in_vmem(
        row_kernel,
        [(64, 8, 128)],
        [
            pltpu.VMEM((4, 512, 256), BF),
            pltpu.VMEM((2048, 256), BF),
            pltpu.VMEM((256, 2048), BF),
            pltpu.VMEM((64, 8, 128), F32),
        ],
        place,
        *blocks,
        w_row,
        bias,
        row_output_weight,
    )
    columns = exchange(columns, both)
    returning, left, right = in_vmem(
        column_kernel,
        [(64, 8, 128), (32, 256), (8, 32, 256)],
        [pltpu.VMEM((64, 8, 128), F32)],
        place,
        columns,
        w_column,
        column_output_weight,
        outer_input_weight.T,
    )

    right = exchange(right, "col")
    lefts = [left]
    for mask in (1, 2, 3):
        lefts.append(lax.ppermute(left, "branch", [(b, b ^ mask) for b in range(4)]))
    factors = in_vmem(spread_kernel, [(16, 160, 256)], [], place, right, *lefts)
    factors = exchange(factors, "row")

    mid, message = in_vmem(
        pair_kernel,
        [(512, 128), (64, 2, 8, 128)],
        [
            pltpu.VMEM((64, 32, 256), F32),
            pltpu.VMEM((512, 1024), BF),
            pltpu.VMEM((2, 64, 8, 128), F32),
            pltpu.VMEM((64, 8, 128), F32),
        ],
        place,
        factors,
        pair_features,
        w_outer_out,
        w_triangle_in,
    )
    message = exchange(message, both)
    tri_left = message[:, 0].reshape(512, 128)
    same, other = gather_col(message[:, 1].reshape(512, 128))
    sums = in_vmem(
        triangle_kernel, [(64, 2, 8, 128)], [], place, tri_left, returning, *same, *other
    )
    sums = exchange(sums, both)
    parts = in_vmem(
        output_kernel,
        [(4, 4, 32, 128)],
        [pltpu.VMEM((64, 8, 128), F32)],
        place,
        sums,
        mid,
        w_triangle_gate,
        w_triangle_out,
    )
    parts = exchange(parts, "branch")
    pair_out = pl.pallas_call(
        unpack_kernel,
        out_shape=jax.ShapeDtypeStruct((32, 32, 64), BF),
        in_specs=[VM],
        name="unpack",
    )(pltpu.with_memory_space_constraint(parts, pltpu.VMEM))
    back = sums[:, 1].reshape(4, 2, 8, 2, 4, 128)
    alignment_out = jnp.transpose(back, (4, 1, 0, 2, 3, 5)).reshape(4, 64, 256)
    return (alignment_out, jnp.transpose(pair_out, (2, 0, 1)))


def solution(mesh):
    in_specs = (P(("branch", "row"), "col", None), P("col", "row", None)) + (P(),) * 10
    out_specs = (P(("branch", "row"), "col", None), P("col", "row", "branch"))
    return jax.shard_map(local, mesh=mesh, in_specs=in_specs, out_specs=out_specs, check_vma=False)
```

```python
import jax
import jax.numpy as jnp
from jax import lax
from jax.experimental import pallas as pl
from jax.experimental.pallas import tpu as pltpu
from jax.sharding import PartitionSpec as P


BF = jnp.bfloat16
F32 = jnp.float32
EPSILON = 1e-05
SCALE = 32**-0.5

NT = (((1,), (1,)), ((), ()))
TN = (((0,), (0,)), ((), ()))
TT = (((0,), (1,)), ((), ()))


def mm(a, b, dims):
    return lax.dot_general(a, b, dims, preferred_element_type=F32)


def layer_norm(inputs):
    inputs = inputs.astype(F32)
    average = jnp.mean(inputs, axis=-1, keepdims=True)
    centered = inputs - average
    variance = jnp.mean(jnp.square(centered), axis=-1, keepdims=True)
    return centered * lax.rsqrt(variance + EPSILON)


def sigmoid(x):
    return 1.0 / (1.0 + jnp.exp(-x))


def exp_rows(scores):
    top = jnp.max(scores, axis=0, keepdims=True)
    weights = jnp.exp(scores - top)
    total = jnp.sum(weights, axis=0, keepdims=True)
    return weights.astype(BF), 1.0 / total


VM = pl.BlockSpec(memory_space=pltpu.VMEM)
SM = pl.BlockSpec(memory_space=pltpu.SMEM)
HB = pl.BlockSpec(memory_space=pltpu.HBM)


def in_vmem(kernel, outs, scratch, place, *args, loose=0, results=0):
    loosely = [pltpu.with_memory_space_constraint(a, pltpu.HBM) for a in args[:loose]]
    fixed = [pltpu.with_memory_space_constraint(a, pltpu.VMEM) for a in args[loose:]]
    inner = len(outs) - results
    shapes = [pltpu.VMEM(shape, BF) for shape in outs[:inner]]
    shapes += [jax.ShapeDtypeStruct(shape, BF) for shape in outs[inner:]]
    outputs = pl.pallas_call(
        kernel,
        out_shape=tuple(shapes),
        in_specs=[SM] + [HB] * loose + [VM] * len(fixed),
        out_specs=(VM,) * inner + (pl.BlockSpec(),) * results,
        scratch_shapes=scratch,
        compiler_params=pltpu.CompilerParams(vmem_limit_bytes=24 << 20),
    )(place, *loosely, *fixed)
    return outputs if len(outs) > 1 else outputs[0]


def col_of(place):
    return place[0] & 7


def half_of(place):
    return (place[0] >> 3) & 1


def branch_of(place):
    return place[0] >> 7


def source_of(col, m):
    return (((col >> 1) + (m >> 1)) & 3) * 2 + ((col & 1) ^ (m & 1))


def bias_kernel(place, pair_ref, w_ref, out_ref, pair, weight, rows, heads, sems):
    del place
    copies = [pltpu.make_async_copy(w_ref, weight, sems.at[4])]
    for q in range(4):
        part = pl.ds(q * 16, 16)
        copies.append(pltpu.make_async_copy(pair_ref.at[part], pair.at[part], sems.at[q]))
    for copy in copies:
        copy.start()
    for q in range(4):
        copies[q + 1].wait()
        block = pair[q * 16 : (q + 1) * 16].reshape(512, 128)
        rows[q * 16 : (q + 1) * 16] = layer_norm(block).astype(BF).astype(F32).reshape(16, 32, 128)
    copies[0].wait()
    for j in range(16):
        pairs = jnp.concatenate([rows[:, j, :], rows[:, j + 16, :]], axis=0).astype(BF)
        heads[j] = mm(weight[...], pairs, NT)
    lane = lax.broadcasted_iota(jnp.int32, (16, 128), 1) < 64
    tiles = []
    for p in range(4):
        a = heads[:, 2 * p, :]
        b = heads[:, 2 * p + 1, :]
        first = jnp.where(lane, a, pltpu.roll(b, 64, 1))
        second = jnp.where(lane, pltpu.roll(a, 64, 1), b)
        tiles.append(jnp.concatenate([first, second], axis=0))
    tile = jnp.concatenate(tiles, axis=1).astype(BF)
    for r in range(16):
        out_ref[r] = tile


def row_kernel(place, *refs):
    own_ref, z1_ref, z3_ref, z2_ref, swap_ref, last_ref = refs[:6]
    w_ref, bias_ref, wo_ref, out_ref, rows, keys, values, packed = refs[6:]
    for m, block in (
        (0, own_ref[...]),
        (2, z1_ref[...]),
        (6, z3_ref[...]),
        (1, swap_ref[0]),
        (3, swap_ref[1]),
        (7, swap_ref[2]),
        (4, z2_ref[...]),
        (5, last_ref[...]),
    ):
        start = pl.multiple_of(source_of(col_of(place), m) * 64, 64)
        normed = layer_norm(block.reshape(256, 256)).astype(BF)
        if m == 0:
            own = normed
        for s in range(4):
            rows[s, pl.ds(start, 64), :] = normed[s * 64 : (s + 1) * 64]
    x = rows[...].reshape(2048, 256)
    keys[...] = jnp.dot(x, w_ref[:, 256:512], preferred_element_type=F32).astype(BF)
    values[...] = mm(w_ref[:, 512:768], x, TT).astype(BF)
    query_t = (mm(w_ref[:, 0:256], own, TT) * SCALE).astype(BF)
    gate_t = sigmoid(mm(w_ref[:, 768:1024], own, TT))
    head_row = lax.broadcasted_iota(jnp.int32, (256, 512), 0) // 32
    head_lane = lax.broadcasted_iota(jnp.int32, (256, 512), 1) // 64
    upper = lax.broadcasted_iota(jnp.int32, (64, 64), 0) < 32

    def scores_of(s):
        wide = jnp.concatenate([query_t[:, s * 64 : (s + 1) * 64]] * 8, axis=1)
        diag = jnp.where(head_row == head_lane, wide, jnp.zeros_like(wide))
        scores = jnp.dot(keys[s * 512 : (s + 1) * 512], diag, preferred_element_type=F32)
        return scores + bias_ref[...].astype(F32)

    ahead = scores_of(0)
    for s in range(4):
        scores = ahead
        if s < 3:
            ahead = scores_of(s + 1)
        weights, scale = exp_rows(scores)
        parts = []
        for p in range(4):
            lanes = slice(p * 128, (p + 1) * 128)
            mixed = jnp.dot(
                values[p * 64 : (p + 1) * 64, s * 512 : (s + 1) * 512],
                weights[:, lanes],
                preferred_element_type=F32,
            )
            mixed = mixed * scale[:, lanes]
            parts.append(jnp.where(upper, mixed[:, :64], mixed[:, 64:]))
        attended_t = jnp.concatenate(parts, axis=0)
        gated = (gate_t[:, s * 64 : (s + 1) * 64] * attended_t).astype(BF)
        result = own_ref[s].astype(F32) + mm(gated, wo_ref[...], TN)
        for h in range(2):
            for b in range(4):
                source = (h * 4 + b) * 8
                target = (b * 2 + h) * 8
                for half in range(2):
                    packed[target : target + 8, half * 4 + s, :] = result[
                        source : source + 8, half * 128 : (half + 1) * 128
                    ]
    out_ref[...] = packed[...].astype(BF)


def column_kernel(place, x_ref, w_ref, wo_ref, wf_ref, out_ref, left_ref, right_ref, scratch):
    del place
    scratch[...] = x_ref[...].astype(F32)
    x = jnp.concatenate(
        [
            jnp.concatenate([scratch[:, s, :], scratch[:, 4 + s, :]], axis=1)
            for s in range(4)
        ],
        axis=0,
    )
    normed = layer_norm(x).astype(BF)
    key = jnp.dot(normed, w_ref[:, 256:512], preferred_element_type=F32).astype(BF)
    value_t = mm(w_ref[:, 512:768], normed, TT).astype(BF)
    query_t = (mm(w_ref[:, 0:256], normed, TT) * SCALE).astype(BF)
    gate_t = sigmoid(mm(w_ref[:, 768:1024], normed, TT))
    head_row = lax.broadcasted_iota(jnp.int32, (256, 1024), 0) // 32
    head_lane = lax.broadcasted_iota(jnp.int32, (256, 1024), 1) // 256
    wide = jnp.concatenate([query_t] * 4, axis=1)

    def scores_of(group):
        diag = jnp.where(head_row == head_lane + group * 4, wide, jnp.zeros_like(wide))
        return jnp.dot(key, diag, preferred_element_type=F32)

    parts = []
    ahead = scores_of(0)
    for group in range(2):
        scores = ahead
        if group == 0:
            ahead = scores_of(1)
        weights, scale = exp_rows(scores)
        for k in range(4):
            h = group * 4 + k
            lanes = slice(k * 256, (k + 1) * 256)
            mixed = jnp.dot(
                value_t[h * 32 : (h + 1) * 32], weights[:, lanes], preferred_element_type=F32
            )
            parts.append(mixed * scale[:, lanes])
    gated = (gate_t * jnp.concatenate(parts, axis=0)).astype(BF)
    result = (x + mm(gated, wo_ref[...], TN)).astype(BF)
    factors = mm(wf_ref[...], layer_norm(result).astype(BF), NT).astype(BF)
    left_ref[...] = factors[:32]
    for c in range(8):
        right_ref[c] = factors[32:]
    wide = result.astype(F32)
    for s in range(4):
        for half in range(2):
            scratch[:, half * 4 + s, :] = wide[
                s * 64 : (s + 1) * 64, half * 128 : (half + 1) * 128
            ]
    out_ref[...] = scratch[...].astype(BF)


def spread_kernel(place, right_ref, *refs):
    lefts, out_ref = refs[:4], refs[4]
    blocks = [left[...] for left in lefts]
    for mask in range(4):
        start = pl.multiple_of((branch_of(place) ^ mask) * 32, 32)
        for r in range(16):
            out_ref[r, pl.ds(start, 32), :] = blocks[mask]
    for r in range(16):
        out_ref[r, 128:] = right_ref[r // 2]


def block_transpose(arrays):
    rows = arrays[0].shape[0]
    lane = lax.broadcasted_iota(jnp.int32, (rows, 128), 1)
    low = lane < 64
    even = (lane // 32) % 2 == 0
    a0, a1, a2, a3 = arrays
    u0 = jnp.where(low, a0, pltpu.roll(a2, 64, 1))
    u2 = jnp.where(low, pltpu.roll(a0, 64, 1), a2)
    u1 = jnp.where(low, a1, pltpu.roll(a3, 64, 1))
    u3 = jnp.where(low, pltpu.roll(a1, 64, 1), a3)
    b0 = jnp.where(even, u0, pltpu.roll(u1, 32, 1))
    b1 = jnp.where(even, pltpu.roll(u0, 96, 1), u1)
    b2 = jnp.where(even, u2, pltpu.roll(u3, 32, 1))
    b3 = jnp.where(even, pltpu.roll(u2, 96, 1), u3)
    return b0, b1, b2, b3


def by_target(rows):
    order = [(h * 4 + b) * 8 for b in range(4) for h in range(2)]
    count = rows.shape[0] // 64
    return jnp.concatenate(
        [rows[j * 64 + s : j * 64 + s + 8] for j in range(count) for s in order], axis=0
    )


def pair_kernel(place, factor_ref, pair_ref, wo_ref, w_ref, mid_ref, out_ref,
                outer, flat, scratch, tile_rows):
    right = factor_ref[pl.ds(half_of(place) * 8, 8), 128:, :].reshape(256, 256)
    for b in range(4):
        left = factor_ref[:, b * 32 : (b + 1) * 32, :].reshape(512, 256)
        product = (mm(left, right, NT) * (1.0 / 256)).reshape(16, 32, 256)
        for h in range(2):
            start = (h * 4 + b) * 8
            outer[start : start + 8] = product[h * 8 : (h + 1) * 8]
    for group in range(8):
        chans = [outer[:, group * 4 + k, :] for k in range(4)]
        for tile in range(2):
            moved = block_transpose([c[:, tile * 128 : (tile + 1) * 128] for c in chans])
            for k in range(4):
                j = tile * 4 + k
                flat[j * 64 : (j + 1) * 64, group * 128 : (group + 1) * 128] = moved[k].astype(BF)
    update = jnp.dot(flat[...], wo_ref[...], preferred_element_type=F32).astype(BF)
    first = pl.multiple_of(branch_of(place) * 8, 8)
    tile_rows[...] = pair_ref[:, pl.ds(first, 8), :].astype(F32)
    pair = jnp.concatenate([tile_rows[:, j, :] for j in range(8)], axis=0)
    mid = (pair + update.astype(F32)).astype(BF)
    mid_ref[...] = mid
    normed = layer_norm(mid)
    lane = lax.broadcasted_iota(jnp.int32, (64, 128), 1) < 64
    for side in range(2):
        rows = (by_target(normed) if side else normed).astype(BF)
        base = side * 256
        value = mm(w_ref[:, base : base + 128], rows, TT)
        gate = mm(w_ref[:, base + 128 : base + 256], rows, TT)
        both = sigmoid(gate) * value
        for pair in range(4):
            low = both[:64, pair * 128 : (pair + 1) * 128]
            high = both[64:, pair * 128 : (pair + 1) * 128]
            scratch[side, :, 2 * pair, :] = jnp.where(lane, low, pltpu.roll(high, 64, 1))
            scratch[side, :, 2 * pair + 1, :] = jnp.where(lane, pltpu.roll(low, 64, 1), high)
    out_ref[:, 0] = scratch[0].astype(BF)
    out_ref[:, 1] = scratch[1].astype(BF)


def triangle_kernel(place, left_ref, back_ref, *refs):
    same, near, far, out_ref = refs[:4], refs[4], refs[5], refs[6]
    left = left_ref[...]
    lane = lax.broadcasted_iota(jnp.int32, (64, 128), 1) < 64
    steps = (0, 1, 3, 2)
    for m in range(8):
        step = steps[m // 2]
        if m % 2 == 0:
            right = same[m // 2][...]
        else:
            right = far[...] if step == 2 else near[m // 2]
        product = mm(right, left, TN)
        block = jnp.where(lane, product[:64], product[64:]).astype(BF)
        target = source_of(col_of(place), step * 2 + m % 2) * 2
        for b in range(4):
            for h in range(2):
                out_ref[b * 16 + target + h, 0] = block[(b * 2 + h) * 8 : (b * 2 + h + 1) * 8]
    out_ref[:, 1] = back_ref[...]


def output_kernel(place, sum_ref, mid_ref, wg_ref, w_ref, out_ref, back_ref, scratch, rows):
    del place
    sums = sum_ref[:, 0].astype(F32)
    fold = lambda v: (v + pltpu.roll(v, 64, 1)) * (1.0 / 128)
    average = fold(jnp.sum(sums, axis=0))
    centered = sums - average[None]
    variance = fold(jnp.sum(jnp.square(centered), axis=0))
    scratch[...] = centered * lax.rsqrt(variance + EPSILON)[None]
    mid = mid_ref[...].astype(F32)
    gate_t = sigmoid(mm(wg_ref[...], layer_norm(mid).astype(BF), TT))
    weight = jnp.concatenate([w_ref[:64], w_ref[64:]], axis=1)
    lane = lax.broadcasted_iota(jnp.int32, (128, 128), 1) < 64

    def mixed_of(j):
        product = mm(weight, scratch[:, j, :].astype(BF), TN)
        return product[:128, :64] + product[128:, 64:]

    for j in range(4):
        mixed = jnp.concatenate([mixed_of(j), mixed_of(j + 4)], axis=1)
        ends = (slice(j * 64, (j + 1) * 64), slice((j + 4) * 64, (j + 5) * 64))
        residual = jnp.concatenate([mid[e] for e in ends], axis=0).T
        gate = jnp.concatenate([gate_t[:, e] for e in ends], axis=1)
        part = (residual + gate * mixed).astype(BF)
        for b in range(4):
            out_ref[b, j] = part[b * 32 : (b + 1) * 32]
    rows[...] = sum_ref[:, 1].astype(F32)
    order = [(b * 2 + h) * 8 for h in range(2) for b in range(4)]
    for s in range(4):
        for half in range(2):
            block = rows[:, half * 4 + s, :]
            block = jnp.concatenate([block[k : k + 8] for k in order], axis=0)
            back_ref[s, :, half * 128 : (half + 1) * 128] = block.astype(BF)


def unpack_kernel(x_ref, out_ref):
    for b in range(4):
        for j in range(4):
            block = x_ref[b, j]
            out_ref[b * 8 + j] = block[:, :64]
            out_ref[b * 8 + 4 + j] = block[:, 64:]


def shifted(x, step, flip):
    perm = [(c, (c // 2 - step) % 4 * 2 + (c % 2 ^ flip)) for c in range(8)]
    return lax.ppermute(x, "col", perm)


def gather_col(x):
    same = [x]
    for step in (1, 3, 2):
        same.append(shifted(x, step, 0))
    near = shifted(jnp.stack(same[:3]), 0, 1)
    far = shifted(same[3], 0, 1)
    return same + [near, far]


def local(
    alignment,
    pair_features,
    w_row,
    row_output_weight,
    w_bias,
    w_column,
    column_output_weight,
    outer_input_weight,
    w_outer_out,
    w_triangle_in,
    w_triangle_gate,
    w_triangle_out,
):
    both = ("branch", "row")
    place = lax.axis_index(("branch", "row", "col")).astype(jnp.int32).reshape(1)
    exchange = lambda x, axis: lax.all_to_all(x, axis, 0, 0, tiled=True)

    blocks = gather_col(alignment)
    bias = in_vmem(
        bias_kernel,
        [(16, 32, 512)],
        [
            pltpu.VMEM((64, 32, 128), BF),
            pltpu.VMEM((8, 128), BF),
            pltpu.VMEM((64, 32, 128), F32),
            pltpu.VMEM((16, 8, 128), F32),
            pltpu.SemaphoreType.DMA((5,)),
        ],
        place,
        pair_features,
        w_bias.T,
        loose=2,
    )
    bias = exchange(bias, "row").reshape(512, 512)

    columns = in_vmem(
        row_kernel,
        [(64, 8, 128)],
        [
            pltpu.VMEM((4, 512, 256), BF),
            pltpu.VMEM((2048, 256), BF),
            pltpu.VMEM((256, 2048), BF),
            pltpu.VMEM((64, 8, 128), F32),
        ],
        place,
        *blocks,
        w_row,
        bias,
        row_output_weight,
    )
    columns = exchange(columns, both)
    returning, left, right = in_vmem(
        column_kernel,
        [(64, 8, 128), (32, 256), (8, 32, 256)],
        [pltpu.VMEM((64, 8, 128), F32)],
        place,
        columns,
        w_column,
        column_output_weight,
        outer_input_weight.T,
    )

    right = exchange(right, "col")
    lefts = [left]
    for mask in (1, 2, 3):
        lefts.append(lax.ppermute(left, "branch", [(b, b ^ mask) for b in range(4)]))
    factors = in_vmem(spread_kernel, [(16, 160, 256)], [], place, right, *lefts)
    factors = exchange(factors, "row")

    mid, message = in_vmem(
        pair_kernel,
        [(512, 128), (64, 2, 8, 128)],
        [
            pltpu.VMEM((64, 32, 256), F32),
            pltpu.VMEM((512, 1024), BF),
            pltpu.VMEM((2, 64, 8, 128), F32),
            pltpu.VMEM((64, 8, 128), F32),
        ],
        place,
        factors,
        pair_features,
        w_outer_out,
        w_triangle_in,
    )
    message = exchange(message, both)
    tri_left = message[:, 0].reshape(512, 128)
    rights = gather_col(message[:, 1].reshape(512, 128))
    sums = in_vmem(triangle_kernel, [(64, 2, 8, 128)], [], place, tri_left, returning, *rights)
    sums = exchange(sums, both)
    parts, alignment_out = in_vmem(
        output_kernel,
        [(4, 4, 32, 128), (4, 64, 256)],
        [pltpu.VMEM((64, 8, 128), F32), pltpu.VMEM((64, 8, 128), F32)],
        place,
        sums,
        mid,
        w_triangle_gate,
        w_triangle_out,
        results=1,
    )
    parts = exchange(parts, "branch")
    pair_out = pl.pallas_call(
        unpack_kernel,
        out_shape=jax.ShapeDtypeStruct((32, 32, 64), BF),
        in_specs=[VM],
        name="unpack",
    )(pltpu.with_memory_space_constraint(parts, pltpu.VMEM))
    return (alignment_out, jnp.transpose(pair_out, (2, 0, 1)))


def solution(mesh):
    in_specs = (P(("branch", "row"), "col", None), P("col", "row", None)) + (P(),) * 10
    out_specs = (P(("branch", "row"), "col", None), P("col", "row", "branch"))
    return jax.shard_map(local, mesh=mesh, in_specs=in_specs, out_specs=out_specs, check_vma=False)
```

```python
import jax
import jax.numpy as jnp
from jax import lax
from jax.experimental import pallas as pl
from jax.experimental.pallas import tpu as pltpu
from jax.sharding import PartitionSpec as P


BF = jnp.bfloat16
F32 = jnp.float32
EPSILON = 1e-05
SCALE = 32**-0.5

NT = (((1,), (1,)), ((), ()))
TN = (((0,), (0,)), ((), ()))
TT = (((0,), (1,)), ((), ()))


def mm(a, b, dims):
    return lax.dot_general(a, b, dims, preferred_element_type=F32)


def layer_norm(inputs):
    inputs = inputs.astype(F32)
    average = jnp.mean(inputs, axis=-1, keepdims=True)
    centered = inputs - average
    variance = jnp.mean(jnp.square(centered), axis=-1, keepdims=True)
    return centered * lax.rsqrt(variance + EPSILON)


def sigmoid(x):
    return 1.0 / (1.0 + jnp.exp(-x))


def exp_rows(scores):
    top = jnp.max(scores, axis=0, keepdims=True)
    weights = jnp.exp(scores - top)
    total = jnp.sum(weights, axis=0, keepdims=True)
    return weights.astype(BF), 1.0 / total


VM = pl.BlockSpec(memory_space=pltpu.VMEM)
SM = pl.BlockSpec(memory_space=pltpu.SMEM)
HB = pl.BlockSpec(memory_space=pltpu.HBM)


def in_vmem(kernel, outs, scratch, place, *args, loose=0, results=0):
    loosely = [pltpu.with_memory_space_constraint(a, pltpu.HBM) for a in args[:loose]]
    fixed = [pltpu.with_memory_space_constraint(a, pltpu.VMEM) for a in args[loose:]]
    inner = len(outs) - results
    shapes = [pltpu.VMEM(shape, BF) for shape in outs[:inner]]
    shapes += [jax.ShapeDtypeStruct(shape, BF) for shape in outs[inner:]]
    outputs = pl.pallas_call(
        kernel,
        out_shape=tuple(shapes),
        in_specs=[SM] + [HB] * loose + [VM] * len(fixed),
        out_specs=(VM,) * inner + (pl.BlockSpec(),) * results,
        scratch_shapes=scratch,
        compiler_params=pltpu.CompilerParams(vmem_limit_bytes=24 << 20),
    )(place, *loosely, *fixed)
    return outputs if len(outs) > 1 else outputs[0]


def col_of(place):
    return place[0] & 7


def half_of(place):
    return (place[0] >> 3) & 1


def branch_of(place):
    return place[0] >> 7


def source_of(col, m):
    return (((col >> 1) + (m >> 1)) & 3) * 2 + ((col & 1) ^ (m & 1))


def bias_kernel(place, pair_ref, w_ref, out_ref, pair, weight, rows, heads, sems):
    del place
    copies = [pltpu.make_async_copy(w_ref, weight, sems.at[4])]
    for q in range(4):
        part = pl.ds(q * 16, 16)
        copies.append(pltpu.make_async_copy(pair_ref.at[part], pair.at[part], sems.at[q]))
    for copy in copies:
        copy.start()
    for q in range(4):
        copies[q + 1].wait()
        block = pair[q * 16 : (q + 1) * 16].reshape(512, 128)
        rows[q * 16 : (q + 1) * 16] = layer_norm(block).astype(BF).astype(F32).reshape(16, 32, 128)
    copies[0].wait()
    for j in range(16):
        pairs = jnp.concatenate([rows[:, j, :], rows[:, j + 16, :]], axis=0).astype(BF)
        heads[j] = mm(weight[...], pairs, NT)
    lane = lax.broadcasted_iota(jnp.int32, (16, 128), 1) < 64
    tiles = []
    for p in range(4):
        a = heads[:, 2 * p, :]
        b = heads[:, 2 * p + 1, :]
        first = jnp.where(lane, a, pltpu.roll(b, 64, 1))
        second = jnp.where(lane, pltpu.roll(a, 64, 1), b)
        tiles.append(jnp.concatenate([first, second], axis=0))
    tile = jnp.concatenate(tiles, axis=1).astype(BF)
    for r in range(16):
        out_ref[r] = tile


def row_kernel(place, *refs):
    own_ref, z1_ref, z3_ref, z2_ref, swap_ref, last_ref = refs[:6]
    w_ref, bias_ref, wo_ref, out_ref, rows, keys, values, packed = refs[6:]
    for m, block in (
        (0, own_ref[...]),
        (2, z1_ref[...]),
        (6, z3_ref[...]),
        (1, swap_ref[0]),
        (3, swap_ref[1]),
        (7, swap_ref[2]),
        (4, z2_ref[...]),
        (5, last_ref[...]),
    ):
        start = pl.multiple_of(source_of(col_of(place), m) * 64, 64)
        normed = layer_norm(block.reshape(256, 256)).astype(BF)
        if m == 0:
            own = normed
        for s in range(4):
            rows[s, pl.ds(start, 64), :] = normed[s * 64 : (s + 1) * 64]
    x = rows[...].reshape(2048, 256)
    keys[...] = jnp.dot(x, w_ref[:, 256:512], preferred_element_type=F32).astype(BF)
    values[...] = mm(w_ref[:, 512:768], x, TT).astype(BF)
    query_t = (mm(w_ref[:, 0:256], own, TT) * SCALE).astype(BF)
    gate_t = sigmoid(mm(w_ref[:, 768:1024], own, TT))
    head_row = lax.broadcasted_iota(jnp.int32, (256, 512), 0) // 32
    head_lane = lax.broadcasted_iota(jnp.int32, (256, 512), 1) // 64
    upper = lax.broadcasted_iota(jnp.int32, (64, 64), 0) < 32

    def scores_of(s):
        wide = jnp.concatenate([query_t[:, s * 64 : (s + 1) * 64]] * 8, axis=1)
        diag = jnp.where(head_row == head_lane, wide, jnp.zeros_like(wide))
        scores = jnp.dot(keys[s * 512 : (s + 1) * 512], diag, preferred_element_type=F32)
        return scores + bias_ref[...].astype(F32)

    ahead = scores_of(0)
    for s in range(4):
        scores = ahead
        if s < 3:
            ahead = scores_of(s + 1)
        weights, scale = exp_rows(scores)
        parts = []
        for p in range(4):
            lanes = slice(p * 128, (p + 1) * 128)
            mixed = jnp.dot(
                values[p * 64 : (p + 1) * 64, s * 512 : (s + 1) * 512],
                weights[:, lanes],
                preferred_element_type=F32,
            )
            mixed = mixed * scale[:, lanes]
            parts.append(jnp.where(upper, mixed[:, :64], mixed[:, 64:]))
        attended_t = jnp.concatenate(parts, axis=0)
        gated = (gate_t[:, s * 64 : (s + 1) * 64] * attended_t).astype(BF)
        result = own_ref[s].astype(F32) + mm(gated, wo_ref[...], TN)
        for h in range(2):
            for b in range(4):
                source = (h * 4 + b) * 8
                target = (b * 2 + h) * 8
                for half in range(2):
                    packed[target : target + 8, half * 4 + s, :] = result[
                        source : source + 8, half * 128 : (half + 1) * 128
                    ]
    out_ref[...] = packed[...].astype(BF)


def column_kernel(place, x_ref, w_ref, wo_ref, wf_ref, out_ref, left_ref, right_ref, scratch):
    del place
    scratch[...] = x_ref[...].astype(F32)
    x = jnp.concatenate(
        [
            jnp.concatenate([scratch[:, s, :], scratch[:, 4 + s, :]], axis=1)
            for s in range(4)
        ],
        axis=0,
    )
    normed = layer_norm(x).astype(BF)
    key = jnp.dot(normed, w_ref[:, 256:512], preferred_element_type=F32).astype(BF)
    value_t = mm(w_ref[:, 512:768], normed, TT).astype(BF)
    query_t = (mm(w_ref[:, 0:256], normed, TT) * SCALE).astype(BF)
    gate_t = sigmoid(mm(w_ref[:, 768:1024], normed, TT))
    head_row = lax.broadcasted_iota(jnp.int32, (256, 1024), 0) // 32
    head_lane = lax.broadcasted_iota(jnp.int32, (256, 1024), 1) // 256
    wide = jnp.concatenate([query_t] * 4, axis=1)

    def scores_of(group):
        diag = jnp.where(head_row == head_lane + group * 4, wide, jnp.zeros_like(wide))
        return jnp.dot(key, diag, preferred_element_type=F32)

    parts = []
    ahead = scores_of(0)
    for group in range(2):
        scores = ahead
        if group == 0:
            ahead = scores_of(1)
        weights, scale = exp_rows(scores)
        for k in range(4):
            h = group * 4 + k
            lanes = slice(k * 256, (k + 1) * 256)
            mixed = jnp.dot(
                value_t[h * 32 : (h + 1) * 32], weights[:, lanes], preferred_element_type=F32
            )
            parts.append(mixed * scale[:, lanes])
    gated = (gate_t * jnp.concatenate(parts, axis=0)).astype(BF)
    result = (x + mm(gated, wo_ref[...], TN)).astype(BF)
    factors = mm(wf_ref[...], layer_norm(result).astype(BF), NT).astype(BF)
    left_ref[...] = factors[:32]
    for c in range(8):
        right_ref[c] = factors[32:]
    wide = result.astype(F32)
    for s in range(4):
        for half in range(2):
            scratch[:, half * 4 + s, :] = wide[
                s * 64 : (s + 1) * 64, half * 128 : (half + 1) * 128
            ]
    out_ref[...] = scratch[...].astype(BF)


def spread_kernel(place, right_ref, *refs):
    lefts, out_ref = refs[:4], refs[4]
    blocks = [left[...] for left in lefts]
    for mask in range(4):
        start = pl.multiple_of((branch_of(place) ^ mask) * 32, 32)
        for r in range(16):
            out_ref[r, pl.ds(start, 32), :] = blocks[mask]
    for r in range(16):
        out_ref[r, 128:] = right_ref[r // 2]


def block_transpose(arrays):
    rows = arrays[0].shape[0]
    lane = lax.broadcasted_iota(jnp.int32, (rows, 128), 1)
    low = lane < 64
    even = (lane // 32) % 2 == 0
    a0, a1, a2, a3 = arrays
    u0 = jnp.where(low, a0, pltpu.roll(a2, 64, 1))
    u2 = jnp.where(low, pltpu.roll(a0, 64, 1), a2)
    u1 = jnp.where(low, a1, pltpu.roll(a3, 64, 1))
    u3 = jnp.where(low, pltpu.roll(a1, 64, 1), a3)
    b0 = jnp.where(even, u0, pltpu.roll(u1, 32, 1))
    b1 = jnp.where(even, pltpu.roll(u0, 96, 1), u1)
    b2 = jnp.where(even, u2, pltpu.roll(u3, 32, 1))
    b3 = jnp.where(even, pltpu.roll(u2, 96, 1), u3)
    return b0, b1, b2, b3


def by_target(rows):
    order = [(h * 4 + b) * 8 for b in range(4) for h in range(2)]
    count = rows.shape[0] // 64
    return jnp.concatenate(
        [rows[j * 64 + s : j * 64 + s + 8] for j in range(count) for s in order], axis=0
    )


def pair_kernel(place, factor_ref, pair_ref, wo_ref, w_ref, mid_ref, out_ref,
                outer, flat, scratch, tile_rows):
    right = factor_ref[pl.ds(half_of(place) * 8, 8), 128:, :].reshape(256, 256)
    for b in range(4):
        left = factor_ref[:, b * 32 : (b + 1) * 32, :].reshape(512, 256)
        product = (mm(left, right, NT) * (1.0 / 256)).reshape(16, 32, 256)
        for h in range(2):
            start = (h * 4 + b) * 8
            outer[start : start + 8] = product[h * 8 : (h + 1) * 8]
    for group in range(8):
        chans = [outer[:, group * 4 + k, :] for k in range(4)]
        for tile in range(2):
            moved = block_transpose([c[:, tile * 128 : (tile + 1) * 128] for c in chans])
            for k in range(4):
                j = tile * 4 + k
                flat[j * 64 : (j + 1) * 64, group * 128 : (group + 1) * 128] = moved[k].astype(BF)
    update = jnp.dot(flat[...], wo_ref[...], preferred_element_type=F32).astype(BF)
    first = pl.multiple_of(branch_of(place) * 8, 8)
    tile_rows[...] = pair_ref[:, pl.ds(first, 8), :].astype(F32)
    pair = jnp.concatenate([tile_rows[:, j, :] for j in range(8)], axis=0)
    mid = (pair + update.astype(F32)).astype(BF)
    mid_ref[...] = mid
    normed = layer_norm(mid)
    lane = lax.broadcasted_iota(jnp.int32, (64, 128), 1) < 64
    for side in range(2):
        rows = (by_target(normed) if side else normed).astype(BF)
        base = side * 256
        value = mm(w_ref[:, base : base + 128], rows, TT)
        gate = mm(w_ref[:, base + 128 : base + 256], rows, TT)
        both = sigmoid(gate) * value
        for pair in range(4):
            low = both[:64, pair * 128 : (pair + 1) * 128]
            high = both[64:, pair * 128 : (pair + 1) * 128]
            scratch[side, :, 2 * pair, :] = jnp.where(lane, low, pltpu.roll(high, 64, 1))
            scratch[side, :, 2 * pair + 1, :] = jnp.where(lane, pltpu.roll(low, 64, 1), high)
    out_ref[:, 0] = scratch[0].astype(BF)
    out_ref[:, 1] = scratch[1].astype(BF)


def triangle_kernel(place, left_ref, back_ref, *refs):
    same, other, out_ref = refs[:4], refs[4:6], refs[6]
    left = left_ref[...]
    lane = lax.broadcasted_iota(jnp.int32, (64, 128), 1) < 64
    for m in range(8):
        step = m // 2
        right = other[step % 2][step // 2] if m % 2 else same[step][...]
        product = mm(right, left, TN)
        block = jnp.where(lane, product[:64], product[64:]).astype(BF)
        target = source_of(col_of(place), m) * 2
        for b in range(4):
            for h in range(2):
                out_ref[b * 16 + target + h, 0] = block[(b * 2 + h) * 8 : (b * 2 + h + 1) * 8]
    out_ref[:, 1] = back_ref[...]


def output_kernel(place, sum_ref, mid_ref, wg_ref, w_ref, out_ref, back_ref, scratch, rows):
    del place
    sums = sum_ref[:, 0].astype(F32)
    fold = lambda v: (v + pltpu.roll(v, 64, 1)) * (1.0 / 128)
    average = fold(jnp.sum(sums, axis=0))
    centered = sums - average[None]
    variance = fold(jnp.sum(jnp.square(centered), axis=0))
    scratch[...] = centered * lax.rsqrt(variance + EPSILON)[None]
    mid = mid_ref[...].astype(F32)
    gate_t = sigmoid(mm(wg_ref[...], layer_norm(mid).astype(BF), TT))
    weight = jnp.concatenate([w_ref[:64], w_ref[64:]], axis=1)
    lane = lax.broadcasted_iota(jnp.int32, (128, 128), 1) < 64

    def mixed_of(j):
        product = mm(weight, scratch[:, j, :].astype(BF), TN)
        return product[:128, :64] + product[128:, 64:]

    for j in range(4):
        mixed = jnp.concatenate([mixed_of(j), mixed_of(j + 4)], axis=1)
        ends = (slice(j * 64, (j + 1) * 64), slice((j + 4) * 64, (j + 5) * 64))
        residual = jnp.concatenate([mid[e] for e in ends], axis=0).T
        gate = jnp.concatenate([gate_t[:, e] for e in ends], axis=1)
        part = (residual + gate * mixed).astype(BF)
        for b in range(4):
            out_ref[b, j] = part[b * 32 : (b + 1) * 32]
    rows[...] = sum_ref[:, 1].astype(F32)
    order = [(b * 2 + h) * 8 for h in range(2) for b in range(4)]
    for s in range(4):
        for half in range(2):
            block = rows[:, half * 4 + s, :]
            block = jnp.concatenate([block[k : k + 8] for k in order], axis=0)
            back_ref[s, :, half * 128 : (half + 1) * 128] = block.astype(BF)


def unpack_kernel(x_ref, out_ref):
    for b in range(4):
        for j in range(4):
            block = x_ref[b, j]
            out_ref[b * 8 + j] = block[:, :64]
            out_ref[b * 8 + 4 + j] = block[:, 64:]


def shifted(x, step, flip):
    perm = [(c, (c // 2 - step) % 4 * 2 + (c % 2 ^ flip)) for c in range(8)]
    return lax.ppermute(x, "col", perm)


def gather_col(x):
    same = [x]
    for step in (1, 3, 2):
        same.append(shifted(x, step, 0))
    near = shifted(jnp.stack(same[:3]), 0, 1)
    far = shifted(same[3], 0, 1)
    return same + [near, far]


def gather_far_first(x):
    same, other = {0: x}, {}
    for step in (2, 1, 3):
        same[step] = shifted(x, step, 0)
    for pair in ((0, 2), (1, 3)):
        other[pair[0]] = shifted(jnp.stack([same[k] for k in pair]), 0, 1)
    return [same[k] for k in range(4)] + [other[0], other[1]]


def local(
    alignment,
    pair_features,
    w_row,
    row_output_weight,
    w_bias,
    w_column,
    column_output_weight,
    outer_input_weight,
    w_outer_out,
    w_triangle_in,
    w_triangle_gate,
    w_triangle_out,
):
    both = ("branch", "row")
    place = lax.axis_index(("branch", "row", "col")).astype(jnp.int32).reshape(1)
    exchange = lambda x, axis: lax.all_to_all(x, axis, 0, 0, tiled=True)

    blocks = gather_col(alignment)
    bias = in_vmem(
        bias_kernel,
        [(16, 32, 512)],
        [
            pltpu.VMEM((64, 32, 128), BF),
            pltpu.VMEM((8, 128), BF),
            pltpu.VMEM((64, 32, 128), F32),
            pltpu.VMEM((16, 8, 128), F32),
            pltpu.SemaphoreType.DMA((5,)),
        ],
        place,
        pair_features,
        w_bias.T,
        loose=2,
    )
    bias = exchange(bias, "row").reshape(512, 512)

    columns = in_vmem(
        row_kernel,
        [(64, 8, 128)],
        [
            pltpu.VMEM((4, 512, 256), BF),
            pltpu.VMEM((2048, 256), BF),
            pltpu.VMEM((256, 2048), BF),
            pltpu.VMEM((64, 8, 128), F32),
        ],
        place,
        *blocks,
        w_row,
        bias,
        row_output_weight,
    )
    columns = exchange(columns, both)
    returning, left, right = in_vmem(
        column_kernel,
        [(64, 8, 128), (32, 256), (8, 32, 256)],
        [pltpu.VMEM((64, 8, 128), F32)],
        place,
        columns,
        w_column,
        column_output_weight,
        outer_input_weight.T,
    )

    right = exchange(right, "col")
    lefts = [left]
    for mask in (1, 2, 3):
        lefts.append(lax.ppermute(left, "branch", [(b, b ^ mask) for b in range(4)]))
    factors = in_vmem(spread_kernel, [(16, 160, 256)], [], place, right, *lefts)
    factors = exchange(factors, "row")

    mid, message = in_vmem(
        pair_kernel,
        [(512, 128), (64, 2, 8, 128)],
        [
            pltpu.VMEM((64, 32, 256), F32),
            pltpu.VMEM((512, 1024), BF),
            pltpu.VMEM((2, 64, 8, 128), F32),
            pltpu.VMEM((64, 8, 128), F32),
        ],
        place,
        factors,
        pair_features,
        w_outer_out,
        w_triangle_in,
    )
    message = exchange(message, both)
    tri_left = message[:, 0].reshape(512, 128)
    rights = gather_far_first(message[:, 1].reshape(512, 128))
    sums = in_vmem(triangle_kernel, [(64, 2, 8, 128)], [], place, tri_left, returning, *rights)
    sums = exchange(sums, both)
    parts, alignment_out = in_vmem(
        output_kernel,
        [(4, 4, 32, 128), (4, 64, 256)],
        [pltpu.VMEM((64, 8, 128), F32), pltpu.VMEM((64, 8, 128), F32)],
        place,
        sums,
        mid,
        w_triangle_gate,
        w_triangle_out,
        results=1,
    )
    parts = exchange(parts, "branch")
    pair_out = pl.pallas_call(
        unpack_kernel,
        out_shape=jax.ShapeDtypeStruct((32, 32, 64), BF),
        in_specs=[VM],
        name="unpack",
    )(pltpu.with_memory_space_constraint(parts, pltpu.VMEM))
    return (alignment_out, jnp.transpose(pair_out, (2, 0, 1)))


def solution(mesh):
    in_specs = (P(("branch", "row"), "col", None), P("col", "row", None)) + (P(),) * 10
    out_specs = (P(("branch", "row"), "col", None), P("col", "row", "branch"))
    return jax.shard_map(local, mesh=mesh, in_specs=in_specs, out_specs=out_specs, check_vma=False)
```

```python
import jax
import jax.numpy as jnp
from jax import lax
from jax.experimental import pallas as pl
from jax.experimental.pallas import tpu as pltpu
from jax.sharding import PartitionSpec as P


BF = jnp.bfloat16
F32 = jnp.float32
EPSILON = 1e-05
SCALE = 32**-0.5

NT = (((1,), (1,)), ((), ()))
TN = (((0,), (0,)), ((), ()))
TT = (((0,), (1,)), ((), ()))


def mm(a, b, dims):
    return lax.dot_general(a, b, dims, preferred_element_type=F32)


def layer_norm(inputs):
    inputs = inputs.astype(F32)
    average = jnp.mean(inputs, axis=-1, keepdims=True)
    centered = inputs - average
    variance = jnp.mean(jnp.square(centered), axis=-1, keepdims=True)
    return centered * lax.rsqrt(variance + EPSILON)


def sigmoid(x):
    return 1.0 / (1.0 + jnp.exp(-x))


def exp_rows(scores):
    top = jnp.max(scores, axis=0, keepdims=True)
    weights = jnp.exp(scores - top)
    total = jnp.sum(weights, axis=0, keepdims=True)
    return weights.astype(BF), 1.0 / total


VM = pl.BlockSpec(memory_space=pltpu.VMEM)
SM = pl.BlockSpec(memory_space=pltpu.SMEM)
HB = pl.BlockSpec(memory_space=pltpu.HBM)


def in_vmem(kernel, outs, scratch, place, *args, loose=0, results=0):
    loosely = [pltpu.with_memory_space_constraint(a, pltpu.HBM) for a in args[:loose]]
    fixed = [pltpu.with_memory_space_constraint(a, pltpu.VMEM) for a in args[loose:]]
    inner = len(outs) - results
    shapes = [pltpu.VMEM(shape, BF) for shape in outs[:inner]]
    shapes += [jax.ShapeDtypeStruct(shape, BF) for shape in outs[inner:]]
    outputs = pl.pallas_call(
        kernel,
        out_shape=tuple(shapes),
        in_specs=[SM] + [HB] * loose + [VM] * len(fixed),
        out_specs=(VM,) * inner + (pl.BlockSpec(),) * results,
        scratch_shapes=scratch,
        compiler_params=pltpu.CompilerParams(vmem_limit_bytes=24 << 20),
    )(place, *loosely, *fixed)
    return outputs if len(outs) > 1 else outputs[0]


def col_of(place):
    return place[0] & 7


def half_of(place):
    return (place[0] >> 3) & 1


def branch_of(place):
    return place[0] >> 7


def source_of(col, m):
    return (((col >> 1) + (m >> 1)) & 3) * 2 + ((col & 1) ^ (m & 1))


def bias_kernel(place, pair_ref, w_ref, out_ref, pair, weight, rows, heads, sems):
    del place
    copies = [pltpu.make_async_copy(w_ref, weight, sems.at[4])]
    for q in range(4):
        part = pl.ds(q * 16, 16)
        copies.append(pltpu.make_async_copy(pair_ref.at[part], pair.at[part], sems.at[q]))
    for copy in copies:
        copy.start()
    for q in range(4):
        copies[q + 1].wait()
        block = pair[q * 16 : (q + 1) * 16].reshape(512, 128)
        rows[q * 16 : (q + 1) * 16] = layer_norm(block).astype(BF).astype(F32).reshape(16, 32, 128)
    copies[0].wait()
    for j in range(16):
        pairs = jnp.concatenate([rows[:, j, :], rows[:, j + 16, :]], axis=0).astype(BF)
        heads[j] = mm(weight[...], pairs, NT)
    lane = lax.broadcasted_iota(jnp.int32, (16, 128), 1) < 64
    tiles = []
    for p in range(4):
        a = heads[:, 2 * p, :]
        b = heads[:, 2 * p + 1, :]
        first = jnp.where(lane, a, pltpu.roll(b, 64, 1))
        second = jnp.where(lane, pltpu.roll(a, 64, 1), b)
        tiles.append(jnp.concatenate([first, second], axis=0))
    tile = jnp.concatenate(tiles, axis=1).astype(BF)
    for r in range(16):
        out_ref[r] = tile


def row_kernel(place, *refs):
    own_ref, z1_ref, z2_ref, z3_ref, even_ref, odd_ref = refs[:6]
    w_ref, bias_ref, wo_ref, out_ref, rows, keys, values, packed = refs[6:]
    for m, block in (
        (0, own_ref[...]),
        (4, z2_ref[...]),
        (1, even_ref[0]),
        (5, even_ref[1]),
        (2, z1_ref[...]),
        (6, z3_ref[...]),
        (3, odd_ref[0]),
        (7, odd_ref[1]),
    ):
        start = pl.multiple_of(source_of(col_of(place), m) * 64, 64)
        normed = layer_norm(block.reshape(256, 256)).astype(BF)
        if m == 0:
            own = normed
        for s in range(4):
            rows[s, pl.ds(start, 64), :] = normed[s * 64 : (s + 1) * 64]
    x = rows[...].reshape(2048, 256)
    keys[...] = jnp.dot(x, w_ref[:, 256:512], preferred_element_type=F32).astype(BF)
    values[...] = mm(w_ref[:, 512:768], x, TT).astype(BF)
    query_t = (mm(w_ref[:, 0:256], own, TT) * SCALE).astype(BF)
    gate_t = sigmoid(mm(w_ref[:, 768:1024], own, TT))
    head_row = lax.broadcasted_iota(jnp.int32, (256, 512), 0) // 32
    head_lane = lax.broadcasted_iota(jnp.int32, (256, 512), 1) // 64
    upper = lax.broadcasted_iota(jnp.int32, (64, 64), 0) < 32

    def scores_of(s):
        wide = jnp.concatenate([query_t[:, s * 64 : (s + 1) * 64]] * 8, axis=1)
        diag = jnp.where(head_row == head_lane, wide, jnp.zeros_like(wide))
        scores = jnp.dot(keys[s * 512 : (s + 1) * 512], diag, preferred_element_type=F32)
        return scores + bias_ref[...].astype(F32)

    ahead = scores_of(0)
    for s in range(4):
        scores = ahead
        if s < 3:
            ahead = scores_of(s + 1)
        weights, scale = exp_rows(scores)
        parts = []
        for p in range(4):
            lanes = slice(p * 128, (p + 1) * 128)
            mixed = jnp.dot(
                values[p * 64 : (p + 1) * 64, s * 512 : (s + 1) * 512],
                weights[:, lanes],
                preferred_element_type=F32,
            )
            mixed = mixed * scale[:, lanes]
            parts.append(jnp.where(upper, mixed[:, :64], mixed[:, 64:]))
        attended_t = jnp.concatenate(parts, axis=0)
        gated = (gate_t[:, s * 64 : (s + 1) * 64] * attended_t).astype(BF)
        result = own_ref[s].astype(F32) + mm(gated, wo_ref[...], TN)
        for h in range(2):
            for b in range(4):
                source = (h * 4 + b) * 8
                target = (b * 2 + h) * 8
                for half in range(2):
                    packed[target : target + 8, half * 4 + s, :] = result[
                        source : source + 8, half * 128 : (half + 1) * 128
                    ]
    out_ref[...] = packed[...].astype(BF)


def column_kernel(place, x_ref, w_ref, wo_ref, wf_ref, out_ref, left_ref, right_ref, scratch):
    del place
    scratch[...] = x_ref[...].astype(F32)
    x = jnp.concatenate(
        [
            jnp.concatenate([scratch[:, s, :], scratch[:, 4 + s, :]], axis=1)
            for s in range(4)
        ],
        axis=0,
    )
    normed = layer_norm(x).astype(BF)
    key = jnp.dot(normed, w_ref[:, 256:512], preferred_element_type=F32).astype(BF)
    value_t = mm(w_ref[:, 512:768], normed, TT).astype(BF)
    query_t = (mm(w_ref[:, 0:256], normed, TT) * SCALE).astype(BF)
    gate_t = sigmoid(mm(w_ref[:, 768:1024], normed, TT))
    head_row = lax.broadcasted_iota(jnp.int32, (256, 1024), 0) // 32
    head_lane = lax.broadcasted_iota(jnp.int32, (256, 1024), 1) // 256
    wide = jnp.concatenate([query_t] * 4, axis=1)

    def scores_of(group):
        diag = jnp.where(head_row == head_lane + group * 4, wide, jnp.zeros_like(wide))
        return jnp.dot(key, diag, preferred_element_type=F32)

    parts = []
    ahead = scores_of(0)
    for group in range(2):
        scores = ahead
        if group == 0:
            ahead = scores_of(1)
        weights, scale = exp_rows(scores)
        for k in range(4):
            h = group * 4 + k
            lanes = slice(k * 256, (k + 1) * 256)
            mixed = jnp.dot(
                value_t[h * 32 : (h + 1) * 32], weights[:, lanes], preferred_element_type=F32
            )
            parts.append(mixed * scale[:, lanes])
    gated = (gate_t * jnp.concatenate(parts, axis=0)).astype(BF)
    result = (x + mm(gated, wo_ref[...], TN)).astype(BF)
    factors = mm(wf_ref[...], layer_norm(result).astype(BF), NT).astype(BF)
    left_ref[...] = factors[:32]
    for c in range(8):
        right_ref[c] = factors[32:]
    wide = result.astype(F32)
    for s in range(4):
        for half in range(2):
            scratch[:, half * 4 + s, :] = wide[
                s * 64 : (s + 1) * 64, half * 128 : (half + 1) * 128
            ]
    out_ref[...] = scratch[...].astype(BF)


def spread_kernel(place, right_ref, *refs):
    lefts, out_ref = refs[:4], refs[4]
    blocks = [left[...] for left in lefts]
    for mask in range(4):
        start = pl.multiple_of((branch_of(place) ^ mask) * 32, 32)
        for r in range(16):
            out_ref[r, pl.ds(start, 32), :] = blocks[mask]
    for r in range(16):
        out_ref[r, 128:] = right_ref[r // 2]


def block_transpose(arrays):
    rows = arrays[0].shape[0]
    lane = lax.broadcasted_iota(jnp.int32, (rows, 128), 1)
    low = lane < 64
    even = (lane // 32) % 2 == 0
    a0, a1, a2, a3 = arrays
    u0 = jnp.where(low, a0, pltpu.roll(a2, 64, 1))
    u2 = jnp.where(low, pltpu.roll(a0, 64, 1), a2)
    u1 = jnp.where(low, a1, pltpu.roll(a3, 64, 1))
    u3 = jnp.where(low, pltpu.roll(a1, 64, 1), a3)
    b0 = jnp.where(even, u0, pltpu.roll(u1, 32, 1))
    b1 = jnp.where(even, pltpu.roll(u0, 96, 1), u1)
    b2 = jnp.where(even, u2, pltpu.roll(u3, 32, 1))
    b3 = jnp.where(even, pltpu.roll(u2, 96, 1), u3)
    return b0, b1, b2, b3


def by_target(rows):
    order = [(h * 4 + b) * 8 for b in range(4) for h in range(2)]
    count = rows.shape[0] // 64
    return jnp.concatenate(
        [rows[j * 64 + s : j * 64 + s + 8] for j in range(count) for s in order], axis=0
    )


def pair_kernel(place, factor_ref, pair_ref, wo_ref, w_ref, mid_ref, out_ref,
                outer, flat, scratch, tile_rows):
    right = factor_ref[pl.ds(half_of(place) * 8, 8), 128:, :].reshape(256, 256)
    for b in range(4):
        left = factor_ref[:, b * 32 : (b + 1) * 32, :].reshape(512, 256)
        product = (mm(left, right, NT) * (1.0 / 256)).reshape(16, 32, 256)
        for h in range(2):
            start = (h * 4 + b) * 8
            outer[start : start + 8] = product[h * 8 : (h + 1) * 8]
    for group in range(8):
        chans = [outer[:, group * 4 + k, :] for k in range(4)]
        for tile in range(2):
            moved = block_transpose([c[:, tile * 128 : (tile + 1) * 128] for c in chans])
            for k in range(4):
                j = tile * 4 + k
                flat[j * 64 : (j + 1) * 64, group * 128 : (group + 1) * 128] = moved[k].astype(BF)
    update = jnp.dot(flat[...], wo_ref[...], preferred_element_type=F32).astype(BF)
    first = pl.multiple_of(branch_of(place) * 8, 8)
    tile_rows[...] = pair_ref[:, pl.ds(first, 8), :].astype(F32)
    pair = jnp.concatenate([tile_rows[:, j, :] for j in range(8)], axis=0)
    mid = (pair + update.astype(F32)).astype(BF)
    mid_ref[...] = mid
    normed = layer_norm(mid)
    lane = lax.broadcasted_iota(jnp.int32, (64, 128), 1) < 64
    for side in range(2):
        rows = (by_target(normed) if side else normed).astype(BF)
        base = side * 256
        value = mm(w_ref[:, base : base + 128], rows, TT)
        gate = mm(w_ref[:, base + 128 : base + 256], rows, TT)
        both = sigmoid(gate) * value
        for pair in range(4):
            low = both[:64, pair * 128 : (pair + 1) * 128]
            high = both[64:, pair * 128 : (pair + 1) * 128]
            scratch[side, :, 2 * pair, :] = jnp.where(lane, low, pltpu.roll(high, 64, 1))
            scratch[side, :, 2 * pair + 1, :] = jnp.where(lane, pltpu.roll(low, 64, 1), high)
    out_ref[:, 0] = scratch[0].astype(BF)
    out_ref[:, 1] = scratch[1].astype(BF)


def triangle_kernel(place, left_ref, back_ref, *refs):
    same, other, out_ref = refs[:4], refs[4:6], refs[6]
    left = left_ref[...]
    lane = lax.broadcasted_iota(jnp.int32, (64, 128), 1) < 64
    for m in range(8):
        step = m // 2
        right = other[step % 2][step // 2] if m % 2 else same[step][...]
        product = mm(right, left, TN)
        block = jnp.where(lane, product[:64], product[64:]).astype(BF)
        target = source_of(col_of(place), m) * 2
        for b in range(4):
            for h in range(2):
                out_ref[b * 16 + target + h, 0] = block[(b * 2 + h) * 8 : (b * 2 + h + 1) * 8]
    out_ref[:, 1] = back_ref[...]


def output_kernel(place, sum_ref, mid_ref, wg_ref, w_ref, out_ref, back_ref, scratch, rows):
    del place
    sums = sum_ref[:, 0].astype(F32)
    fold = lambda v: (v + pltpu.roll(v, 64, 1)) * (1.0 / 128)
    average = fold(jnp.sum(sums, axis=0))
    centered = sums - average[None]
    variance = fold(jnp.sum(jnp.square(centered), axis=0))
    scratch[...] = centered * lax.rsqrt(variance + EPSILON)[None]
    mid = mid_ref[...].astype(F32)
    gate_t = sigmoid(mm(wg_ref[...], layer_norm(mid).astype(BF), TT))
    weight = jnp.concatenate([w_ref[:64], w_ref[64:]], axis=1)
    lane = lax.broadcasted_iota(jnp.int32, (128, 128), 1) < 64

    def mixed_of(j):
        product = mm(weight, scratch[:, j, :].astype(BF), TN)
        return product[:128, :64] + product[128:, 64:]

    for j in range(4):
        mixed = jnp.concatenate([mixed_of(j), mixed_of(j + 4)], axis=1)
        ends = (slice(j * 64, (j + 1) * 64), slice((j + 4) * 64, (j + 5) * 64))
        residual = jnp.concatenate([mid[e] for e in ends], axis=0).T
        gate = jnp.concatenate([gate_t[:, e] for e in ends], axis=1)
        part = (residual + gate * mixed).astype(BF)
        for b in range(4):
            out_ref[b, j] = part[b * 32 : (b + 1) * 32]
    rows[...] = sum_ref[:, 1].astype(F32)
    order = [(b * 2 + h) * 8 for h in range(2) for b in range(4)]
    for s in range(4):
        for half in range(2):
            block = rows[:, half * 4 + s, :]
            block = jnp.concatenate([block[k : k + 8] for k in order], axis=0)
            back_ref[s, :, half * 128 : (half + 1) * 128] = block.astype(BF)


def unpack_kernel(x_ref, out_ref):
    for b in range(4):
        for j in range(4):
            block = x_ref[b, j]
            out_ref[b * 8 + j] = block[:, :64]
            out_ref[b * 8 + 4 + j] = block[:, 64:]


def shifted(x, step, flip):
    perm = [(c, (c // 2 - step) % 4 * 2 + (c % 2 ^ flip)) for c in range(8)]
    return lax.ppermute(x, "col", perm)


def gather_col(x):
    same, other = {0: x}, {}
    for step in (2, 1, 3):
        same[step] = shifted(x, step, 0)
    for pair in ((0, 2), (1, 3)):
        other[pair[0]] = shifted(jnp.stack([same[k] for k in pair]), 0, 1)
    return [same[k] for k in range(4)] + [other[0], other[1]]


def local(
    alignment,
    pair_features,
    w_row,
    row_output_weight,
    w_bias,
    w_column,
    column_output_weight,
    outer_input_weight,
    w_outer_out,
    w_triangle_in,
    w_triangle_gate,
    w_triangle_out,
):
    both = ("branch", "row")
    place = lax.axis_index(("branch", "row", "col")).astype(jnp.int32).reshape(1)
    exchange = lambda x, axis: lax.all_to_all(x, axis, 0, 0, tiled=True)

    blocks = gather_col(alignment)
    bias = in_vmem(
        bias_kernel,
        [(16, 32, 512)],
        [
            pltpu.VMEM((64, 32, 128), BF),
            pltpu.VMEM((8, 128), BF),
            pltpu.VMEM((64, 32, 128), F32),
            pltpu.VMEM((16, 8, 128), F32),
            pltpu.SemaphoreType.DMA((5,)),
        ],
        place,
        pair_features,
        w_bias.T,
        loose=2,
    )
    bias = exchange(bias, "row").reshape(512, 512)

    columns = in_vmem(
        row_kernel,
        [(64, 8, 128)],
        [
            pltpu.VMEM((4, 512, 256), BF),
            pltpu.VMEM((2048, 256), BF),
            pltpu.VMEM((256, 2048), BF),
            pltpu.VMEM((64, 8, 128), F32),
        ],
        place,
        *blocks,
        w_row,
        bias,
        row_output_weight,
    )
    columns = exchange(columns, both)
    returning, left, right = in_vmem(
        column_kernel,
        [(64, 8, 128), (32, 256), (8, 32, 256)],
        [pltpu.VMEM((64, 8, 128), F32)],
        place,
        columns,
        w_column,
        column_output_weight,
        outer_input_weight.T,
    )

    right = exchange(right, "col")
    lefts = [left]
    for mask in (1, 2, 3):
        lefts.append(lax.ppermute(left, "branch", [(b, b ^ mask) for b in range(4)]))
    factors = in_vmem(spread_kernel, [(16, 160, 256)], [], place, right, *lefts)
    factors = exchange(factors, "row")

    mid, message = in_vmem(
        pair_kernel,
        [(512, 128), (64, 2, 8, 128)],
        [
            pltpu.VMEM((64, 32, 256), F32),
            pltpu.VMEM((512, 1024), BF),
            pltpu.VMEM((2, 64, 8, 128), F32),
            pltpu.VMEM((64, 8, 128), F32),
        ],
        place,
        factors,
        pair_features,
        w_outer_out,
        w_triangle_in,
    )
    message = exchange(message, both)
    tri_left = message[:, 0].reshape(512, 128)
    rights = gather_col(message[:, 1].reshape(512, 128))
    sums = in_vmem(triangle_kernel, [(64, 2, 8, 128)], [], place, tri_left, returning, *rights)
    sums = exchange(sums, both)
    parts, alignment_out = in_vmem(
        output_kernel,
        [(4, 4, 32, 128), (4, 64, 256)],
        [pltpu.VMEM((64, 8, 128), F32), pltpu.VMEM((64, 8, 128), F32)],
        place,
        sums,
        mid,
        w_triangle_gate,
        w_triangle_out,
        results=1,
    )
    parts = exchange(parts, "branch")
    pair_out = pl.pallas_call(
        unpack_kernel,
        out_shape=jax.ShapeDtypeStruct((32, 32, 64), BF),
        in_specs=[VM],
        name="unpack",
    )(pltpu.with_memory_space_constraint(parts, pltpu.VMEM))
    return (alignment_out, jnp.transpose(pair_out, (2, 0, 1)))


def solution(mesh):
    in_specs = (P(("branch", "row"), "col", None), P("col", "row", None)) + (P(),) * 10
    out_specs = (P(("branch", "row"), "col", None), P("col", "row", "branch"))
    return jax.shard_map(local, mesh=mesh, in_specs=in_specs, out_specs=out_specs, check_vma=False)
```

```python
import jax
import jax.numpy as jnp
from jax import lax
from jax.experimental import pallas as pl
from jax.experimental.pallas import tpu as pltpu
from jax.sharding import PartitionSpec as P


BF = jnp.bfloat16
F32 = jnp.float32
EPSILON = 1e-05
SCALE = 32**-0.5

NT = (((1,), (1,)), ((), ()))
TN = (((0,), (0,)), ((), ()))
TT = (((0,), (1,)), ((), ()))


def mm(a, b, dims):
    return lax.dot_general(a, b, dims, preferred_element_type=F32)


def layer_norm(inputs):
    inputs = inputs.astype(F32)
    average = jnp.mean(inputs, axis=-1, keepdims=True)
    centered = inputs - average
    variance = jnp.mean(jnp.square(centered), axis=-1, keepdims=True)
    return centered * lax.rsqrt(variance + EPSILON)


def sigmoid(x):
    return 1.0 / (1.0 + jnp.exp(-x))


def exp_rows(scores):
    top = jnp.max(scores, axis=0, keepdims=True)
    weights = jnp.exp(scores - top)
    total = jnp.sum(weights, axis=0, keepdims=True)
    return weights.astype(BF), 1.0 / total


VM = pl.BlockSpec(memory_space=pltpu.VMEM)
SM = pl.BlockSpec(memory_space=pltpu.SMEM)
HB = pl.BlockSpec(memory_space=pltpu.HBM)


def in_vmem(kernel, outs, scratch, place, *args, loose=0, results=0):
    loosely = [pltpu.with_memory_space_constraint(a, pltpu.HBM) for a in args[:loose]]
    fixed = [pltpu.with_memory_space_constraint(a, pltpu.VMEM) for a in args[loose:]]
    inner = len(outs) - results
    shapes = [pltpu.VMEM(shape, BF) for shape in outs[:inner]]
    shapes += [jax.ShapeDtypeStruct(shape, BF) for shape in outs[inner:]]
    outputs = pl.pallas_call(
        kernel,
        out_shape=tuple(shapes),
        in_specs=[SM] + [HB] * loose + [VM] * len(fixed),
        out_specs=(VM,) * inner + (pl.BlockSpec(),) * results,
        scratch_shapes=scratch,
        compiler_params=pltpu.CompilerParams(vmem_limit_bytes=24 << 20),
    )(place, *loosely, *fixed)
    return outputs if len(outs) > 1 else outputs[0]


def col_of(place):
    return place[0] & 7


def half_of(place):
    return (place[0] >> 3) & 1


def branch_of(place):
    return place[0] >> 7


def source_of(col, m):
    return (((col >> 1) + (m >> 1)) & 3) * 2 + ((col & 1) ^ (m & 1))


def bias_kernel(place, pair_ref, w_ref, out_ref, pair, weight, rows, heads, sems):
    del place
    copies = [pltpu.make_async_copy(w_ref, weight, sems.at[4])]
    for q in range(4):
        part = pl.ds(q * 16, 16)
        copies.append(pltpu.make_async_copy(pair_ref.at[part], pair.at[part], sems.at[q]))
    for copy in copies:
        copy.start()
    for q in range(4):
        copies[q + 1].wait()
        block = pair[q * 16 : (q + 1) * 16].reshape(512, 128)
        rows[q * 16 : (q + 1) * 16] = layer_norm(block).astype(BF).astype(F32).reshape(16, 32, 128)
    copies[0].wait()
    for j in range(16):
        pairs = jnp.concatenate([rows[:, j, :], rows[:, j + 16, :]], axis=0).astype(BF)
        heads[j] = mm(weight[...], pairs, NT)
    lane = lax.broadcasted_iota(jnp.int32, (16, 128), 1) < 64
    tiles = []
    for p in range(4):
        a = heads[:, 2 * p, :]
        b = heads[:, 2 * p + 1, :]
        first = jnp.where(lane, a, pltpu.roll(b, 64, 1))
        second = jnp.where(lane, pltpu.roll(a, 64, 1), b)
        tiles.append(jnp.concatenate([first, second], axis=0))
    tile = jnp.concatenate(tiles, axis=1).astype(BF)
    for r in range(16):
        out_ref[r] = tile


def row_kernel(place, *refs):
    own_ref, z1_ref, z2_ref, z3_ref, even_ref, odd_ref = refs[:6]
    w_ref, bias_ref, wo_ref, out_ref, rows, keys, values, packed = refs[6:]
    for m, block in (
        (0, own_ref[...]),
        (4, z2_ref[...]),
        (1, even_ref[0]),
        (5, even_ref[1]),
        (2, z1_ref[...]),
        (6, z3_ref[...]),
        (3, odd_ref[0]),
        (7, odd_ref[1]),
    ):
        start = pl.multiple_of(source_of(col_of(place), m) * 64, 64)
        normed = layer_norm(block.reshape(256, 256)).astype(BF)
        if m == 0:
            own = normed
        for s in range(4):
            rows[s, pl.ds(start, 64), :] = normed[s * 64 : (s + 1) * 64]
    x = rows[...].reshape(2048, 256)
    keys[...] = jnp.dot(x, w_ref[:, 256:512], preferred_element_type=F32).astype(BF)
    values[...] = mm(w_ref[:, 512:768], x, TT).astype(BF)
    query_t = (mm(w_ref[:, 0:256], own, TT) * SCALE).astype(BF)
    gate_t = sigmoid(mm(w_ref[:, 768:1024], own, TT))
    head_row = lax.broadcasted_iota(jnp.int32, (256, 512), 0) // 32
    head_lane = lax.broadcasted_iota(jnp.int32, (256, 512), 1) // 64
    upper = lax.broadcasted_iota(jnp.int32, (64, 64), 0) < 32

    def scores_of(s):
        wide = jnp.concatenate([query_t[:, s * 64 : (s + 1) * 64]] * 8, axis=1)
        diag = jnp.where(head_row == head_lane, wide, jnp.zeros_like(wide))
        scores = jnp.dot(keys[s * 512 : (s + 1) * 512], diag, preferred_element_type=F32)
        return scores + bias_ref[...].astype(F32)

    ahead = scores_of(0)
    for s in range(4):
        scores = ahead
        if s < 3:
            ahead = scores_of(s + 1)
        weights, scale = exp_rows(scores)
        parts = []
        for p in range(4):
            lanes = slice(p * 128, (p + 1) * 128)
            mixed = jnp.dot(
                values[p * 64 : (p + 1) * 64, s * 512 : (s + 1) * 512],
                weights[:, lanes],
                preferred_element_type=F32,
            )
            mixed = mixed * scale[:, lanes]
            parts.append(jnp.where(upper, mixed[:, :64], mixed[:, 64:]))
        attended_t = jnp.concatenate(parts, axis=0)
        gated = (gate_t[:, s * 64 : (s + 1) * 64] * attended_t).astype(BF)
        result = own_ref[s].astype(F32) + mm(gated, wo_ref[...], TN)
        for h in range(2):
            for b in range(4):
                source = (h * 4 + b) * 8
                for half in range(2):
                    packed[pl.ds(h * 32 + b, 8, stride=4), half * 4 + s, :] = result[
                        source : source + 8, half * 128 : (half + 1) * 128
                    ]
    out_ref[...] = packed[...].astype(BF)


def column_kernel(place, x_ref, w_ref, wo_ref, wf_ref, out_ref, left_ref, right_ref, scratch):
    del place
    scratch[...] = x_ref[...].astype(F32)
    x = jnp.concatenate(
        [
            jnp.concatenate([scratch[:, s, :], scratch[:, 4 + s, :]], axis=1)
            for s in range(4)
        ],
        axis=0,
    )
    normed = layer_norm(x).astype(BF)
    key = jnp.dot(normed, w_ref[:, 256:512], preferred_element_type=F32).astype(BF)
    value_t = mm(w_ref[:, 512:768], normed, TT).astype(BF)
    query_t = (mm(w_ref[:, 0:256], normed, TT) * SCALE).astype(BF)
    gate_t = sigmoid(mm(w_ref[:, 768:1024], normed, TT))
    head_row = lax.broadcasted_iota(jnp.int32, (256, 1024), 0) // 32
    head_lane = lax.broadcasted_iota(jnp.int32, (256, 1024), 1) // 256
    wide = jnp.concatenate([query_t] * 4, axis=1)

    def scores_of(group):
        diag = jnp.where(head_row == head_lane + group * 4, wide, jnp.zeros_like(wide))
        return jnp.dot(key, diag, preferred_element_type=F32)

    parts = []
    ahead = scores_of(0)
    for group in range(2):
        scores = ahead
        if group == 0:
            ahead = scores_of(1)
        weights, scale = exp_rows(scores)
        for k in range(4):
            h = group * 4 + k
            lanes = slice(k * 256, (k + 1) * 256)
            mixed = jnp.dot(
                value_t[h * 32 : (h + 1) * 32], weights[:, lanes], preferred_element_type=F32
            )
            parts.append(mixed * scale[:, lanes])
    gated = (gate_t * jnp.concatenate(parts, axis=0)).astype(BF)
    result = (x + mm(gated, wo_ref[...], TN)).astype(BF)
    factors = mm(wf_ref[...], layer_norm(result).astype(BF), NT).astype(BF)
    left_ref[...] = factors[:32]
    for c in range(8):
        right_ref[c] = factors[32:]
    wide = result.astype(F32)
    for s in range(4):
        for half in range(2):
            scratch[:, half * 4 + s, :] = wide[
                s * 64 : (s + 1) * 64, half * 128 : (half + 1) * 128
            ]
    out_ref[...] = scratch[...].astype(BF)


def spread_kernel(place, right_ref, *refs):
    lefts, out_ref = refs[:4], refs[4]
    blocks = [left[...] for left in lefts]
    for mask in range(4):
        start = pl.multiple_of((branch_of(place) ^ mask) * 32, 32)
        for r in range(16):
            out_ref[r, pl.ds(start, 32), :] = blocks[mask]
    for r in range(16):
        out_ref[r, 128:] = right_ref[r // 2]


def block_transpose(arrays):
    rows = arrays[0].shape[0]
    lane = lax.broadcasted_iota(jnp.int32, (rows, 128), 1)
    low = lane < 64
    even = (lane // 32) % 2 == 0
    a0, a1, a2, a3 = arrays
    u0 = jnp.where(low, a0, pltpu.roll(a2, 64, 1))
    u2 = jnp.where(low, pltpu.roll(a0, 64, 1), a2)
    u1 = jnp.where(low, a1, pltpu.roll(a3, 64, 1))
    u3 = jnp.where(low, pltpu.roll(a1, 64, 1), a3)
    b0 = jnp.where(even, u0, pltpu.roll(u1, 32, 1))
    b1 = jnp.where(even, pltpu.roll(u0, 96, 1), u1)
    b2 = jnp.where(even, u2, pltpu.roll(u3, 32, 1))
    b3 = jnp.where(even, pltpu.roll(u2, 96, 1), u3)
    return b0, b1, b2, b3


def by_target(rows):
    order = [(h * 4 + b) * 8 for b in range(4) for h in range(2)]
    count = rows.shape[0] // 64
    return jnp.concatenate(
        [rows[j * 64 + s : j * 64 + s + 8] for j in range(count) for s in order], axis=0
    )


def pair_kernel(place, factor_ref, pair_ref, wo_ref, w_ref, mid_ref, out_ref,
                outer, flat, scratch, tile_rows):
    right = factor_ref[pl.ds(half_of(place) * 8, 8), 128:, :].reshape(256, 256)
    for b in range(4):
        left = factor_ref[:, b * 32 : (b + 1) * 32, :].reshape(512, 256)
        product = (mm(left, right, NT) * (1.0 / 256)).reshape(16, 32, 256)
        for h in range(2):
            start = (h * 4 + b) * 8
            outer[start : start + 8] = product[h * 8 : (h + 1) * 8]
    for group in range(8):
        chans = [outer[:, group * 4 + k, :] for k in range(4)]
        for tile in range(2):
            moved = block_transpose([c[:, tile * 128 : (tile + 1) * 128] for c in chans])
            for k in range(4):
                j = tile * 4 + k
                flat[j * 64 : (j + 1) * 64, group * 128 : (group + 1) * 128] = moved[k].astype(BF)
    update = jnp.dot(flat[...], wo_ref[...], preferred_element_type=F32).astype(BF)
    first = pl.multiple_of(branch_of(place) * 8, 8)
    tile_rows[...] = pair_ref[:, pl.ds(first, 8), :].astype(F32)
    pair = jnp.concatenate([tile_rows[:, j, :] for j in range(8)], axis=0)
    mid = (pair + update.astype(F32)).astype(BF)
    mid_ref[...] = mid
    normed = layer_norm(mid)
    lane = lax.broadcasted_iota(jnp.int32, (64, 128), 1) < 64
    for side in range(2):
        rows = (by_target(normed) if side else normed).astype(BF)
        base = side * 256
        value = mm(w_ref[:, base : base + 128], rows, TT)
        gate = mm(w_ref[:, base + 128 : base + 256], rows, TT)
        both = sigmoid(gate) * value
        for pair in range(4):
            low = both[:64, pair * 128 : (pair + 1) * 128]
            high = both[64:, pair * 128 : (pair + 1) * 128]
            scratch[side, :, 2 * pair, :] = jnp.where(lane, low, pltpu.roll(high, 64, 1))
            scratch[side, :, 2 * pair + 1, :] = jnp.where(lane, pltpu.roll(low, 64, 1), high)
    out_ref[:, 0] = scratch[0].astype(BF)
    out_ref[:, 1] = scratch[1].astype(BF)


def triangle_kernel(place, left_ref, back_ref, *refs):
    same, other, out_ref = refs[:4], refs[4:6], refs[6]
    left = left_ref[...]
    lane = lax.broadcasted_iota(jnp.int32, (64, 128), 1) < 64
    for m in range(8):
        step = m // 2
        right = other[step % 2][step // 2] if m % 2 else same[step][...]
        product = mm(right, left, TN)
        block = jnp.where(lane, product[:64], product[64:]).astype(BF)
        target = source_of(col_of(place), m) * 2
        for b in range(4):
            for h in range(2):
                out_ref[(target + h) * 4 + b, 0] = block[(b * 2 + h) * 8 : (b * 2 + h + 1) * 8]
    out_ref[:, 1] = back_ref[...]


def output_kernel(place, sum_ref, mid_ref, wg_ref, w_ref, out_ref, back_ref, scratch, rows):
    del place
    sums = sum_ref[:, 0].astype(F32)
    fold = lambda v: (v + pltpu.roll(v, 64, 1)) * (1.0 / 128)
    average = fold(jnp.sum(sums, axis=0))
    centered = sums - average[None]
    variance = fold(jnp.sum(jnp.square(centered), axis=0))
    scratch[...] = centered * lax.rsqrt(variance + EPSILON)[None]
    mid = mid_ref[...].astype(F32)
    gate_t = sigmoid(mm(wg_ref[...], layer_norm(mid).astype(BF), TT))
    weight = jnp.concatenate([w_ref[:64], w_ref[64:]], axis=1)
    lane = lax.broadcasted_iota(jnp.int32, (128, 128), 1) < 64

    def mixed_of(j):
        product = mm(weight, scratch[:, j, :].astype(BF), TN)
        return product[:128, :64] + product[128:, 64:]

    for j in range(4):
        mixed = jnp.concatenate([mixed_of(j), mixed_of(j + 4)], axis=1)
        ends = (slice(j * 64, (j + 1) * 64), slice((j + 4) * 64, (j + 5) * 64))
        residual = jnp.concatenate([mid[e] for e in ends], axis=0).T
        gate = jnp.concatenate([gate_t[:, e] for e in ends], axis=1)
        part = (residual + gate * mixed).astype(BF)
        for b in range(4):
            out_ref[b, j] = part[b * 32 : (b + 1) * 32]
    rows[...] = sum_ref[:, 1].astype(F32)
    starts = [h * 32 + b for h in range(2) for b in range(4)]
    for s in range(4):
        for half in range(2):
            block = jnp.concatenate(
                [rows[pl.ds(k, 8, stride=4), half * 4 + s, :] for k in starts], axis=0
            )
            back_ref[s, :, half * 128 : (half + 1) * 128] = block.astype(BF)


def unpack_kernel(x_ref, out_ref):
    for b in range(4):
        for j in range(4):
            block = x_ref[b, j]
            out_ref[b * 8 + j] = block[:, :64]
            out_ref[b * 8 + 4 + j] = block[:, 64:]


def shifted(x, step, flip):
    perm = [(c, (c // 2 - step) % 4 * 2 + (c % 2 ^ flip)) for c in range(8)]
    return lax.ppermute(x, "col", perm)


def gather_col(x):
    same, other = {0: x}, {}
    for step in (2, 1, 3):
        same[step] = shifted(x, step, 0)
    for pair in ((0, 2), (1, 3)):
        other[pair[0]] = shifted(jnp.stack([same[k] for k in pair]), 0, 1)
    return [same[k] for k in range(4)] + [other[0], other[1]]


def local(
    alignment,
    pair_features,
    w_row,
    row_output_weight,
    w_bias,
    w_column,
    column_output_weight,
    outer_input_weight,
    w_outer_out,
    w_triangle_in,
    w_triangle_gate,
    w_triangle_out,
):
    both = ("row", "branch")
    place = lax.axis_index(("branch", "row", "col")).astype(jnp.int32).reshape(1)
    exchange = lambda x, axis: lax.all_to_all(x, axis, 0, 0, tiled=True)

    blocks = gather_col(alignment)
    bias = in_vmem(
        bias_kernel,
        [(16, 32, 512)],
        [
            pltpu.VMEM((64, 32, 128), BF),
            pltpu.VMEM((8, 128), BF),
            pltpu.VMEM((64, 32, 128), F32),
            pltpu.VMEM((16, 8, 128), F32),
            pltpu.SemaphoreType.DMA((5,)),
        ],
        place,
        pair_features,
        w_bias.T,
        loose=2,
    )
    bias = exchange(bias, "row").reshape(512, 512)

    columns = in_vmem(
        row_kernel,
        [(64, 8, 128)],
        [
            pltpu.VMEM((4, 512, 256), BF),
            pltpu.VMEM((2048, 256), BF),
            pltpu.VMEM((256, 2048), BF),
            pltpu.VMEM((64, 8, 128), F32),
        ],
        place,
        *blocks,
        w_row,
        bias,
        row_output_weight,
    )
    columns = exchange(columns, both)
    returning, left, right = in_vmem(
        column_kernel,
        [(64, 8, 128), (32, 256), (8, 32, 256)],
        [pltpu.VMEM((64, 8, 128), F32)],
        place,
        columns,
        w_column,
        column_output_weight,
        outer_input_weight.T,
    )

    right = exchange(right, "col")
    lefts = [left]
    for mask in (1, 2, 3):
        lefts.append(lax.ppermute(left, "branch", [(b, b ^ mask) for b in range(4)]))
    factors = in_vmem(spread_kernel, [(16, 160, 256)], [], place, right, *lefts)
    factors = exchange(factors, "row")

    mid, message = in_vmem(
        pair_kernel,
        [(512, 128), (64, 2, 8, 128)],
        [
            pltpu.VMEM((64, 32, 256), F32),
            pltpu.VMEM((512, 1024), BF),
            pltpu.VMEM((2, 64, 8, 128), F32),
            pltpu.VMEM((64, 8, 128), F32),
        ],
        place,
        factors,
        pair_features,
        w_outer_out,
        w_triangle_in,
    )
    message = exchange(message, both)
    tri_left = message[:, 0].reshape(512, 128)
    rights = gather_col(message[:, 1].reshape(512, 128))
    sums = in_vmem(triangle_kernel, [(64, 2, 8, 128)], [], place, tri_left, returning, *rights)
    sums = exchange(sums, both)
    parts, alignment_out = in_vmem(
        output_kernel,
        [(4, 4, 32, 128), (4, 64, 256)],
        [pltpu.VMEM((64, 8, 128), F32), pltpu.VMEM((64, 8, 128), F32)],
        place,
        sums,
        mid,
        w_triangle_gate,
        w_triangle_out,
        results=1,
    )
    parts = exchange(parts, "branch")
    pair_out = pl.pallas_call(
        unpack_kernel,
        out_shape=jax.ShapeDtypeStruct((32, 32, 64), BF),
        in_specs=[VM],
        name="unpack",
    )(pltpu.with_memory_space_constraint(parts, pltpu.VMEM))
    return (alignment_out, jnp.transpose(pair_out, (2, 0, 1)))


def solution(mesh):
    in_specs = (P(("branch", "row"), "col", None), P("col", "row", None)) + (P(),) * 10
    out_specs = (P(("branch", "row"), "col", None), P("col", "row", "branch"))
    return jax.shard_map(local, mesh=mesh, in_specs=in_specs, out_specs=out_specs, check_vma=False)
```
